32 devices in a mesh: gx: 4 (over z), gz: 2 (over y), row: 4 (over x, core).
Axes of the slice: x: 2, y: 2, z: 4, core: 2. Of those that a mesh axis runs over, the one named last changes fastest.
Arguments:
- flow_field: float32 [5, 16, 64, 512], P(None, 'gx', 'gz', 'row'), may hold values from -6 to 6
- flux_jacobian: float32 [3, 5, 5], replicated, may hold values from -2.5 to 2.5
- history: float32 [12288, 5, 128], P(('gx', 'gz', 'row')), may hold values from -6 to 6
- surface_cell: int32 [1536, 8], P(('gx', 'gz', 'row')), may hold values from 0 to 16383
- surface_blocks: int32 [4, 8], P('row', ('gx', 'gz')), may hold values from 1 to 48, 128 in all within a row
- observers: float32 [3, 256], replicated, may hold values from 0 to 1
Outputs:
- field_out: float32 [5, 16, 64, 512], P(None, 'gx', 'gz', 'row')
- spectrum: float32 [256, 64], P(('gx', 'gz', 'row'))
The draws below stay inside these ranges and needn't reach their ends.
Inputs may be any that keep to these rules, and one draw needn't show every extreme that they name: The patch with index g of gx+gz and index q of row has exactly 8 * surface_blocks[q, g] live slots, its first ones.
All inputs are finite; a program needn't handle non-finite values. No bound on the sum of `surface_blocks` on one device may be relied on, other than what follows from the above.
Results may differ from the reference program's by a relative error of at most 0.0003.
Values sent between devices are 32-bit elements; how exact they have to be, the bound alone decides.
No kernel may reach another device: no remote copies, remote signals or barrier semaphores. Data moves between devices by JAX's collectives and lax.ppermute only.
A program may use at most 64 MiB of HBM per device.

```python
import math
import jax
import jax.numpy as jnp
import numpy as np
from jax import lax

CX = 4
CZ = 32
CR = 128
SURF_DEV = 128
NT = 128
FREQ = 32
OBS = 256
STEPS = 3
OWNERS = 8
SLOT = 48
SP_CAP = 384
NX = 16
NZ = 64
NR = 512
N_GX = 4
N_GZ = 2
N_ROW = 4
DEVICES = 32


def plant(array, rng, low, high):
    longest = array.shape.index(max(array.shape))
    spots = []
    for shift in (0, 1):
        where = [jax.random.randint(jax.random.fold_in(rng, axis), (), 0, length) for axis, length in enumerate(array.shape)]
        where[longest] = (where[longest] + shift) % array.shape[longest]
        spots.append(tuple(where))
    return array.at[spots[0]].set(low).at[spots[1]].set(high)


def steps_of(own_key, extent, pieces, least, top_value):
    loudness = 1.0
    for position, blocks in pieces:
        draws = jax.random.uniform(jax.random.fold_in(jax.random.fold_in(own_key, 6), position), (blocks,), jnp.float32, least / len(pieces), top_value / len(pieces))
        loudness = loudness * jnp.repeat(jnp.exp(draws), extent[position] // blocks).reshape((-1,) + (1,) * (len(extent) - 1 - position))
    return loudness


def profile(amount, total, limit, lean):
    loads = [(1 << 20) // math.isqrt(grade ** lean) + 1 for grade in range(2, amount + 1)]
    surplus, holding = total - limit - (amount - 1), [1] * (amount - 1)
    while surplus > 0:
        candidates = [i for i in range(amount - 1) if holding[i] < limit]
        mass, budget = sum([loads[i] for i in candidates]), surplus
        for i in candidates:
            extra = min(limit - holding[i], max(1, budget * loads[i] // mass), surplus)
            holding[i] = holding[i] + extra
            surplus = surplus - extra
    return np.array([limit] + holding)


def uneven_parts(stream_key, number_of, total, most, slope):
    if number_of == 2:
        one = jax.random.randint(stream_key, (), max(1, total - most), min(most, total - 1) + 1)
        return jnp.stack([one, total - one])
    tallies = jnp.asarray(profile(number_of, total, most, slope), jnp.int32)
    twos = (number_of - 1) // 2
    giver, sink = tallies[1:1 + 2 * twos:2], tallies[2:2 + 2 * twos:2]
    slack = jnp.minimum(giver - 1, most - sink)
    passed = jax.random.randint(jax.random.fold_in(stream_key, 1), (twos,), 0, 1 << 20) % (slack + 1)
    tallies = tallies.at[1:1 + 2 * twos:2].set(giver - passed).at[2:2 + 2 * twos:2].set(sink + passed)
    return tallies[jax.random.permutation(jax.random.fold_in(stream_key, 2), number_of)]


def gaussian(key, extent, spread, most, pieces=(), held_as=jnp.bfloat16):
    result = jax.random.normal(key, extent, jnp.float32) * spread
    if len(pieces) > 0:
        result = steps_of(key, extent, pieces, -0.22, 0.18) * result
    return jnp.clip(result, min=-most, max=most).astype(held_as)


def setup_inputs(seed: int = 0) -> dict:
    keys = jax.random.split(jax.random.key(seed), 7)
    return {
        "flow_field": gaussian(keys[0], (5, NX, NZ, NR), 1.0, 6.0, ((1, 4), (2, 2), (3, 4)), jnp.float32),
        "flux_jacobian": gaussian(keys[1], (3, 5, 5), 5 ** -0.5, 2.5, (), jnp.float32),
        "history": gaussian(keys[2], (DEVICES * SP_CAP, 5, NT), 1.0, 6.0, ((0, 32),), jnp.float32),
        "surface_cell": plant(jax.random.randint(keys[3], (DEVICES * SLOT, OWNERS), 0, CX * CZ * CR), jax.random.fold_in(keys[3], 1), 0, (CX * CZ * CR) - 1).astype(jnp.int32),
        "surface_blocks": jax.vmap(lambda own: uneven_parts(own, OWNERS, SURF_DEV, SLOT, 2))(jax.random.split(keys[4], N_ROW)).reshape((N_ROW, OWNERS)).astype(jnp.int32),
        "observers": jnp.clip(jax.random.uniform(keys[5], (3, OBS), jnp.float32, 0.0, 1.0), 0.0, 1.0),
    }


TIME_STEP = 0.3
VISCOSITY = 0.05

def stencil_rate(padded, flux_jacobian):
    center = padded[:, 1:-1, 1:-1, 1:-1]
    along_x = (padded[:, 2:, 1:-1, 1:-1] - padded[:, :-2, 1:-1, 1:-1]) * 0.5
    along_z = (padded[:, 1:-1, 2:, 1:-1] - padded[:, 1:-1, :-2, 1:-1]) * 0.5
    along_r = (padded[:, 1:-1, 1:-1, 2:] - padded[:, 1:-1, 1:-1, :-2]) * 0.5
    beside = padded[:, 2:, 1:-1, 1:-1] + padded[:, :-2, 1:-1, 1:-1]
    beside = beside + padded[:, 1:-1, 2:, 1:-1] + padded[:, 1:-1, :-2, 1:-1]
    beside = beside + padded[:, 1:-1, 1:-1, 2:] + padded[:, 1:-1, 1:-1, :-2]
    slopes = jnp.stack([along_x, along_z, along_r])
    transport = jnp.einsum('dvw,dwxzr->vxzr', flux_jacobian, slopes, precision=lax.Precision.HIGHEST)
    return transport + VISCOSITY * (beside - 6.0 * center)

def advance(current, rate_of):
    section_one = current + TIME_STEP * rate_of(current)
    section_two = 0.75 * current + 0.25 * (section_one + TIME_STEP * rate_of(section_one))
    return current / 3.0 + 2.0 / 3.0 * (section_two + TIME_STEP * rate_of(section_two))

def fourier_table(samples, freq_count):
    time_ids = jnp.arange(samples, dtype=jnp.int32)
    freq_ids = jnp.arange(1, freq_count + 1, dtype=jnp.int32)
    turn_ids = freq_ids[:, None] * time_ids[None, :] % samples
    angles = 2.0 * math.pi / samples * turn_ids.astype(jnp.float32)
    norm_scale = 1.0 / math.sqrt(samples)
    return jnp.concatenate([jnp.cos(angles), -jnp.sin(angles)], axis=0) * norm_scale

def spectra_of(signals, fourier):
    return jnp.einsum('ft,svt->vfs', fourier, signals, precision=lax.Precision.HIGHEST)

def radiate(points, monopole, dipole, watchers, radial_cells, freq_count):
    wavenumbers = jnp.arange(1, freq_count + 1, dtype=jnp.float32) * (2.0 / radial_cells)
    offset_vec = watchers[:, :, None] - points[None, :, :]
    distance = jnp.sqrt(lax.optimization_barrier(jnp.sum(offset_vec * offset_vec, axis=1)))
    direction = offset_vec / distance[:, None, :]
    amplitude = (radial_cells / distance)[:, None, :]
    dip_real = direction[:, 0, None, :] * dipole[0, None, :freq_count, :]
    dip_real = dip_real + direction[:, 1, None, :] * dipole[1, None, :freq_count, :]
    dip_real = dip_real + direction[:, 2, None, :] * dipole[2, None, :freq_count, :]
    dip_imag = direction[:, 0, None, :] * dipole[0, None, freq_count:, :]
    dip_imag = dip_imag + direction[:, 1, None, :] * dipole[1, None, freq_count:, :]
    dip_imag = dip_imag + direction[:, 2, None, :] * dipole[2, None, freq_count:, :]
    mono_real = monopole[None, :freq_count, :]
    mono_imag = monopole[None, freq_count:, :]
    phase_arg = distance[:, None, :] * wavenumbers[None, :, None]
    near_term = 1.0 / phase_arg
    cosine = amplitude * jnp.cos(phase_arg)
    sine = amplitude * jnp.sin(phase_arg)
    plus_weight = cosine * near_term + sine
    minus_weight = cosine - sine * near_term
    out_real = lax.optimization_barrier(jnp.sum(plus_weight * dip_real - minus_weight * dip_imag + sine * mono_real - cosine * mono_imag, axis=2))
    out_imag = lax.optimization_barrier(jnp.sum(minus_weight * dip_real + plus_weight * dip_imag + cosine * mono_real + sine * mono_imag, axis=2))
    return jnp.concatenate([out_real, out_imag], axis=1)

def reference(flow_field, flux_jacobian, history, surface_cell, surface_blocks, observers):
    padding = ((0, 0), (1, 1), (1, 1), (1, 1))

    def rate_of(values):
        return stencil_rate(jnp.pad(values, padding), flux_jacobian)
    owners = N_GX * N_GZ
    capacity = SLOT * owners
    cell_ids = surface_cell.reshape(-1)
    slot_ids = jnp.arange(DEVICES * capacity, dtype=jnp.int32)
    device = slot_ids // capacity
    local_slot = slot_ids % capacity
    index_x = device // (N_GZ * N_ROW)
    index_z = device // N_ROW % N_GZ
    index_r = device % N_ROW
    global_x = index_x * CX + cell_ids // (CZ * CR)
    global_z = index_z * CZ + cell_ids // CR % CZ
    global_r = index_r * CR + cell_ids % CR
    flat_index = ((global_x * NZ + global_z) * NR + global_r).astype(jnp.int32)
    current = flow_field
    sampled = []
    for step_index in range(STEPS):
        current = advance(current, rate_of)
        sampled.append(jnp.take(current.reshape(5, -1), flat_index, axis=1))
    live_limit = surface_blocks[index_r, index_x * N_GZ + index_z]
    is_live = local_slot // owners < live_limit
    chosen = jnp.nonzero(is_live, size=DEVICES * SURF_DEV)[0].astype(jnp.int32)
    recent = jnp.stack(sampled, axis=2)[:, chosen, :]
    signals = jnp.concatenate([history[chosen][:, :, :NT - STEPS], jnp.transpose(recent, (1, 0, 2))], axis=2)
    points = jnp.stack([global_x, global_z, global_r])[:, chosen].astype(jnp.float32) + 0.5
    spectra = spectra_of(signals, fourier_table(NT, FREQ))
    monopole = spectra[0] + spectra[4]
    dipole = spectra[1:4]
    watchers = jnp.stack([observers[0] * NX, observers[1] * NZ, (1.25 + 0.75 * observers[2]) * NR], axis=1)

    def one_block(block):
        return radiate(points, monopole, dipole, block, NR, FREQ)
    blocks_out = lax.map(one_block, watchers.reshape(OBS // 8, 8, 3))
    spectrum = blocks_out.reshape(OBS, 2 * FREQ) / math.sqrt(DEVICES * SURF_DEV)
    return (current, spectrum)
```

```python
import functools
import math

import jax
import jax.numpy as jnp
import numpy as np
from jax import lax
from jax.experimental import pallas as pl
from jax.experimental.pallas import tpu as pltpu
from jax.sharding import PartitionSpec as P

SURF_DEV = 128
FREQ = 32
STEPS = 3


TIME_STEP = 0.3
VISCOSITY = 0.05


def padded_2(value, sides, width):
    for axis, dim in sides:
        peers, length = (lax.axis_size(axis), value.shape[dim])
        up = [(i, (i + 1) % peers) for i in range(peers - 1)]
        down = [(j, i) for i, j in up]
        last = lax.slice_in_dim(value, length - width, length, axis=dim)
        leading = lax.slice_in_dim(value, 0, width, axis=dim)
        before = lax.ppermute(last, axis, up)
        after = lax.ppermute(leading, axis, down)
        value = jnp.concatenate([before, value, after], axis=dim)
    return value


def stencil_rate(padded, flux_jacobian):
    center = padded[:, 1:-1, 1:-1, 1:-1]
    along_x = (padded[:, 2:, 1:-1, 1:-1] - padded[:, :-2, 1:-1, 1:-1]) * 0.5
    along_z = (padded[:, 1:-1, 2:, 1:-1] - padded[:, 1:-1, :-2, 1:-1]) * 0.5
    along_r = (padded[:, 1:-1, 1:-1, 2:] - padded[:, 1:-1, 1:-1, :-2]) * 0.5
    beside = padded[:, 2:, 1:-1, 1:-1] + padded[:, :-2, 1:-1, 1:-1]
    beside = beside + padded[:, 1:-1, 2:, 1:-1] + padded[:, 1:-1, :-2, 1:-1]
    beside = beside + padded[:, 1:-1, 1:-1, 2:] + padded[:, 1:-1, 1:-1, :-2]
    slopes = jnp.stack([along_x, along_z, along_r])
    transport = jnp.einsum(
        "dvw,dwxzr->vxzr", flux_jacobian, slopes, precision=lax.Precision.HIGHEST
    )
    return transport + VISCOSITY * (beside - 6.0 * center)


def fourier_table(samples, freq_count):
    time_ids = jnp.arange(samples, dtype=jnp.int32)
    freq_ids = jnp.arange(1, freq_count + 1, dtype=jnp.int32)
    turn_ids = freq_ids[:, None] * time_ids[None, :] % samples
    angles = 2.0 * math.pi / samples * turn_ids.astype(jnp.float32)
    norm_scale = 1.0 / math.sqrt(samples)
    return jnp.concatenate([jnp.cos(angles), -jnp.sin(angles)], axis=0) * norm_scale


def spectra_of(signals, fourier):
    return jnp.einsum("ft,svt->vfs", fourier, signals, precision=lax.Precision.HIGHEST)


def radiate(points, monopole, dipole, watchers, radial_cells, freq_count):
    wavenumbers = jnp.arange(1, freq_count + 1, dtype=jnp.float32) * (2.0 / radial_cells)
    offset_vec = watchers[:, :, None] - points[None, :, :]
    distance = jnp.sqrt(jnp.sum(offset_vec * offset_vec, axis=1))
    direction = offset_vec / distance[:, None, :]
    amplitude = (radial_cells / distance)[:, None, :]
    dip_real = direction[:, 0, None, :] * dipole[0, None, :freq_count, :]
    dip_real = dip_real + direction[:, 1, None, :] * dipole[1, None, :freq_count, :]
    dip_real = dip_real + direction[:, 2, None, :] * dipole[2, None, :freq_count, :]
    dip_imag = direction[:, 0, None, :] * dipole[0, None, freq_count:, :]
    dip_imag = dip_imag + direction[:, 1, None, :] * dipole[1, None, freq_count:, :]
    dip_imag = dip_imag + direction[:, 2, None, :] * dipole[2, None, freq_count:, :]
    mono_real = monopole[None, :freq_count, :]
    mono_imag = monopole[None, freq_count:, :]
    phase_arg = distance[:, None, :] * wavenumbers[None, :, None]
    near_term = 1.0 / phase_arg
    cosine = amplitude * jnp.cos(phase_arg)
    sine = amplitude * jnp.sin(phase_arg)
    plus_weight = cosine * near_term + sine
    minus_weight = cosine - sine * near_term
    out_real = jnp.sum(
        plus_weight * dip_real - minus_weight * dip_imag + sine * mono_real - cosine * mono_imag,
        axis=2,
    )
    out_imag = jnp.sum(
        minus_weight * dip_real + plus_weight * dip_imag + cosine * mono_real + sine * mono_imag,
        axis=2,
    )
    return jnp.concatenate([out_real, out_imag], axis=1)


def general_device(flow_field, flux_jacobian, history, surface_cell, surface_blocks, observers):
    width_x, width_z, width_r = (flow_field.shape[1], flow_field.shape[2], flow_field.shape[3])
    count_x, count_z, count_r = (lax.axis_size("gx"), lax.axis_size("gz"), lax.axis_size("row"))
    index_x, index_z, index_r = (lax.axis_index("gx"), lax.axis_index("gz"), lax.axis_index("row"))
    owners = count_x * count_z
    devices = owners * count_r
    radial_cells = width_r * count_r
    slot_rows = surface_cell.shape[0]
    capacity = slot_rows * owners
    samples = history.shape[2]
    cell_ids = surface_cell.reshape(-1)

    def inside_mask(margin):
        coord_x = index_x * width_x + jnp.arange(width_x + 2 * margin, dtype=jnp.int32) - margin
        coord_z = index_z * width_z + jnp.arange(width_z + 2 * margin, dtype=jnp.int32) - margin
        coord_r = index_r * width_r + jnp.arange(width_r + 2 * margin, dtype=jnp.int32) - margin
        valid_x = (coord_x >= 0) & (coord_x < width_x * count_x)
        valid_z = (coord_z >= 0) & (coord_z < width_z * count_z)
        valid_r = (coord_r >= 0) & (coord_r < radial_cells)
        joined = valid_x[:, None, None] & valid_z[None, :, None] & valid_r[None, None, :]
        return joined.astype(jnp.float32)[None]

    mask_outer = inside_mask(2)
    mask_inner = inside_mask(1)
    current = flow_field
    sampled = []
    for step_index in range(STEPS):
        extended = padded_2(current, (("gx", 1), ("gz", 2), ("row", 3)), 3)
        section_one = (
            extended[:, 1:-1, 1:-1, 1:-1] + TIME_STEP * stencil_rate(extended, flux_jacobian)
        ) * mask_outer
        section_two = 0.75 * extended[:, 2:-2, 2:-2, 2:-2] + 0.25 * (
            section_one[:, 1:-1, 1:-1, 1:-1] + TIME_STEP * stencil_rate(section_one, flux_jacobian)
        )
        section_two = section_two * mask_inner
        current = extended[:, 3:-3, 3:-3, 3:-3] / 3.0 + 2.0 / 3.0 * (
            section_two[:, 1:-1, 1:-1, 1:-1] + TIME_STEP * stencil_rate(section_two, flux_jacobian)
        )
        sampled.append(jnp.take(current.reshape(5, -1), cell_ids, axis=1))
    recent = jnp.transpose(jnp.stack(sampled, axis=2), (1, 0, 2))
    signals = jnp.concatenate([history[:, :, : samples - STEPS], recent], axis=2)
    global_x = index_x * width_x + cell_ids // (width_z * width_r)
    global_z = index_z * width_z + cell_ids // width_r % width_z
    global_r = index_r * width_r + cell_ids % width_r
    positions = jnp.stack([global_x, global_z, global_r]).astype(jnp.float32) + 0.5
    fourier = fourier_table(samples, FREQ)
    live_mask = (jnp.arange(capacity, dtype=jnp.int32) // owners < surface_blocks[0, 0]).astype(
        jnp.float32
    )
    spectra = spectra_of(signals, fourier) * live_mask
    monopole = spectra[0] + spectra[4]
    dipole = spectra[1:4]
    watchers = jnp.stack(
        [
            observers[0] * (width_x * count_x),
            observers[1] * (width_z * count_z),
            (1.25 + 0.75 * observers[2]) * radial_cells,
        ],
        axis=1,
    )
    norm_scale = math.sqrt(devices * SURF_DEV)
    row_count = observers.shape[1] // devices * lax.axis_size(("gx", "gz", "row"))
    block_size = math.gcd(row_count, 32)

    def one_block(block):
        return radiate(positions, monopole, dipole, block, radial_cells, FREQ)

    blocks_out = lax.map(one_block, watchers.reshape(row_count // block_size, block_size, 3))
    spectrum = lax.psum_scatter(
        blocks_out.reshape(row_count, 2 * FREQ) / norm_scale,
        ("gx", "gz", "row"),
        scatter_dimension=0,
        tiled=True,
    )
    return (current, spectrum)


HALO = 3 * STEPS
AXES = ("gx", "gz", "row")
GROUP = ("gx", "gz")
VMEM = pl.BlockSpec(memory_space=pltpu.VMEM)
SMEM = pl.BlockSpec(memory_space=pltpu.SMEM)


def halves(value, by):
    if by & (by - 1) == 0:
        return value >> (by.bit_length() - 1), value & (by - 1)
    return value // by, value % by


def sin_cos(angle):
    turns = jnp.floor(angle * (2.0 / math.pi) + 0.5)
    rest = ((angle - turns * 1.5703125) - turns * 4.837512969970703e-4) - turns * 7.549789954891882e-8
    square = rest * rest
    sine = rest + rest * square * (
        -1.6666654611e-1 + square * (8.3321608736e-3 + square * -1.9515295891e-4)
    )
    cosine = (1.0 - 0.5 * square) + square * square * (
        4.166664568298827e-2 + square * (-1.388731625493765e-3 + square * 2.443315711809948e-5)
    )
    quarter = turns.astype(jnp.int32) & 3
    odd = (quarter & 1) == 1
    out_sine = jnp.where(odd, cosine, sine)
    out_cosine = jnp.where(odd, sine, cosine)
    out_sine = jnp.where(quarter >= 2, -out_sine, out_sine)
    out_cosine = jnp.where((quarter == 1) | (quarter == 2), -out_cosine, out_cosine)
    return out_sine, out_cosine


class Plan:
    def __init__(self, mesh, flow, cells, hist, obs):
        self.ax, self.az, self.rows = mesh["gx"], mesh["gz"], mesh["row"]
        self.group = self.ax * self.az
        self.devices = self.group * self.rows
        self.wx, self.wz, self.wr = flow
        self.blocks = cells[0]
        self.capacity = cells[0] * cells[1]
        self.samples = hist[2]
        self.lanes = self.wx * self.wz
        self.chunk = self.wr // self.group
        self.nx, self.nz, self.nr = self.wx * self.ax, self.wz * self.az, self.wr * self.rows
        self.obs = obs
        self.body = 5 * self.chunk
        self.sent = self.body + 8
        self.per_obs = obs // self.devices

    def fits(self):
        return (
            self.group == 8
            and self.lanes == 128
            and self.wr % 128 == 0
            and self.chunk % 8 == 0
            and self.chunk >= HALO
            and self.capacity == self.blocks * 8
            and self.blocks < 127
            and self.capacity % 128 == 0
            and self.samples == 128
            and self.obs % 128 == 0
            and self.obs % self.devices == 0
            and FREQ == 32
            and STEPS == 3
        )

    def order_of(self, a, b):
        return b * self.ax + (a if b % 2 == 0 else self.ax - 1 - a)

    def table(self):
        return [self.order_of(j // self.az, j % self.az) for j in range(self.group)]

    def line(self):
        out = []
        for c in range(self.rows):
            order = self.table()
            if c % 2:
                order = [self.group - 1 - q for q in order]
            for q in range(self.group):
                out.append(order.index(q) * self.rows + c)
        return out

    def chunk_of(self, j, c):
        q = self.table()[j]
        return jnp.where(c % 2 == 1, self.group - 1 - q, q)

    def own_chunk(self):
        a, b, c = lax.axis_index("gx"), lax.axis_index("gz"), lax.axis_index("row")
        q = b * self.ax + jnp.where(b % 2 == 0, a, self.ax - 1 - a)
        return jnp.where(c % 2 == 1, self.group - 1 - q, q), c


def call(kernel, out_shape, in_specs, out_specs, scratch=(), flops=10**6, name=None):
    return pl.pallas_call(
        kernel,
        out_shape=out_shape,
        in_specs=in_specs,
        out_specs=out_specs,
        scratch_shapes=list(scratch),
        name=name,
        compiler_params=pltpu.CompilerParams(vmem_limit_bytes=40 * 1024 * 1024),
        cost_estimate=pl.CostEstimate(flops=flops, bytes_accessed=10**5, transcendentals=0),
    )


def pack_kernel(plan, flow_ref, cell_ref, live_ref, out_ref, turned):
    c = lax.axis_index("row")
    for v in range(5):
        turned[v * plan.wr : (v + 1) * plan.wr, :] = flow_ref[v].T
    cells = cell_ref[...].astype(jnp.float32)
    wide = jnp.concatenate([cells, jnp.zeros((plan.blocks, 120), jnp.float32)], axis=1)
    wide = jnp.concatenate([wide, jnp.zeros((128 - plan.blocks, 128), jnp.float32)], axis=0)
    ids = wide.T[:8, :]
    lane = lax.broadcasted_iota(jnp.int32, (8, 128), 1)
    ids = jnp.where(lane == 127, live_ref[0, 0].astype(jnp.float32), ids)
    for j in range(plan.group):
        q = plan.chunk_of(j, c)
        for v in range(5):
            start = pl.multiple_of(v * plan.wr + q * plan.chunk, 8)
            out_ref[j, v * plan.chunk : (v + 1) * plan.chunk, :] = turned[pl.ds(start, plan.chunk), :]
        out_ref[j, plan.body : plan.body + 8, :] = ids


def edge_kernel(plan, got_ref, first_ref, second_ref):
    q, c = plan.own_chunk()
    even = (c * plan.group + q) % 2 == 0
    high, low = plan.chunk - HALO, 0
    first = jnp.where(even, high, low)
    second = jnp.where(even, low, high)
    for v in range(5):
        for i in range(HALO):
            first_ref[v * HALO + i] = got_ref[pl.ds(v * plan.chunk + first + i, 8, stride=plan.sent), :]
            second_ref[v * HALO + i] = got_ref[pl.ds(v * plan.chunk + second + i, 8, stride=plan.sent), :]


def stencil_kernel(plan, got_ref, first_ref, second_ref, jac_ref, back_ref, samp_ref, cur, one, two, coef):
    q, c = plan.own_chunk()
    place = c * plan.group + q
    even = place % 2 == 0
    tall = plan.chunk + 2 * HALO
    wz, lanes, az, ax, wx = plan.wz, plan.lanes, plan.az, plan.ax, plan.wx
    has_low = jnp.where(place > 0, 1.0, 0.0)
    has_high = jnp.where(place < plan.rows * plan.group - 1, 1.0, 0.0)
    for d in range(3):
        for v in range(5):
            for w in range(5):
                coef[(d * 5 + v) * 5 + w] = jnp.full((8, 128), jac_ref[d, v, w] * (0.5 * TIME_STEP), jnp.float32)
    for v in range(5):
        for i in range(plan.chunk):
            cur[v * tall + HALO + i] = got_ref[pl.ds(v * plan.chunk + i, 8, stride=plan.sent), :]

    def put(low_ref, high_ref):
        for v in range(5):
            for i in range(HALO):
                cur[v * tall + i] = low_ref[v * HALO + i]
                cur[v * tall + HALO + plan.chunk + i] = high_ref[v * HALO + i]

    @pl.when(even)
    def _():
        put(second_ref, first_ref)

    @pl.when(jnp.logical_not(even))
    def _():
        put(first_ref, second_ref)

    lane = lax.broadcasted_iota(jnp.int32, (8, 128), 1)
    sub = lax.broadcasted_iota(jnp.int32, (8, 128), 0)
    x_l, z_l = halves(lane, wz)
    a, b = halves(sub, az)
    zero = jnp.zeros((8, 128), jnp.float32)

    def shifts(value):
        up = pltpu.roll(value, lanes - wz, 1)
        x_next = jnp.where(x_l < wx - 1, up, jnp.where(a < ax - 1, pltpu.roll(up, 8 - az, 0), zero))
        down = pltpu.roll(value, wz, 1)
        x_prev = jnp.where(x_l > 0, down, jnp.where(a > 0, pltpu.roll(down, az, 0), zero))
        up = pltpu.roll(pltpu.roll(value, wz - 1, 1), 7, 0)
        z_next = jnp.where(z_l < wz - 1, pltpu.roll(value, lanes - 1, 1), jnp.where(b < az - 1, up, zero))
        down = pltpu.roll(pltpu.roll(value, lanes - (wz - 1), 1), 1, 0)
        z_prev = jnp.where(z_l > 0, pltpu.roll(value, 1, 1), jnp.where(b > 0, down, zero))
        return x_next, x_prev, z_next, z_prev

    damp = VISCOSITY * TIME_STEP

    def stage(number, src, dst, keep, gain):
        @pl.loop(0, tall // 2 - number)
        def _(pair):
            start = number + 2 * pair
            total = [[None, None] for _ in range(5)]
            slopes = []
            for w in range(5):
                column = [src[w * tall + start + k] for k in (-1, 0, 1, 2)]
                per = []
                for k in range(2):
                    before, center, after = column[k : k + 3]
                    x_next, x_prev, z_next, z_prev = shifts(center)
                    around = ((x_next + x_prev) + (z_next + z_prev)) + (after + before)
                    total[w][k] = (1.0 - 6.0 * damp) * center + damp * around
                    per.append((x_next - x_prev, z_next - z_prev, after - before))
                slopes.append(per)
            for v in range(5):
                for d in range(3):
                    for w in range(5):
                        factor = coef[(d * 5 + v) * 5 + w]
                        for k in range(2):
                            total[v][k] = total[v][k] + factor * slopes[w][k][d]
            for k in range(2):
                at = start + k
                inside = jnp.where(at < HALO, has_low, jnp.where(at >= HALO + plan.chunk, has_high, 1.0))
                for v in range(5):
                    value = total[v][k]
                    if keep:
                        value = keep * cur[v * tall + at] + gain * value
                    dst[v * tall + at] = value * inside

    for step in range(STEPS):
        stage(3 * step + 1, cur, one, 0.0, 1.0)
        stage(3 * step + 2, one, two, 0.75, 0.25)
        stage(3 * step + 3, two, cur, 1.0 / 3.0, 2.0 / 3.0)
        for i in range(plan.chunk):
            at = HALO + i
            planes = [
                cur[at] + cur[4 * tall + at],
                cur[tall + at],
                cur[2 * tall + at],
                cur[3 * tall + at],
            ]
            for ch in range(4):
                samp_ref[pl.ds(i * 128 + ch * STEPS + step, 8, stride=16), :] = planes[ch]
    for v in range(5):
        for i in range(plan.chunk):
            back_ref[pl.ds(v * plan.chunk + i, 8, stride=plan.body), :] = cur[v * tall + HALO + i]


def unpack_kernel(plan, back_ref, out_ref, turned):
    c = lax.axis_index("row")
    for j in range(plan.group):
        q = plan.chunk_of(j, c)
        for v in range(5):
            start = pl.multiple_of(v * plan.wr + q * plan.chunk, 8)
            turned[pl.ds(start, plan.chunk), :] = back_ref[j, v * plan.chunk : (v + 1) * plan.chunk, :]
    for v in range(5):
        out_ref[v] = turned[v * plan.wr : (v + 1) * plan.wr, :].T


def list_kernel(plan, ids_ref, list_ref, count_ref):
    mine, _ = plan.own_chunk()

    def source(g, count):
        def block(n, count):
            for k in range(8):
                cell = ids_ref[g * 8 + k, n]
                lane, r = halves(cell, plan.wr)
                q, r_l = halves(r, plan.chunk)
                list_ref[count] = (r_l * 8 + g) * 128 + lane
                count = count + jnp.where(q == mine, 1, 0)
            return count

        return lax.fori_loop(0, ids_ref[g * 8, 127], block, count)

    count = lax.fori_loop(0, 8, source, 0)
    count_ref[0] = count
    for k in range(8):
        list_ref[count + k] = 0


def dft_kernel(plan, hist_ref, table_ref, live_ref, out_ref):
    tile = pl.program_id(0)
    live = live_ref[0, 0] * 8
    keep = lax.broadcasted_iota(jnp.int32, (64, 128), 1) + tile * 128 < live
    for ch in range(4):
        signal = hist_ref[:, ch, :]
        if ch == 0:
            signal = signal + hist_ref[:, 4, :]
        spec = lax.dot_general(
            table_ref[...],
            signal,
            (((1,), (1,)), ((), ())),
            precision=lax.Precision.HIGHEST,
            preferred_element_type=jnp.float32,
        )
        out_ref[0, ch * 64 : (ch + 1) * 64, :] = jnp.where(keep, spec, 0.0)


def geometry(plan, watch, point):
    offset = [w - p for w, p in zip(watch, point, strict=True)]
    square = offset[0] * offset[0] + offset[1] * offset[1] + offset[2] * offset[2]
    distance = jnp.sqrt(square)
    inverse = 1.0 / distance
    along = [o * inverse for o in offset]
    amplitude = plan.nr * inverse
    sine, cosine = sin_cos(distance * (2.0 / plan.nr))
    near = (plan.nr * 0.5) * inverse
    return along, amplitude, sine, cosine, near


def hist_kernel(plan, first, wide, watch_ref, point_ref, spec_ref, live_ref, out_ref, acc):
    tiles = (live_ref[0, 0] * 8 + 127) // 128
    lane = lax.broadcasted_iota(jnp.int32, (wide, 64), 1)

    @pl.loop(0, out_ref.shape[0] // wide)
    def _(ob):
        start = pl.multiple_of(ob * wide, 8)
        watch = [watch_ref[pl.ds(first + start, wide), d : d + 1] for d in range(3)]
        acc[...] = jnp.zeros_like(acc)

        @pl.loop(0, tiles)
        def _(tile):
            point = [point_ref[tile, d : d + 1, :] for d in range(3)]
            along, amplitude, sine, cosine, near = geometry(plan, watch, point)
            twice = 2.0 * cosine
            cos_last, sin_last = amplitude, jnp.zeros_like(amplitude)
            cos_now, sin_now = amplitude * cosine, amplitude * sine
            for f in range(FREQ):
                rows = [spec_ref[tile, pl.ds(k * 32 + f, 1), :] for k in range(8)]
                d_re = along[0] * rows[2] + along[1] * rows[4] + along[2] * rows[6]
                d_im = along[0] * rows[3] + along[1] * rows[5] + along[2] * rows[7]
                weight = near * (1.0 / (f + 1))
                e_re = (rows[0] + d_re) + weight * d_im
                e_im = (rows[1] + d_im) - weight * d_re
                acc[f] = acc[f] + (sin_now * e_re - cos_now * e_im)
                acc[FREQ + f] = acc[FREQ + f] + (cos_now * e_re + sin_now * e_im)
                cos_now, cos_last = twice * cos_now - cos_last, cos_now
                sin_now, sin_last = twice * sin_now - sin_last, sin_now

        out = jnp.zeros((wide, 64), jnp.float32)
        for f in range(2 * FREQ):
            out = jnp.where(lane == f, jnp.sum(acc[f], axis=1, keepdims=True), out)
        out_ref[pl.ds(start, wide), :] = out


def recent_kernel(plan, parts, list_ref, count_ref, samp_ref, obs_ref, tab_ref, *refs):
    hist_refs, out_ref = refs[:parts], refs[parts]
    value, place, cos_s, sin_s, mono, dip, acc, final = refs[parts + 1 :]
    q, c = plan.own_chunk()
    count = count_ref[0]
    tiles = plan.obs // 128
    lane = lax.broadcasted_iota(jnp.int32, (16, 128), 1)
    acc[...] = jnp.zeros_like(acc)

    @pl.loop(0, (count + 7) // 8)
    def _(group):
        for k in range(8):
            entry = list_ref[group * 8 + k]
            row, at = halves(entry, 128)
            tile = samp_ref[pl.ds(pl.multiple_of(row * 16, 16), 16), :]
            at = jnp.where(group * 8 + k < count, at, -1)
            picked = jnp.sum(jnp.where(lane == at, tile, 0.0), axis=1, keepdims=True)
            value[k * 16 : (k + 1) * 16, :] = jnp.broadcast_to(picked, (16, 128))
            r_l, g = halves(row, 8)
            a, b = halves(g, plan.az)
            _, at = halves(entry, 128)
            x_l, z_l = halves(at, plan.wz)
            spot = (a * plan.wx + x_l, b * plan.wz + z_l, c * plan.wr + q * plan.chunk + r_l)
            for d in range(3):
                place[d * 8 + k : d * 8 + k + 1, :] = jnp.full((1, 128), spot[d].astype(jnp.float32) + 0.5)
        point = [place[d * 8 : (d + 1) * 8, :] for d in range(3)]
        for t in range(tiles):
            seen = obs_ref[:, t * 128 : (t + 1) * 128]
            watch = [
                seen[0:1] * float(plan.nx),
                seen[1:2] * float(plan.nz),
                (1.25 + 0.75 * seen[2:3]) * float(plan.nr),
            ]
            along, amplitude, sine, cosine, near = geometry(plan, watch, point)
            for s in range(STEPS):
                drawn = [value[pl.ds(ch * STEPS + s, 8, stride=16), :] for ch in range(4)]
                push = along[0] * drawn[1] + along[1] * drawn[2] + along[2] * drawn[3]
                mono[s * 8 : (s + 1) * 8, :] = drawn[0] + push
                dip[s * 8 : (s + 1) * 8, :] = near * push
            twice = 2.0 * cosine
            cos_last, sin_last = amplitude, jnp.zeros_like(amplitude)
            cos_now, sin_now = amplitude * cosine, amplitude * sine
            for f in range(FREQ):
                cos_s[f * 8 : (f + 1) * 8, :] = cos_now
                sin_s[f * 8 : (f + 1) * 8, :] = sin_now
                cos_now, cos_last = twice * cos_now - cos_last, cos_now
                sin_now, sin_last = twice * sin_now - sin_last, sin_now
            for fv in range(FREQ // 8):
                base = (t * (FREQ // 8) + fv) * 12
                sums = [acc[base + i] for i in range(12)]
                for k in range(8):
                    wave_c = cos_s[pl.ds(fv * 64 + k, 8, stride=8), :]
                    wave_s = sin_s[pl.ds(fv * 64 + k, 8, stride=8), :]
                    for s in range(STEPS):
                        m = mono[s * 8 + k : s * 8 + k + 1, :]
                        p = dip[s * 8 + k : s * 8 + k + 1, :]
                        sums[4 * s] = sums[4 * s] + wave_c * m
                        sums[4 * s + 1] = sums[4 * s + 1] + wave_s * m
                        sums[4 * s + 2] = sums[4 * s + 2] + wave_c * p
                        sums[4 * s + 3] = sums[4 * s + 3] + wave_s * p
                for i in range(12):
                    acc[base + i] = sums[i]

    scale = 1.0 / math.sqrt(plan.devices * SURF_DEV)
    final[...] = jnp.zeros_like(final)
    for t in range(tiles):
        for fv in range(FREQ // 8):
            base = (t * (FREQ // 8) + fv) * 12
            column = tab_ref[fv * 8 : (fv + 1) * 8, :]
            out_re = jnp.zeros((8, 128), jnp.float32)
            out_im = jnp.zeros((8, 128), jnp.float32)
            below = column[:, 6:7]
            for s in range(STEPS):
                part_re = acc[base + 4 * s + 1] + acc[base + 4 * s + 2] * below
                part_im = acc[base + 4 * s] - acc[base + 4 * s + 3] * below
                turn_re, turn_im = column[:, 2 * s : 2 * s + 1], column[:, 2 * s + 1 : 2 * s + 2]
                out_re = out_re + (turn_re * part_re - turn_im * part_im)
                out_im = out_im + (turn_im * part_re + turn_re * part_im)
            final[fv * 8 : (fv + 1) * 8, :] = out_re
            final[FREQ + fv * 8 : FREQ + (fv + 1) * 8, :] = out_im
        across = final[...].T[:, : 2 * FREQ]
        share = plan.obs // parts
        for i in range(128 // share):
            piece = across[i * share : (i + 1) * share, :]
            row = t * 128 + i * share
            out_ref[row : row + share, :] = (piece + hist_refs[row // share][...]) * scale


def fourier_numpy(samples):
    turn = np.arange(1, FREQ + 1)[:, None] * np.arange(samples)[None, :] % samples
    angle = 2.0 * np.pi / samples * turn
    return np.cos(angle) / np.sqrt(samples), -np.sin(angle) / np.sqrt(samples)


def fast_device(plan, flow_field, flux_jacobian, history, surface_cell, surface_blocks, observers):
    f32 = jnp.float32
    shape = jax.ShapeDtypeStruct
    group, wr, lanes = plan.group, plan.wr, plan.lanes
    tall = plan.chunk + 2 * HALO
    parts = 4
    bind = functools.partial

    packed = call(
        bind(pack_kernel, plan),
        shape((group, plan.sent, lanes), f32),
        [VMEM, VMEM, SMEM],
        VMEM,
        [pltpu.VMEM((5 * wr, lanes), f32)],
        name="pack",
    )(flow_field.reshape(5, lanes, wr), surface_cell, surface_blocks)
    got = lax.all_to_all(packed, GROUP, 0, 0, tiled=True)

    tile_count = plan.capacity // 128
    cos_t, sin_t = fourier_numpy(plan.samples)
    table = np.concatenate([cos_t, sin_t], axis=0).astype(np.float32)
    table[:, plan.samples - STEPS :] = 0.0
    spec = pl.pallas_call(
        bind(dft_kernel, plan),
        out_shape=shape((tile_count, 256, 128), f32),
        grid=(tile_count,),
        in_specs=[
            pl.BlockSpec((128, 5, plan.samples), lambda i: (i, 0, 0)),
            pl.BlockSpec((64, plan.samples), lambda i: (0, 0)),
            SMEM,
        ],
        out_specs=pl.BlockSpec((1, 256, 128), lambda i: (i, 0, 0)),
        name="dft",
        compiler_params=pltpu.CompilerParams(vmem_limit_bytes=40 * 1024 * 1024),
        cost_estimate=pl.CostEstimate(flops=10**9, bytes_accessed=10**6, transcendentals=0),
    )(history, jnp.asarray(table), surface_blocks)

    cell = surface_cell.reshape(-1)
    index_x, index_z, index_r = (lax.axis_index(name) for name in AXES)
    points = jnp.stack(
        [
            index_x * plan.wx + cell // (plan.wz * wr),
            index_z * plan.wz + cell // wr % plan.wz,
            index_r * wr + cell % wr,
        ]
    ).astype(f32) + 0.5
    points = jnp.transpose(points.reshape(3, tile_count, 128), (1, 0, 2))
    watch = jnp.stack(
        [
            observers[0] * plan.nx,
            observers[1] * plan.nz,
            (1.25 + 0.75 * observers[2]) * plan.nr,
        ],
        axis=1,
    )
    share = plan.obs // parts
    wide = 16
    hists = []
    for i in range(parts):
        hists.append(
            call(
                bind(hist_kernel, plan, i * share, wide),
                shape((share, 64), f32),
                [VMEM, VMEM, VMEM, SMEM],
                VMEM,
                [pltpu.VMEM((64, wide, 128), f32)],
                flops=10**9,
                name=f"hist{i}",
            )(watch, points, spec, surface_blocks)
        )

    flat = got.reshape(group * plan.sent, lanes)
    first, second = call(
        bind(edge_kernel, plan),
        (shape((5 * HALO, 8, lanes), f32),) * 2,
        [VMEM],
        (VMEM, VMEM),
        name="edges",
    )(flat)
    line = plan.line()
    swap_a = [(line[i], line[i ^ 1]) for i in range(len(line))]
    swap_b = [
        (line[i], line[((i + 1) ^ 1) - 1]) for i in range(1, len(line) - 1)
    ]
    first = lax.ppermute(first, AXES, swap_a)
    second = lax.ppermute(second, AXES, swap_b)

    ids = got[:, plan.body :, :].astype(jnp.int32).reshape(group * 8, lanes)
    listed, count = call(
        bind(list_kernel, plan),
        (shape((group * plan.capacity + 8,), jnp.int32), shape((1,), jnp.int32)),
        [SMEM],
        (SMEM, SMEM),
        name="list",
    )(ids)

    back, samp = call(
        bind(stencil_kernel, plan),
        (shape((group * plan.body, lanes), f32), shape((plan.chunk * 8 * 16, lanes), f32)),
        [VMEM, VMEM, VMEM, SMEM],
        (VMEM, VMEM),
        [
            pltpu.VMEM((5 * tall, 8, lanes), f32),
            pltpu.VMEM((5 * tall, 8, lanes), f32),
            pltpu.VMEM((5 * tall, 8, lanes), f32),
            pltpu.VMEM((75, 8, lanes), f32),
        ],
        flops=10**9,
        name="stencil",
    )(flat, first, second, flux_jacobian)
    back = lax.all_to_all(back.reshape(group, plan.body, lanes), GROUP, 0, 0, tiled=True)

    columns = np.zeros((FREQ, 8), np.float32)
    for s in range(STEPS):
        columns[:, 2 * s] = cos_t[:, plan.samples - STEPS + s]
        columns[:, 2 * s + 1] = sin_t[:, plan.samples - STEPS + s]
    columns[:, 6] = 1.0 / np.arange(1, FREQ + 1)
    partial = call(
        bind(recent_kernel, plan, parts),
        shape((plan.obs, 2 * FREQ), f32),
        [SMEM, SMEM, VMEM, VMEM, VMEM] + [VMEM] * parts,
        VMEM,
        [
            pltpu.VMEM((128, 128), f32),
            pltpu.VMEM((24, 128), f32),
            pltpu.VMEM((FREQ * 8, 128), f32),
            pltpu.VMEM((FREQ * 8, 128), f32),
            pltpu.VMEM((STEPS * 8, 128), f32),
            pltpu.VMEM((STEPS * 8, 128), f32),
            pltpu.VMEM((plan.obs // 128 * (FREQ // 8) * 12, 8, 128), f32),
            pltpu.VMEM((128, 128), f32),
        ],
        flops=10**9,
        name="recent",
    )(listed, count, samp, observers, jnp.asarray(columns), *hists)
    pieces = lax.all_to_all(
        partial.reshape(plan.devices, plan.per_obs, 2 * FREQ), AXES, 0, 0, tiled=True
    )
    spectrum = jnp.sum(pieces, axis=0)
    field = call(
        bind(unpack_kernel, plan),
        shape((5, lanes, wr), f32),
        [VMEM],
        VMEM,
        [pltpu.VMEM((5 * wr, lanes), f32)],
        name="unpack",
    )(back)
    return field.reshape(flow_field.shape), spectrum


def per_device(*args):
    flow_field, _, history, surface_cell, _, observers = args
    mesh = {name: lax.axis_size(name) for name in AXES}
    plan = Plan(mesh, flow_field.shape[1:], surface_cell.shape, history.shape, observers.shape[1])
    if plan.fits():
        return fast_device(plan, *args)
    return general_device(*args)


def solution(mesh):
    return jax.shard_map(
        per_device,
        mesh=mesh,
        in_specs=(
            P(None, "gx", "gz", "row"),
            P(),
            P(("gx", "gz", "row"), None, None),
            P(("gx", "gz", "row"), None),
            P("row", ("gx", "gz")),
            P(),
        ),
        out_specs=(P(None, "gx", "gz", "row"), P(("gx", "gz", "row"), None)),
        check_vma=False,
    )
```

```python
import functools
import math

import jax
import jax.numpy as jnp
import numpy as np
from jax import lax
from jax.experimental import pallas as pl
from jax.experimental.pallas import tpu as pltpu
from jax.sharding import PartitionSpec as P

SURF_DEV = 128
FREQ = 32
STEPS = 3


TIME_STEP = 0.3
VISCOSITY = 0.05


def padded_2(value, sides, width):
    for axis, dim in sides:
        peers, length = (lax.axis_size(axis), value.shape[dim])
        up = [(i, (i + 1) % peers) for i in range(peers - 1)]
        down = [(j, i) for i, j in up]
        last = lax.slice_in_dim(value, length - width, length, axis=dim)
        leading = lax.slice_in_dim(value, 0, width, axis=dim)
        before = lax.ppermute(last, axis, up)
        after = lax.ppermute(leading, axis, down)
        value = jnp.concatenate([before, value, after], axis=dim)
    return value


def stencil_rate(padded, flux_jacobian):
    center = padded[:, 1:-1, 1:-1, 1:-1]
    along_x = (padded[:, 2:, 1:-1, 1:-1] - padded[:, :-2, 1:-1, 1:-1]) * 0.5
    along_z = (padded[:, 1:-1, 2:, 1:-1] - padded[:, 1:-1, :-2, 1:-1]) * 0.5
    along_r = (padded[:, 1:-1, 1:-1, 2:] - padded[:, 1:-1, 1:-1, :-2]) * 0.5
    beside = padded[:, 2:, 1:-1, 1:-1] + padded[:, :-2, 1:-1, 1:-1]
    beside = beside + padded[:, 1:-1, 2:, 1:-1] + padded[:, 1:-1, :-2, 1:-1]
    beside = beside + padded[:, 1:-1, 1:-1, 2:] + padded[:, 1:-1, 1:-1, :-2]
    slopes = jnp.stack([along_x, along_z, along_r])
    transport = jnp.einsum(
        "dvw,dwxzr->vxzr", flux_jacobian, slopes, precision=lax.Precision.HIGHEST
    )
    return transport + VISCOSITY * (beside - 6.0 * center)


def fourier_table(samples, freq_count):
    time_ids = jnp.arange(samples, dtype=jnp.int32)
    freq_ids = jnp.arange(1, freq_count + 1, dtype=jnp.int32)
    turn_ids = freq_ids[:, None] * time_ids[None, :] % samples
    angles = 2.0 * math.pi / samples * turn_ids.astype(jnp.float32)
    norm_scale = 1.0 / math.sqrt(samples)
    return jnp.concatenate([jnp.cos(angles), -jnp.sin(angles)], axis=0) * norm_scale


def spectra_of(signals, fourier):
    return jnp.einsum("ft,svt->vfs", fourier, signals, precision=lax.Precision.HIGHEST)


def radiate(points, monopole, dipole, watchers, radial_cells, freq_count):
    wavenumbers = jnp.arange(1, freq_count + 1, dtype=jnp.float32) * (2.0 / radial_cells)
    offset_vec = watchers[:, :, None] - points[None, :, :]
    distance = jnp.sqrt(jnp.sum(offset_vec * offset_vec, axis=1))
    direction = offset_vec / distance[:, None, :]
    amplitude = (radial_cells / distance)[:, None, :]
    dip_real = direction[:, 0, None, :] * dipole[0, None, :freq_count, :]
    dip_real = dip_real + direction[:, 1, None, :] * dipole[1, None, :freq_count, :]
    dip_real = dip_real + direction[:, 2, None, :] * dipole[2, None, :freq_count, :]
    dip_imag = direction[:, 0, None, :] * dipole[0, None, freq_count:, :]
    dip_imag = dip_imag + direction[:, 1, None, :] * dipole[1, None, freq_count:, :]
    dip_imag = dip_imag + direction[:, 2, None, :] * dipole[2, None, freq_count:, :]
    mono_real = monopole[None, :freq_count, :]
    mono_imag = monopole[None, freq_count:, :]
    phase_arg = distance[:, None, :] * wavenumbers[None, :, None]
    near_term = 1.0 / phase_arg
    cosine = amplitude * jnp.cos(phase_arg)
    sine = amplitude * jnp.sin(phase_arg)
    plus_weight = cosine * near_term + sine
    minus_weight = cosine - sine * near_term
    out_real = jnp.sum(
        plus_weight * dip_real - minus_weight * dip_imag + sine * mono_real - cosine * mono_imag,
        axis=2,
    )
    out_imag = jnp.sum(
        minus_weight * dip_real + plus_weight * dip_imag + cosine * mono_real + sine * mono_imag,
        axis=2,
    )
    return jnp.concatenate([out_real, out_imag], axis=1)


def general_device(flow_field, flux_jacobian, history, surface_cell, surface_blocks, observers):
    width_x, width_z, width_r = (flow_field.shape[1], flow_field.shape[2], flow_field.shape[3])
    count_x, count_z, count_r = (lax.axis_size("gx"), lax.axis_size("gz"), lax.axis_size("row"))
    index_x, index_z, index_r = (lax.axis_index("gx"), lax.axis_index("gz"), lax.axis_index("row"))
    owners = count_x * count_z
    devices = owners * count_r
    radial_cells = width_r * count_r
    slot_rows = surface_cell.shape[0]
    capacity = slot_rows * owners
    samples = history.shape[2]
    cell_ids = surface_cell.reshape(-1)

    def inside_mask(margin):
        coord_x = index_x * width_x + jnp.arange(width_x + 2 * margin, dtype=jnp.int32) - margin
        coord_z = index_z * width_z + jnp.arange(width_z + 2 * margin, dtype=jnp.int32) - margin
        coord_r = index_r * width_r + jnp.arange(width_r + 2 * margin, dtype=jnp.int32) - margin
        valid_x = (coord_x >= 0) & (coord_x < width_x * count_x)
        valid_z = (coord_z >= 0) & (coord_z < width_z * count_z)
        valid_r = (coord_r >= 0) & (coord_r < radial_cells)
        joined = valid_x[:, None, None] & valid_z[None, :, None] & valid_r[None, None, :]
        return joined.astype(jnp.float32)[None]

    mask_outer = inside_mask(2)
    mask_inner = inside_mask(1)
    current = flow_field
    sampled = []
    for step_index in range(STEPS):
        extended = padded_2(current, (("gx", 1), ("gz", 2), ("row", 3)), 3)
        section_one = (
            extended[:, 1:-1, 1:-1, 1:-1] + TIME_STEP * stencil_rate(extended, flux_jacobian)
        ) * mask_outer
        section_two = 0.75 * extended[:, 2:-2, 2:-2, 2:-2] + 0.25 * (
            section_one[:, 1:-1, 1:-1, 1:-1] + TIME_STEP * stencil_rate(section_one, flux_jacobian)
        )
        section_two = section_two * mask_inner
        current = extended[:, 3:-3, 3:-3, 3:-3] / 3.0 + 2.0 / 3.0 * (
            section_two[:, 1:-1, 1:-1, 1:-1] + TIME_STEP * stencil_rate(section_two, flux_jacobian)
        )
        sampled.append(jnp.take(current.reshape(5, -1), cell_ids, axis=1))
    recent = jnp.transpose(jnp.stack(sampled, axis=2), (1, 0, 2))
    signals = jnp.concatenate([history[:, :, : samples - STEPS], recent], axis=2)
    global_x = index_x * width_x + cell_ids // (width_z * width_r)
    global_z = index_z * width_z + cell_ids // width_r % width_z
    global_r = index_r * width_r + cell_ids % width_r
    positions = jnp.stack([global_x, global_z, global_r]).astype(jnp.float32) + 0.5
    fourier = fourier_table(samples, FREQ)
    live_mask = (jnp.arange(capacity, dtype=jnp.int32) // owners < surface_blocks[0, 0]).astype(
        jnp.float32
    )
    spectra = spectra_of(signals, fourier) * live_mask
    monopole = spectra[0] + spectra[4]
    dipole = spectra[1:4]
    watchers = jnp.stack(
        [
            observers[0] * (width_x * count_x),
            observers[1] * (width_z * count_z),
            (1.25 + 0.75 * observers[2]) * radial_cells,
        ],
        axis=1,
    )
    norm_scale = math.sqrt(devices * SURF_DEV)
    row_count = observers.shape[1] // devices * lax.axis_size(("gx", "gz", "row"))
    block_size = math.gcd(row_count, 32)

    def one_block(block):
        return radiate(positions, monopole, dipole, block, radial_cells, FREQ)

    blocks_out = lax.map(one_block, watchers.reshape(row_count // block_size, block_size, 3))
    spectrum = lax.psum_scatter(
        blocks_out.reshape(row_count, 2 * FREQ) / norm_scale,
        ("gx", "gz", "row"),
        scatter_dimension=0,
        tiled=True,
    )
    return (current, spectrum)


HALO = 3 * STEPS
AXES = ("gx", "gz", "row")
GROUP = ("gx", "gz")
VMEM = pl.BlockSpec(memory_space=pltpu.VMEM)
SMEM = pl.BlockSpec(memory_space=pltpu.SMEM)


def halves(value, by):
    if by & (by - 1) == 0:
        return value >> (by.bit_length() - 1), value & (by - 1)
    return value // by, value % by


def sin_cos(angle):
    turns = jnp.floor(angle * (2.0 / math.pi) + 0.5)
    rest = ((angle - turns * 1.5703125) - turns * 4.837512969970703e-4) - turns * 7.549789954891882e-8
    square = rest * rest
    sine = rest + rest * square * (
        -1.6666654611e-1 + square * (8.3321608736e-3 + square * -1.9515295891e-4)
    )
    cosine = (1.0 - 0.5 * square) + square * square * (
        4.166664568298827e-2 + square * (-1.388731625493765e-3 + square * 2.443315711809948e-5)
    )
    quarter = turns.astype(jnp.int32) & 3
    odd = (quarter & 1) == 1
    out_sine = jnp.where(odd, cosine, sine)
    out_cosine = jnp.where(odd, sine, cosine)
    out_sine = jnp.where(quarter >= 2, -out_sine, out_sine)
    out_cosine = jnp.where((quarter == 1) | (quarter == 2), -out_cosine, out_cosine)
    return out_sine, out_cosine


class Plan:
    def __init__(self, mesh, flow, cells, hist, obs):
        self.ax, self.az, self.rows = mesh["gx"], mesh["gz"], mesh["row"]
        self.group = self.ax * self.az
        self.devices = self.group * self.rows
        self.wx, self.wz, self.wr = flow
        self.blocks = cells[0]
        self.capacity = cells[0] * cells[1]
        self.samples = hist[2]
        self.lanes = self.wx * self.wz
        self.chunk = self.wr // self.group
        self.nx, self.nz, self.nr = self.wx * self.ax, self.wz * self.az, self.wr * self.rows
        self.obs = obs
        self.body = 5 * self.chunk
        self.sent = self.body + 8
        self.per_obs = obs // self.devices
        self.tall_pad = (self.chunk + 2 * HALO + 8) // 8 * 8 + 8

    def fits(self):
        return (
            self.group == 8
            and self.lanes == 128
            and self.wr % 128 == 0
            and self.chunk % 8 == 0
            and self.chunk >= HALO
            and self.capacity == self.blocks * 8
            and self.blocks < 127
            and self.capacity % 128 == 0
            and self.samples == 128
            and self.obs % 128 == 0
            and self.obs % self.devices == 0
            and self.obs // self.devices == 8
            and FREQ == 32
            and STEPS == 3
        )

    def order_of(self, a, b):
        return b * self.ax + (a if b % 2 == 0 else self.ax - 1 - a)

    def table(self):
        return [self.order_of(j // self.az, j % self.az) for j in range(self.group)]

    def line(self):
        out = []
        for c in range(self.rows):
            order = self.table()
            if c % 2:
                order = [self.group - 1 - q for q in order]
            for q in range(self.group):
                out.append(order.index(q) * self.rows + c)
        return out

    def chunk_of(self, j, c):
        q = self.table()[j]
        return jnp.where(c % 2 == 1, self.group - 1 - q, q)

    def own_chunk(self):
        a, b, c = lax.axis_index("gx"), lax.axis_index("gz"), lax.axis_index("row")
        q = b * self.ax + jnp.where(b % 2 == 0, a, self.ax - 1 - a)
        return jnp.where(c % 2 == 1, self.group - 1 - q, q), c


def call(kernel, out_shape, in_specs, out_specs, scratch=(), flops=10**6, name=None):
    return pl.pallas_call(
        kernel,
        out_shape=out_shape,
        in_specs=in_specs,
        out_specs=out_specs,
        scratch_shapes=list(scratch),
        name=name,
        compiler_params=pltpu.CompilerParams(vmem_limit_bytes=40 * 1024 * 1024),
        cost_estimate=pl.CostEstimate(flops=flops, bytes_accessed=10**5, transcendentals=0),
    )


def pack_kernel(plan, flow_ref, cell_ref, live_ref, out_ref, turned):
    c = lax.axis_index("row")
    for v in range(5):
        turned[v * plan.wr : (v + 1) * plan.wr, :] = flow_ref[v].T
    cells = cell_ref[...].astype(jnp.float32)
    ids = jnp.concatenate([cells, jnp.zeros((8, 128 - plan.blocks), jnp.float32)], axis=1)
    lane = lax.broadcasted_iota(jnp.int32, (8, 128), 1)
    ids = jnp.where(lane == 127, live_ref[0, 0].astype(jnp.float32), ids)
    for j in range(plan.group):
        q = plan.chunk_of(j, c)
        for v in range(5):
            start = pl.multiple_of(v * plan.wr + q * plan.chunk, 8)
            out_ref[j, v * plan.chunk : (v + 1) * plan.chunk, :] = turned[pl.ds(start, plan.chunk), :]
        out_ref[j, plan.body : plan.body + 8, :] = ids


def edge_kernel(plan, got_ref, first_ref, second_ref):
    q, c = plan.own_chunk()
    even = (c * plan.group + q) % 2 == 0
    high, low = plan.chunk - HALO, 0
    first = jnp.where(even, high, low)
    second = jnp.where(even, low, high)
    for v in range(5):
        for g in range(plan.group):
            at = (v * plan.group + g) * HALO
            row = g * plan.sent + v * plan.chunk
            first_ref[at : at + HALO, :] = got_ref[pl.ds(row + first, HALO), :]
            second_ref[at : at + HALO, :] = got_ref[pl.ds(row + second, HALO), :]


def stencil_kernel(plan, got_ref, first_ref, second_ref, jac_ref, back_ref, samp_ref, cur, one, two, coef, mask, side):
    q, c = plan.own_chunk()
    place = c * plan.group + q
    even = place % 2 == 0
    tall = plan.chunk + 2 * HALO
    wz, lanes, az, ax, wx = plan.wz, plan.lanes, plan.az, plan.ax, plan.wx
    high = plan.tall_pad
    per = (ax + 2) * az * high

    def base(v, a, b):
        return v * per + ((a + 1) * az + b) * high

    has_low = jnp.where(place > 0, 1.0, 0.0)
    has_high = jnp.where(place < plan.rows * plan.group - 1, 1.0, 0.0)
    row = lax.broadcasted_iota(jnp.int32, (high, 128), 0)
    mask[...] = jnp.where(row < HALO, has_low, jnp.where(row >= HALO + plan.chunk, has_high, 1.0))
    for d in range(3):
        for v in range(5):
            for w in range(5):
                coef[(d * 5 + v) * 5 + w] = jnp.full((8, 128), jac_ref[d, v, w] * (0.5 * TIME_STEP), jnp.float32)
    zeros = jnp.zeros((az * high, 128), jnp.float32)
    for ref in (cur, one, two):
        for v in range(5):
            for a in (-1, ax):
                ref[base(v, a, 0) : base(v, a, 0) + az * high, :] = zeros
    for v in range(5):
        for a in range(ax):
            for b in range(az):
                at = base(v, a, b) + HALO
                source = (a * az + b) * plan.sent + v * plan.chunk
                cur[at : at + plan.chunk, :] = got_ref[source : source + plan.chunk, :]

    def put(low_ref, high_ref):
        for v in range(5):
            for a in range(ax):
                for b in range(az):
                    at = base(v, a, b)
                    source = (v * plan.group + a * az + b) * HALO
                    cur[at : at + HALO, :] = low_ref[source : source + HALO, :]
                    at = at + HALO + plan.chunk
                    cur[at : at + HALO, :] = high_ref[source : source + HALO, :]

    @pl.when(even)
    def _():
        put(second_ref, first_ref)

    @pl.when(jnp.logical_not(even))
    def _():
        put(first_ref, second_ref)

    lane = lax.broadcasted_iota(jnp.int32, (8, 128), 1)
    x_l, z_l = halves(lane, wz)
    zero = jnp.zeros((8, 128), jnp.float32)
    damp = VISCOSITY * TIME_STEP

    many = 2 if ax % 2 == 0 else 1
    spots = [(i, b) for i in range(many) for b in range(az)]
    keys = [(w, i, b) for w in range(5) for i, b in spots]

    def stage(number, src, dst, keep, gain):
        turns = -(-(tall - 2 * number) // 8) * (ax // many)

        def places(turn):
            block, a = halves(turn, ax // many)
            start = number + block * 8
            root = (a * many + 1) * (az * high) + start
            return start, {(w, i, b): root + w * per + (i * az + b) * high for w, i, b in keys}

        def across(turn):
            _, at = places(turn)
            mid = {k: src[pl.ds(at[k], 8), :] for k in keys}
            found = []
            for w, i, b in keys:
                k = (w, i, b)
                ahead, behind = src[pl.ds(at[k] + az * high, 8), :], src[pl.ds(at[k] - az * high, 8), :]
                x_next = pltpu.roll(jnp.where(x_l == 0, ahead, mid[k]), lanes - wz, 1)
                x_prev = pltpu.roll(jnp.where(x_l == wx - 1, behind, mid[k]), wz, 1)
                z_edge = pltpu.roll(mid[w, i, b + 1], wz - 1, 1) if b < az - 1 else zero
                z_next = jnp.where(z_l < wz - 1, pltpu.roll(mid[k], lanes - 1, 1), z_edge)
                z_edge = pltpu.roll(mid[w, i, b - 1], lanes - (wz - 1), 1) if b > 0 else zero
                z_prev = jnp.where(z_l > 0, pltpu.roll(mid[k], 1, 1), z_edge)
                found.append((x_next - x_prev, z_next - z_prev, (x_next + x_prev) + (z_next + z_prev)))
            return found

        def store(found):
            for i, values in enumerate(found):
                for d in range(3):
                    side[3 * i + d] = values[d]

        store(across(0))

        @pl.loop(0, turns)
        def _(turn):
            start, at = places(turn)
            near = {k: [side[3 * i + d] for d in range(3)] for i, k in enumerate(keys)}
            coming = across(jnp.minimum(turn + 1, turns - 1))
            total, slope = {}, {}
            for k in keys:
                after, before = src[pl.ds(at[k] + 1, 8), :], src[pl.ds(at[k] - 1, 8), :]
                slope[k] = near[k][0], near[k][1], after - before
                total[k] = (1.0 - 6.0 * damp) * src[pl.ds(at[k], 8), :] + damp * (near[k][2] + (after + before))
            for v in range(5):
                for d in range(3):
                    for w in range(5):
                        factor = coef[(d * 5 + v) * 5 + w]
                        for i, b in spots:
                            total[v, i, b] = total[v, i, b] + factor * slope[w, i, b][d]
            inside = mask[pl.ds(start, 8), :]
            for k in keys:
                value = total[k]
                if keep:
                    value = keep * cur[pl.ds(at[k], 8), :] + gain * value
                dst[pl.ds(at[k], 8), :] = value * inside
            store(coming)

    for step in range(STEPS):
        stage(3 * step + 1, cur, one, 0.0, 1.0)
        stage(3 * step + 2, one, two, 0.75, 0.25)
        stage(3 * step + 3, two, cur, 1.0 / 3.0, 2.0 / 3.0)
        for a in range(ax):
            for b in range(az):
                for r in range(0, plan.chunk, 8):
                    own = [cur[base(v, a, b) + HALO + r : base(v, a, b) + HALO + r + 8, :] for v in range(5)]
                    own[0] = own[0] + own[4]
                    for ch in range(4):
                        at = (r * plan.group + a * az + b) * 16 + ch * STEPS + step
                        samp_ref[pl.ds(at, 8, stride=plan.group * 16), :] = own[ch]
    for v in range(5):
        for a in range(ax):
            for b in range(az):
                at = base(v, a, b) + HALO
                target = (a * az + b) * plan.body + v * plan.chunk
                back_ref[target : target + plan.chunk, :] = cur[at : at + plan.chunk, :]


def unpack_kernel(plan, back_ref, out_ref, turned):
    c = lax.axis_index("row")
    for j in range(plan.group):
        q = plan.chunk_of(j, c)
        for v in range(5):
            start = pl.multiple_of(v * plan.wr + q * plan.chunk, 8)
            turned[pl.ds(start, plan.chunk), :] = back_ref[j, v * plan.chunk : (v + 1) * plan.chunk, :]
    for v in range(5):
        out_ref[v] = turned[v * plan.wr : (v + 1) * plan.wr, :].T


def list_kernel(plan, entry_ref, list_ref, count_ref):
    def source(g, count):
        def block(n, count):
            found = [entry_ref[g * 8 + k, n] for k in range(8)]
            for entry in found:
                list_ref[count] = entry
                count = count + (entry >> 20)
            return count

        return lax.fori_loop(0, entry_ref[g * 8, 127], block, count)

    count = lax.fori_loop(0, 8, source, 0)
    count_ref[0] = count
    for k in range(8):
        list_ref[count + k] = 0


def entries(plan, ids):
    cell = ids.astype(jnp.int32)
    lane, r = halves(cell, plan.wr)
    q, r_l = halves(r, plan.chunk)
    g = lax.broadcasted_iota(jnp.int32, cell.shape, 0)
    mine, _ = plan.own_chunk()
    entry = (r_l * 8 + g) * 128 + lane + jnp.where(q == mine, 1 << 20, 0)
    last = lax.broadcasted_iota(jnp.int32, cell.shape, 2) == 127
    return jnp.where(last, cell, entry).reshape(plan.group * 8, 128)


def dft_kernel(plan, hist_ref, table_ref, point_ref, live_ref, out_ref):
    tile = pl.program_id(0)
    out_ref[0, 256:259, :] = point_ref[0]
    out_ref[0, 259:264, :] = jnp.full((5, 128), live_ref[0, 0].astype(jnp.float32))
    live = live_ref[0, 0] * 8
    keep = lax.broadcasted_iota(jnp.int32, (64, 128), 1) + tile * 128 < live
    for ch in range(4):
        signal = hist_ref[ch]
        if ch == 0:
            signal = signal + hist_ref[4]
        spec = lax.dot_general(
            table_ref[...],
            signal,
            (((1,), (1,)), ((), ())),
            precision=lax.Precision.HIGHEST,
            preferred_element_type=jnp.float32,
        )
        out_ref[0, ch * 64 : (ch + 1) * 64, :] = jnp.where(keep, spec, 0.0)


def geometry(plan, watch, point):
    offset = [w - p for w, p in zip(watch, point, strict=True)]
    square = offset[0] * offset[0] + offset[1] * offset[1] + offset[2] * offset[2]
    distance = jnp.sqrt(square)
    inverse = 1.0 / distance
    along = [o * inverse for o in offset]
    amplitude = plan.nr * inverse
    sine, cosine = sin_cos(distance * (2.0 / plan.nr))
    near = (plan.nr * 0.5) * inverse
    return along, amplitude, sine, cosine, near


def hist_kernel(plan, first, wide, watch_ref, *refs):
    spec_refs, out_ref, acc = refs[:-2], refs[-2], refs[-1]
    lane = lax.broadcasted_iota(jnp.int32, (wide, 64), 1)
    half = (lax.axis_index("row") % len(spec_refs)) * (plan.obs // len(spec_refs))
    tiles = [(jnp.max(ref[0, 259:260, :]).astype(jnp.int32) * 8 + 127) // 128 for ref in spec_refs]

    @pl.loop(0, out_ref.shape[0] // wide)
    def _(ob):
        start = pl.multiple_of(ob * wide, 8)
        row = pl.multiple_of(half + first + start, 8)
        watch = [jnp.broadcast_to(watch_ref[pl.ds(row, wide), d : d + 1], (wide, 128)) for d in range(3)]
        acc[...] = jnp.zeros_like(acc)

        def radiate_tile(spec_ref, tile):
            point = [spec_ref[tile, 256 + d : 257 + d, :] for d in range(3)]
            along, amplitude, sine, cosine, near = geometry(plan, watch, point)
            twice = 2.0 * cosine
            cos_last, sin_last = amplitude, jnp.zeros_like(amplitude)
            cos_now, sin_now = amplitude * cosine, amplitude * sine
            for f in range(FREQ):
                rows = [spec_ref[tile, pl.ds(k * 32 + f, 1), :] for k in range(8)]
                d_re = along[0] * rows[2] + along[1] * rows[4] + along[2] * rows[6]
                d_im = along[0] * rows[3] + along[1] * rows[5] + along[2] * rows[7]
                weight = near * (1.0 / (f + 1))
                e_re = (rows[0] + d_re) + weight * d_im
                e_im = (rows[1] + d_im) - weight * d_re
                acc[f] = acc[f] + (sin_now * e_re - cos_now * e_im)
                acc[FREQ + f] = acc[FREQ + f] + (cos_now * e_re + sin_now * e_im)
                cos_now, cos_last = twice * cos_now - cos_last, cos_now
                sin_now, sin_last = twice * sin_now - sin_last, sin_now

        for spec_ref, count in zip(spec_refs, tiles, strict=True):
            pl.loop(0, count)(functools.partial(radiate_tile, spec_ref))

        out = jnp.zeros((wide, 64), jnp.float32)
        for f in range(2 * FREQ):
            out = jnp.where(lane == f, jnp.sum(acc[f], axis=1, keepdims=True), out)
        out_ref[pl.ds(start, wide), :] = out


def recent_kernel(plan, parts, list_ref, count_ref, samp_ref, obs_ref, tab_ref, *refs):
    hist_refs, out_ref = refs[:parts], refs[parts]
    value, place, cos_s, sin_s, mono, dip, acc, final = refs[parts + 1 :]
    q, c = plan.own_chunk()
    count = count_ref[0]
    tiles = plan.obs // 128
    lane = lax.broadcasted_iota(jnp.int32, (16, 128), 1)
    acc[...] = jnp.zeros_like(acc)

    @pl.loop(0, (count + 7) // 8)
    def _(group):
        for k in range(8):
            entry = list_ref[group * 8 + k] & ((1 << 20) - 1)
            row, at = halves(entry, 128)
            tile = samp_ref[pl.ds(pl.multiple_of(row * 16, 16), 16), :]
            at = jnp.where(group * 8 + k < count, at, -1)
            picked = jnp.sum(jnp.where(lane == at, tile, 0.0), axis=1, keepdims=True)
            value[k * 16 : (k + 1) * 16, :] = jnp.broadcast_to(picked, (16, 128))
            r_l, g = halves(row, 8)
            a, b = halves(g, plan.az)
            _, at = halves(entry, 128)
            x_l, z_l = halves(at, plan.wz)
            spot = (a * plan.wx + x_l, b * plan.wz + z_l, c * plan.wr + q * plan.chunk + r_l)
            for d in range(3):
                place[d * 8 + k : d * 8 + k + 1, :] = jnp.full((1, 128), spot[d].astype(jnp.float32) + 0.5)
        point = [place[d * 8 : (d + 1) * 8, :] for d in range(3)]
        for t in range(tiles):
            seen = obs_ref[:, t * 128 : (t + 1) * 128]
            watch = [
                seen[0:1] * float(plan.nx),
                seen[1:2] * float(plan.nz),
                (1.25 + 0.75 * seen[2:3]) * float(plan.nr),
            ]
            along, amplitude, sine, cosine, near = geometry(plan, watch, point)
            for s in range(STEPS):
                drawn = [value[pl.ds(ch * STEPS + s, 8, stride=16), :] for ch in range(4)]
                push = along[0] * drawn[1] + along[1] * drawn[2] + along[2] * drawn[3]
                mono[s * 8 : (s + 1) * 8, :] = drawn[0] + push
                dip[s * 8 : (s + 1) * 8, :] = near * push
            twice = 2.0 * cosine
            cos_last, sin_last = amplitude, jnp.zeros_like(amplitude)
            cos_now, sin_now = amplitude * cosine, amplitude * sine
            for f in range(FREQ):
                cos_s[f * 8 : (f + 1) * 8, :] = cos_now
                sin_s[f * 8 : (f + 1) * 8, :] = sin_now
                cos_now, cos_last = twice * cos_now - cos_last, cos_now
                sin_now, sin_last = twice * sin_now - sin_last, sin_now
            for fv in range(FREQ // 8):
                base = (t * (FREQ // 8) + fv) * 12
                sums = [acc[base + i] for i in range(12)]
                for k in range(8):
                    wave_c = cos_s[pl.ds(fv * 64 + k, 8, stride=8), :]
                    wave_s = sin_s[pl.ds(fv * 64 + k, 8, stride=8), :]
                    for s in range(STEPS):
                        m = mono[s * 8 + k : s * 8 + k + 1, :]
                        p = dip[s * 8 + k : s * 8 + k + 1, :]
                        sums[4 * s] = sums[4 * s] + wave_c * m
                        sums[4 * s + 1] = sums[4 * s + 1] + wave_s * m
                        sums[4 * s + 2] = sums[4 * s + 2] + wave_c * p
                        sums[4 * s + 3] = sums[4 * s + 3] + wave_s * p
                for i in range(12):
                    acc[base + i] = sums[i]

    scale = 1.0 / math.sqrt(plan.devices * SURF_DEV)
    final[...] = jnp.zeros_like(final)
    for t in range(tiles):
        for fv in range(FREQ // 8):
            base = (t * (FREQ // 8) + fv) * 12
            column = tab_ref[fv * 8 : (fv + 1) * 8, :]
            out_re = jnp.zeros((8, 128), jnp.float32)
            out_im = jnp.zeros((8, 128), jnp.float32)
            below = column[:, 6:7]
            for s in range(STEPS):
                part_re = acc[base + 4 * s + 1] + acc[base + 4 * s + 2] * below
                part_im = acc[base + 4 * s] - acc[base + 4 * s + 3] * below
                turn_re, turn_im = column[:, 2 * s : 2 * s + 1], column[:, 2 * s + 1 : 2 * s + 2]
                out_re = out_re + (turn_re * part_re - turn_im * part_im)
                out_im = out_im + (turn_im * part_re + turn_re * part_im)
            final[fv * 8 : (fv + 1) * 8, :] = out_re
            final[FREQ + fv * 8 : FREQ + (fv + 1) * 8, :] = out_im
        out_ref[t * 128 : (t + 1) * 128, :] = final[...].T * scale
    share = hist_refs[0].shape[0]
    ways = plan.obs // (share * parts)
    half = (lax.axis_index("row") % ways) * (share * parts)
    for i in range(parts):
        row = pl.multiple_of(half + i * share, 8)
        out_ref[pl.ds(row, share), : 2 * FREQ] = out_ref[pl.ds(row, share), : 2 * FREQ] + hist_refs[i][...] * scale


def sum_kernel(pieces_ref, out_ref):
    out_ref[...] = jnp.sum(pieces_ref[...], axis=0)[:, : out_ref.shape[1]]


def fourier_numpy(samples):
    turn = np.arange(1, FREQ + 1)[:, None] * np.arange(samples)[None, :] % samples
    angle = 2.0 * np.pi / samples * turn
    return np.cos(angle) / np.sqrt(samples), -np.sin(angle) / np.sqrt(samples)


def fast_device(plan, flow_field, flux_jacobian, history, surface_cell, surface_blocks, observers):
    f32 = jnp.float32
    shape = jax.ShapeDtypeStruct
    group, wr, lanes = plan.group, plan.wr, plan.lanes
    field_rows = 5 * (plan.ax + 2) * plan.az * plan.tall_pad
    parts = 4
    bind = functools.partial

    packed = call(
        bind(pack_kernel, plan),
        shape((group, plan.sent, lanes), f32),
        [VMEM, VMEM, SMEM],
        VMEM,
        [pltpu.VMEM((5 * wr, lanes), f32)],
        name="pack",
    )(flow_field.reshape(5, lanes, wr), surface_cell.T, surface_blocks)
    packed, surface_cell = lax.optimization_barrier((packed, surface_cell))
    got = lax.all_to_all(packed, GROUP, 0, 0, tiled=True)

    tile_count = plan.capacity // 128
    cell = surface_cell.reshape(-1)
    index_x, index_z, index_r = (lax.axis_index(name) for name in AXES)
    points = jnp.stack(
        [
            index_x * plan.wx + cell // (plan.wz * wr),
            index_z * plan.wz + cell // wr % plan.wz,
            index_r * wr + cell % wr,
        ]
    ).astype(f32) + 0.5
    points = jnp.transpose(points.reshape(3, tile_count, 128), (1, 0, 2))
    cos_t, sin_t = fourier_numpy(plan.samples)
    table = np.concatenate([cos_t, sin_t], axis=0).astype(np.float32)
    table[:, plan.samples - STEPS :] = 0.0
    spec = pl.pallas_call(
        bind(dft_kernel, plan),
        out_shape=shape((tile_count, 264, 128), f32),
        grid=(tile_count,),
        in_specs=[
            pl.BlockSpec((5, 128, plan.samples), lambda i: (0, i, 0)),
            pl.BlockSpec((64, plan.samples), lambda i: (0, 0)),
            pl.BlockSpec((1, 3, 128), lambda i: (i, 0, 0)),
            SMEM,
        ],
        out_specs=pl.BlockSpec((1, 264, 128), lambda i: (i, 0, 0)),
        name="dft",
        compiler_params=pltpu.CompilerParams(vmem_limit_bytes=40 * 1024 * 1024),
        cost_estimate=pl.CostEstimate(flops=10**9, bytes_accessed=10**6, transcendentals=0),
    )(jnp.transpose(history, (1, 0, 2)), jnp.asarray(table), points, surface_blocks)

    watch = jnp.stack(
        [
            observers[0] * plan.nx,
            observers[1] * plan.nz,
            (1.25 + 0.75 * observers[2]) * plan.nr,
        ],
        axis=1,
    )
    sources = [spec]
    if plan.rows % 2 == 0:
        sources.append(lax.ppermute(spec, "row", [(i, i ^ 1) for i in range(plan.rows)]))
    share = plan.obs // len(sources) // parts
    wide = 32
    hists = []
    for i in range(parts):
        hists.append(
            call(
                bind(hist_kernel, plan, i * share, wide),
                shape((share, 64), f32),
                [VMEM] * (1 + len(sources)),
                VMEM,
                [pltpu.VMEM((64, wide, 128), f32)],
                flops=10**9,
                name=f"hist{i}",
            )(watch, *sources)
        )

    flat = got.reshape(group * plan.sent, lanes)
    flat, hists[0], hists[1] = lax.optimization_barrier((flat, hists[0], hists[1]))
    first, second = call(
        bind(edge_kernel, plan),
        (shape((5 * group * HALO, lanes), f32),) * 2,
        [VMEM],
        (VMEM, VMEM),
        name="edges",
    )(flat)
    line = plan.line()
    swap_a = [(line[i], line[i ^ 1]) for i in range(len(line))]
    swap_b = [
        (line[i], line[((i + 1) ^ 1) - 1]) for i in range(1, len(line) - 1)
    ]
    first = lax.ppermute(first, AXES, swap_a)
    second = lax.ppermute(second, AXES, swap_b)

    ids = entries(plan, got[:, plan.body :, :])
    listed, count = call(
        bind(list_kernel, plan),
        (shape((group * plan.capacity + 8,), jnp.int32), shape((1,), jnp.int32)),
        [SMEM],
        (SMEM, SMEM),
        name="list",
    )(ids)

    flat, listed, count, hists = lax.optimization_barrier((flat, listed, count, hists))
    back, samp = call(
        bind(stencil_kernel, plan),
        (shape((group * plan.body, lanes), f32), shape((plan.chunk * 8 * 16, lanes), f32)),
        [VMEM, VMEM, VMEM, SMEM],
        (VMEM, VMEM),
        [
            pltpu.VMEM((field_rows, lanes), f32),
            pltpu.VMEM((field_rows, lanes), f32),
            pltpu.VMEM((field_rows, lanes), f32),
            pltpu.VMEM((75, 8, lanes), f32),
            pltpu.VMEM((plan.tall_pad, lanes), f32),
            pltpu.VMEM((30 * plan.az, 8, lanes), f32),
        ],
        flops=10**9,
        name="stencil",
    )(flat, first, second, flux_jacobian)
    back = lax.all_to_all(back.reshape(group, plan.body, lanes), GROUP, 0, 0, tiled=True)

    columns = np.zeros((FREQ, 8), np.float32)
    for s in range(STEPS):
        columns[:, 2 * s] = cos_t[:, plan.samples - STEPS + s]
        columns[:, 2 * s + 1] = sin_t[:, plan.samples - STEPS + s]
    columns[:, 6] = 1.0 / np.arange(1, FREQ + 1)
    partial = call(
        bind(recent_kernel, plan, parts),
        shape((plan.obs, 128), f32),
        [SMEM, SMEM, VMEM, VMEM, VMEM] + [VMEM] * parts,
        VMEM,
        [
            pltpu.VMEM((128, 128), f32),
            pltpu.VMEM((24, 128), f32),
            pltpu.VMEM((FREQ * 8, 128), f32),
            pltpu.VMEM((FREQ * 8, 128), f32),
            pltpu.VMEM((STEPS * 8, 128), f32),
            pltpu.VMEM((STEPS * 8, 128), f32),
            pltpu.VMEM((plan.obs // 128 * (FREQ // 8) * 12, 8, 128), f32),
            pltpu.VMEM((128, 128), f32),
        ],
        flops=10**9,
        name="recent",
    )(listed, count, samp, observers, jnp.asarray(columns), *hists)
    partial, back = lax.optimization_barrier((partial, back))
    pieces = lax.all_to_all(
        partial.reshape(plan.devices, plan.per_obs, 128), AXES, 0, 0, tiled=True
    )
    spectrum = call(
        sum_kernel, shape((plan.per_obs, 2 * FREQ), f32), [VMEM], VMEM, name="sum"
    )(pieces)
    field = call(
        bind(unpack_kernel, plan),
        shape((5, lanes, wr), f32),
        [VMEM],
        VMEM,
        [pltpu.VMEM((5 * wr, lanes), f32)],
        name="unpack",
    )(back)
    return field.reshape(flow_field.shape), spectrum


def per_device(*args):
    flow_field, _, history, surface_cell, _, observers = args
    mesh = {name: lax.axis_size(name) for name in AXES}
    plan = Plan(mesh, flow_field.shape[1:], surface_cell.shape, history.shape, observers.shape[1])
    if plan.fits():
        return fast_device(plan, *args)
    return general_device(*args)


def solution(mesh):
    return jax.shard_map(
        per_device,
        mesh=mesh,
        in_specs=(
            P(None, "gx", "gz", "row"),
            P(),
            P(("gx", "gz", "row"), None, None),
            P(("gx", "gz", "row"), None),
            P("row", ("gx", "gz")),
            P(),
        ),
        out_specs=(P(None, "gx", "gz", "row"), P(("gx", "gz", "row"), None)),
        check_vma=False,
    )
```

```python
import functools
import math

import jax
import jax.numpy as jnp
import numpy as np
from jax import lax
from jax.experimental import pallas as pl
from jax.experimental.pallas import tpu as pltpu
from jax.sharding import PartitionSpec as P

SURF_DEV = 128
FREQ = 32
STEPS = 3


TIME_STEP = 0.3
VISCOSITY = 0.05


def padded_2(value, sides, width):
    for axis, dim in sides:
        peers, length = (lax.axis_size(axis), value.shape[dim])
        up = [(i, (i + 1) % peers) for i in range(peers - 1)]
        down = [(j, i) for i, j in up]
        last = lax.slice_in_dim(value, length - width, length, axis=dim)
        leading = lax.slice_in_dim(value, 0, width, axis=dim)
        before = lax.ppermute(last, axis, up)
        after = lax.ppermute(leading, axis, down)
        value = jnp.concatenate([before, value, after], axis=dim)
    return value


def stencil_rate(padded, flux_jacobian):
    center = padded[:, 1:-1, 1:-1, 1:-1]
    along_x = (padded[:, 2:, 1:-1, 1:-1] - padded[:, :-2, 1:-1, 1:-1]) * 0.5
    along_z = (padded[:, 1:-1, 2:, 1:-1] - padded[:, 1:-1, :-2, 1:-1]) * 0.5
    along_r = (padded[:, 1:-1, 1:-1, 2:] - padded[:, 1:-1, 1:-1, :-2]) * 0.5
    beside = padded[:, 2:, 1:-1, 1:-1] + padded[:, :-2, 1:-1, 1:-1]
    beside = beside + padded[:, 1:-1, 2:, 1:-1] + padded[:, 1:-1, :-2, 1:-1]
    beside = beside + padded[:, 1:-1, 1:-1, 2:] + padded[:, 1:-1, 1:-1, :-2]
    slopes = jnp.stack([along_x, along_z, along_r])
    transport = jnp.einsum(
        "dvw,dwxzr->vxzr", flux_jacobian, slopes, precision=lax.Precision.HIGHEST
    )
    return transport + VISCOSITY * (beside - 6.0 * center)


def fourier_table(samples, freq_count):
    time_ids = jnp.arange(samples, dtype=jnp.int32)
    freq_ids = jnp.arange(1, freq_count + 1, dtype=jnp.int32)
    turn_ids = freq_ids[:, None] * time_ids[None, :] % samples
    angles = 2.0 * math.pi / samples * turn_ids.astype(jnp.float32)
    norm_scale = 1.0 / math.sqrt(samples)
    return jnp.concatenate([jnp.cos(angles), -jnp.sin(angles)], axis=0) * norm_scale


def spectra_of(signals, fourier):
    return jnp.einsum("ft,svt->vfs", fourier, signals, precision=lax.Precision.HIGHEST)


def radiate(points, monopole, dipole, watchers, radial_cells, freq_count):
    wavenumbers = jnp.arange(1, freq_count + 1, dtype=jnp.float32) * (2.0 / radial_cells)
    offset_vec = watchers[:, :, None] - points[None, :, :]
    distance = jnp.sqrt(jnp.sum(offset_vec * offset_vec, axis=1))
    direction = offset_vec / distance[:, None, :]
    amplitude = (radial_cells / distance)[:, None, :]
    dip_real = direction[:, 0, None, :] * dipole[0, None, :freq_count, :]
    dip_real = dip_real + direction[:, 1, None, :] * dipole[1, None, :freq_count, :]
    dip_real = dip_real + direction[:, 2, None, :] * dipole[2, None, :freq_count, :]
    dip_imag = direction[:, 0, None, :] * dipole[0, None, freq_count:, :]
    dip_imag = dip_imag + direction[:, 1, None, :] * dipole[1, None, freq_count:, :]
    dip_imag = dip_imag + direction[:, 2, None, :] * dipole[2, None, freq_count:, :]
    mono_real = monopole[None, :freq_count, :]
    mono_imag = monopole[None, freq_count:, :]
    phase_arg = distance[:, None, :] * wavenumbers[None, :, None]
    near_term = 1.0 / phase_arg
    cosine = amplitude * jnp.cos(phase_arg)
    sine = amplitude * jnp.sin(phase_arg)
    plus_weight = cosine * near_term + sine
    minus_weight = cosine - sine * near_term
    out_real = jnp.sum(
        plus_weight * dip_real - minus_weight * dip_imag + sine * mono_real - cosine * mono_imag,
        axis=2,
    )
    out_imag = jnp.sum(
        minus_weight * dip_real + plus_weight * dip_imag + cosine * mono_real + sine * mono_imag,
        axis=2,
    )
    return jnp.concatenate([out_real, out_imag], axis=1)


def general_device(flow_field, flux_jacobian, history, surface_cell, surface_blocks, observers):
    width_x, width_z, width_r = (flow_field.shape[1], flow_field.shape[2], flow_field.shape[3])
    count_x, count_z, count_r = (lax.axis_size("gx"), lax.axis_size("gz"), lax.axis_size("row"))
    index_x, index_z, index_r = (lax.axis_index("gx"), lax.axis_index("gz"), lax.axis_index("row"))
    owners = count_x * count_z
    devices = owners * count_r
    radial_cells = width_r * count_r
    slot_rows = surface_cell.shape[0]
    capacity = slot_rows * owners
    samples = history.shape[2]
    cell_ids = surface_cell.reshape(-1)

    def inside_mask(margin):
        coord_x = index_x * width_x + jnp.arange(width_x + 2 * margin, dtype=jnp.int32) - margin
        coord_z = index_z * width_z + jnp.arange(width_z + 2 * margin, dtype=jnp.int32) - margin
        coord_r = index_r * width_r + jnp.arange(width_r + 2 * margin, dtype=jnp.int32) - margin
        valid_x = (coord_x >= 0) & (coord_x < width_x * count_x)
        valid_z = (coord_z >= 0) & (coord_z < width_z * count_z)
        valid_r = (coord_r >= 0) & (coord_r < radial_cells)
        joined = valid_x[:, None, None] & valid_z[None, :, None] & valid_r[None, None, :]
        return joined.astype(jnp.float32)[None]

    mask_outer = inside_mask(2)
    mask_inner = inside_mask(1)
    current = flow_field
    sampled = []
    for step_index in range(STEPS):
        extended = padded_2(current, (("gx", 1), ("gz", 2), ("row", 3)), 3)
        section_one = (
            extended[:, 1:-1, 1:-1, 1:-1] + TIME_STEP * stencil_rate(extended, flux_jacobian)
        ) * mask_outer
        section_two = 0.75 * extended[:, 2:-2, 2:-2, 2:-2] + 0.25 * (
            section_one[:, 1:-1, 1:-1, 1:-1] + TIME_STEP * stencil_rate(section_one, flux_jacobian)
        )
        section_two = section_two * mask_inner
        current = extended[:, 3:-3, 3:-3, 3:-3] / 3.0 + 2.0 / 3.0 * (
            section_two[:, 1:-1, 1:-1, 1:-1] + TIME_STEP * stencil_rate(section_two, flux_jacobian)
        )
        sampled.append(jnp.take(current.reshape(5, -1), cell_ids, axis=1))
    recent = jnp.transpose(jnp.stack(sampled, axis=2), (1, 0, 2))
    signals = jnp.concatenate([history[:, :, : samples - STEPS], recent], axis=2)
    global_x = index_x * width_x + cell_ids // (width_z * width_r)
    global_z = index_z * width_z + cell_ids // width_r % width_z
    global_r = index_r * width_r + cell_ids % width_r
    positions = jnp.stack([global_x, global_z, global_r]).astype(jnp.float32) + 0.5
    fourier = fourier_table(samples, FREQ)
    live_mask = (jnp.arange(capacity, dtype=jnp.int32) // owners < surface_blocks[0, 0]).astype(
        jnp.float32
    )
    spectra = spectra_of(signals, fourier) * live_mask
    monopole = spectra[0] + spectra[4]
    dipole = spectra[1:4]
    watchers = jnp.stack(
        [
            observers[0] * (width_x * count_x),
            observers[1] * (width_z * count_z),
            (1.25 + 0.75 * observers[2]) * radial_cells,
        ],
        axis=1,
    )
    norm_scale = math.sqrt(devices * SURF_DEV)
    row_count = observers.shape[1] // devices * lax.axis_size(("gx", "gz", "row"))
    block_size = math.gcd(row_count, 32)

    def one_block(block):
        return radiate(positions, monopole, dipole, block, radial_cells, FREQ)

    blocks_out = lax.map(one_block, watchers.reshape(row_count // block_size, block_size, 3))
    spectrum = lax.psum_scatter(
        blocks_out.reshape(row_count, 2 * FREQ) / norm_scale,
        ("gx", "gz", "row"),
        scatter_dimension=0,
        tiled=True,
    )
    return (current, spectrum)


HALO = 3 * STEPS
AXES = ("gx", "gz", "row")
GROUP = ("gx", "gz")
VMEM = pl.BlockSpec(memory_space=pltpu.VMEM)
SMEM = pl.BlockSpec(memory_space=pltpu.SMEM)


def halves(value, by):
    if by & (by - 1) == 0:
        return value >> (by.bit_length() - 1), value & (by - 1)
    return value // by, value % by


def sin_cos(angle):
    turns = jnp.floor(angle * (2.0 / math.pi) + 0.5)
    rest = ((angle - turns * 1.5703125) - turns * 4.837512969970703e-4) - turns * 7.549789954891882e-8
    square = rest * rest
    sine = rest + rest * square * (
        -1.6666654611e-1 + square * (8.3321608736e-3 + square * -1.9515295891e-4)
    )
    cosine = (1.0 - 0.5 * square) + square * square * (
        4.166664568298827e-2 + square * (-1.388731625493765e-3 + square * 2.443315711809948e-5)
    )
    quarter = turns.astype(jnp.int32) & 3
    odd = (quarter & 1) == 1
    out_sine = jnp.where(odd, cosine, sine)
    out_cosine = jnp.where(odd, sine, cosine)
    out_sine = jnp.where(quarter >= 2, -out_sine, out_sine)
    out_cosine = jnp.where((quarter == 1) | (quarter == 2), -out_cosine, out_cosine)
    return out_sine, out_cosine


class Plan:
    def __init__(self, mesh, flow, cells, hist, obs):
        self.ax, self.az, self.rows = mesh["gx"], mesh["gz"], mesh["row"]
        self.group = self.ax * self.az
        self.devices = self.group * self.rows
        self.wx, self.wz, self.wr = flow
        self.blocks = cells[0]
        self.capacity = cells[0] * cells[1]
        self.samples = hist[2]
        self.lanes = self.wx * self.wz
        self.chunk = self.wr // self.group
        self.nx, self.nz, self.nr = self.wx * self.ax, self.wz * self.az, self.wr * self.rows
        self.obs = obs
        self.body = 5 * self.chunk
        self.sent = self.body + 8
        self.per_obs = obs // self.devices
        self.tall_pad = (self.chunk + 2 * HALO + 8) // 8 * 8 + 8

    def fits(self):
        return (
            self.group == 8
            and self.lanes == 128
            and self.wr % 128 == 0
            and self.chunk % 8 == 0
            and self.chunk >= 2 * 8
            and self.chunk >= HALO
            and self.capacity == self.blocks * 8
            and self.blocks < 127
            and self.capacity % 128 == 0
            and self.samples == 128
            and self.obs % 128 == 0
            and self.obs % self.devices == 0
            and self.obs // self.devices == 8
            and FREQ == 32
            and STEPS == 3
        )

    def order_of(self, a, b):
        return b * self.ax + (a if b % 2 == 0 else self.ax - 1 - a)

    def table(self):
        return [self.order_of(j // self.az, j % self.az) for j in range(self.group)]

    def line(self):
        out = []
        for c in range(self.rows):
            order = self.table()
            if c % 2:
                order = [self.group - 1 - q for q in order]
            for q in range(self.group):
                out.append(order.index(q) * self.rows + c)
        return out

    def chunk_of(self, j, c):
        q = self.table()[j]
        return jnp.where(c % 2 == 1, self.group - 1 - q, q)

    def own_chunk(self):
        a, b, c = lax.axis_index("gx"), lax.axis_index("gz"), lax.axis_index("row")
        q = b * self.ax + jnp.where(b % 2 == 0, a, self.ax - 1 - a)
        return jnp.where(c % 2 == 1, self.group - 1 - q, q), c


def call(kernel, out_shape, in_specs, out_specs, scratch=(), flops=10**6, name=None):
    return pl.pallas_call(
        kernel,
        out_shape=out_shape,
        in_specs=in_specs,
        out_specs=out_specs,
        scratch_shapes=list(scratch),
        name=name,
        compiler_params=pltpu.CompilerParams(vmem_limit_bytes=40 * 1024 * 1024),
        cost_estimate=pl.CostEstimate(flops=flops, bytes_accessed=10**5, transcendentals=0),
    )


def pack_kernel(plan, flow_ref, cell_ref, live_ref, out_ref, turned):
    c = lax.axis_index("row")
    for v in range(5):
        turned[v * plan.wr : (v + 1) * plan.wr, :] = flow_ref[v].T
    cells = cell_ref[...].astype(jnp.float32)
    ids = jnp.concatenate([cells, jnp.zeros((8, 128 - plan.blocks), jnp.float32)], axis=1)
    lane = lax.broadcasted_iota(jnp.int32, (8, 128), 1)
    ids = jnp.where(lane == 127, live_ref[0, 0].astype(jnp.float32), ids)
    for j in range(plan.group):
        q = plan.chunk_of(j, c)
        for v in range(5):
            start = pl.multiple_of(v * plan.wr + q * plan.chunk, 8)
            out_ref[j, v * plan.chunk : (v + 1) * plan.chunk, :] = turned[pl.ds(start, plan.chunk), :]
        out_ref[j, plan.body : plan.body + 8, :] = ids


def edge_kernel(plan, got_ref, first_ref, second_ref):
    q, c = plan.own_chunk()
    even = (c * plan.group + q) % 2 == 0
    high, low = plan.chunk - HALO, 0
    first = jnp.where(even, high, low)
    second = jnp.where(even, low, high)
    for v in range(5):
        for g in range(plan.group):
            at = (v * plan.group + g) * HALO
            row = g * plan.sent + v * plan.chunk
            first_ref[at : at + HALO, :] = got_ref[pl.ds(row + first, HALO), :]
            second_ref[at : at + HALO, :] = got_ref[pl.ds(row + second, HALO), :]


def stencil_kernel(plan, got_ref, first_ref, second_ref, jac_ref, back_ref, samp_ref, grid, coef, mask, side):
    q, c = plan.own_chunk()
    place = c * plan.group + q
    even = place % 2 == 0
    tall = plan.chunk + 2 * HALO
    wz, lanes, az, ax, wx = plan.wz, plan.lanes, plan.az, plan.ax, plan.wx
    high = plan.tall_pad
    per = (ax + 2) * az * high

    def base(v, a, b):
        return v * per + ((a + 1) * az + b) * high

    has_low = jnp.where(place > 0, 1.0, 0.0)
    has_high = jnp.where(place < plan.rows * plan.group - 1, 1.0, 0.0)
    row = lax.broadcasted_iota(jnp.int32, (high, 128), 0)
    mask[...] = jnp.where(row < HALO, has_low, jnp.where(row >= HALO + plan.chunk, has_high, 1.0))
    for d in range(3):
        for v in range(5):
            for w in range(5):
                coef[(d * 5 + v) * 5 + w] = jnp.full((8, 128), jac_ref[d, v, w] * (0.5 * TIME_STEP), jnp.float32)
    zeros = jnp.zeros((az * high, 128), jnp.float32)
    for buffer in range(3):
        for v in range(5):
            for a in (-1, ax):
                at = buffer * 5 * per + base(v, a, 0)
                grid[at : at + az * high, :] = zeros
    for v in range(5):
        for a in range(ax):
            for b in range(az):
                at = base(v, a, b) + HALO
                source = (a * az + b) * plan.sent + v * plan.chunk
                grid[at : at + plan.chunk, :] = got_ref[source : source + plan.chunk, :]

    def put(low_ref, high_ref):
        for v in range(5):
            for a in range(ax):
                for b in range(az):
                    at = base(v, a, b)
                    source = (v * plan.group + a * az + b) * HALO
                    grid[at : at + HALO, :] = low_ref[source : source + HALO, :]
                    at = at + HALO + plan.chunk
                    grid[at : at + HALO, :] = high_ref[source : source + HALO, :]

    @pl.when(even)
    def _():
        put(second_ref, first_ref)

    @pl.when(jnp.logical_not(even))
    def _():
        put(first_ref, second_ref)

    lane = lax.broadcasted_iota(jnp.int32, (8, 128), 1)
    x_l, z_l = halves(lane, wz)
    zero = jnp.zeros((8, 128), jnp.float32)
    damp = VISCOSITY * TIME_STEP

    many = 2 if ax % 2 == 0 else 1
    spots = [(i, b) for i in range(many) for b in range(az)]
    keys = [(w, i, b) for w in range(5) for i, b in spots]
    whole = 5 * per
    far = {(w, i, b): w * per + (i * az + b) * high for w, i, b in keys}
    side_step = az * high

    def turns_of(number):
        return ((tall - 2 * number + 7) >> 3) * (ax // many)

    def places(number, turn):
        block, a = halves(turn, ax // many)
        start = number + block * 8
        return start, (a * many + 1) * (az * high) + start

    def across(number, turn, offset):
        _, root = places(number, turn)
        root = root + offset
        mid = {k: grid[pl.ds(root + far[k], 8), :] for k in keys}
        found = []
        for w, i, b in keys:
            k = (w, i, b)
            ahead = grid[pl.ds(root + (far[k] + side_step), 8), :]
            behind = grid[pl.ds(root + (far[k] - side_step), 8), :]
            x_next = pltpu.roll(jnp.where(x_l == 0, ahead, mid[k]), lanes - wz, 1)
            x_prev = pltpu.roll(jnp.where(x_l == wx - 1, behind, mid[k]), wz, 1)
            z_edge = pltpu.roll(mid[w, i, b + 1], wz - 1, 1) if b < az - 1 else zero
            z_next = jnp.where(z_l < wz - 1, pltpu.roll(mid[k], lanes - 1, 1), z_edge)
            z_edge = pltpu.roll(mid[w, i, b - 1], lanes - (wz - 1), 1) if b > 0 else zero
            z_prev = jnp.where(z_l > 0, pltpu.roll(mid[k], 1, 1), z_edge)
            found.append((x_next - x_prev, z_next - z_prev, (x_next + x_prev) + (z_next + z_prev)))
        return found

    def store(found):
        for i, values in enumerate(found):
            for d in range(3):
                side[3 * i + d] = values[d]

    store(across(1, 0, 0))

    for step in range(STEPS):

        @pl.loop(0, 3)
        def _(part):
            number = 3 * step + 1 + part
            source = part * whole
            target = jnp.where(part == 2, 0, source + whole)
            keep = jnp.where(part == 0, 0.0, jnp.where(part == 1, 0.75, 1.0 / 3.0))
            gain = jnp.where(part == 0, 1.0, jnp.where(part == 1, 0.25, 2.0 / 3.0))
            turns = turns_of(number)

            @pl.loop(0, turns)
            def _(turn):
                start, root = places(number, turn)
                here, there = root + source, root + target
                near = {k: [side[3 * i + d] for d in range(3)] for i, k in enumerate(keys)}
                last = turn + 1 >= turns
                coming = across(
                    jnp.where(last, number + 1, number),
                    jnp.where(last, 0, turn + 1),
                    jnp.where(last, target, source),
                )
                total, slope = {}, {}
                for k in keys:
                    after, before = grid[pl.ds(here + (far[k] + 1), 8), :], grid[pl.ds(here + (far[k] - 1), 8), :]
                    slope[k] = near[k][0], near[k][1], after - before
                    total[k] = (1.0 - 6.0 * damp) * grid[pl.ds(here + far[k], 8), :] + damp * (near[k][2] + (after + before))
                for v in range(5):
                    for d in range(3):
                        for w in range(5):
                            factor = coef[(d * 5 + v) * 5 + w]
                            for i, b in spots:
                                total[v, i, b] = total[v, i, b] + factor * slope[w, i, b][d]
                inside = mask[pl.ds(start, 8), :]
                for k in keys:
                    value = keep * grid[pl.ds(root + far[k], 8), :] + gain * total[k]
                    grid[pl.ds(there + far[k], 8), :] = value * inside
                store(coming)

        for a in range(ax):
            for b in range(az):
                for r in range(0, plan.chunk, 8):
                    own = [grid[base(v, a, b) + HALO + r : base(v, a, b) + HALO + r + 8, :] for v in range(5)]
                    own[0] = own[0] + own[4]
                    for ch in range(4):
                        at = (r * plan.group + a * az + b) * 16 + ch * STEPS + step
                        samp_ref[pl.ds(at, 8, stride=plan.group * 16), :] = own[ch]
    for v in range(5):
        for a in range(ax):
            for b in range(az):
                at = base(v, a, b) + HALO
                target = (a * az + b) * plan.body + v * plan.chunk
                back_ref[target : target + plan.chunk, :] = grid[at : at + plan.chunk, :]


def unpack_kernel(plan, back_ref, out_ref, turned):
    c = lax.axis_index("row")
    for j in range(plan.group):
        q = plan.chunk_of(j, c)
        for v in range(5):
            start = pl.multiple_of(v * plan.wr + q * plan.chunk, 8)
            turned[pl.ds(start, plan.chunk), :] = back_ref[j, v * plan.chunk : (v + 1) * plan.chunk, :]
    for v in range(5):
        out_ref[v] = turned[v * plan.wr : (v + 1) * plan.wr, :].T


def list_kernel(plan, entry_ref, list_ref, count_ref):
    def source(g, count):
        def block(n, count):
            found = [entry_ref[g * 1024 + n + k * 128] for k in range(8)]
            for entry in found:
                list_ref[count] = entry
                count = count + (entry >> 20)
            return count

        return lax.fori_loop(0, entry_ref[g * 1024 + 127], block, count)

    count = lax.fori_loop(0, 8, source, 0)
    count_ref[0] = count
    for k in range(8):
        list_ref[count + k] = 0


def entries(plan, ids):
    cell = ids.astype(jnp.int32)
    lane, r = halves(cell, plan.wr)
    q, r_l = halves(r, plan.chunk)
    g = lax.broadcasted_iota(jnp.int32, cell.shape, 0)
    mine, _ = plan.own_chunk()
    entry = (r_l * 8 + g) * 128 + lane + jnp.where(q == mine, 1 << 20, 0)
    last = lax.broadcasted_iota(jnp.int32, cell.shape, 2) == 127
    return jnp.where(last, cell, entry).reshape(-1)


def dft_kernel(plan, hist_ref, table_ref, point_ref, live_ref, out_ref):
    tile = pl.program_id(0)
    out_ref[0, 256:259, :] = point_ref[0]
    out_ref[0, 259:264, :] = jnp.full((5, 128), live_ref[0, 0].astype(jnp.float32))
    live = live_ref[0, 0] * 8
    keep = lax.broadcasted_iota(jnp.int32, (64, 128), 1) + tile * 128 < live
    for ch in range(4):
        signal = hist_ref[ch]
        if ch == 0:
            signal = signal + hist_ref[4]
        spec = lax.dot_general(
            table_ref[...],
            signal,
            (((1,), (1,)), ((), ())),
            precision=lax.Precision.HIGHEST,
            preferred_element_type=jnp.float32,
        )
        out_ref[0, ch * 64 : (ch + 1) * 64, :] = jnp.where(keep, spec, 0.0)


def geometry(plan, watch, point):
    offset = [w - p for w, p in zip(watch, point, strict=True)]
    square = offset[0] * offset[0] + offset[1] * offset[1] + offset[2] * offset[2]
    distance = jnp.sqrt(square)
    inverse = 1.0 / distance
    along = [o * inverse for o in offset]
    amplitude = plan.nr * inverse
    sine, cosine = sin_cos(distance * (2.0 / plan.nr))
    near = (plan.nr * 0.5) * inverse
    return along, amplitude, sine, cosine, near


def hist_kernel(plan, first, wide, watch_ref, *refs):
    spec_refs, out_ref, acc = refs[:-2], refs[-2], refs[-1]
    lane = lax.broadcasted_iota(jnp.int32, (wide, 64), 1)
    half = (lax.axis_index("row") % len(spec_refs)) * (plan.obs // len(spec_refs))
    tiles = [(jnp.max(ref[0, 259:260, :]).astype(jnp.int32) * 8 + 127) // 128 for ref in spec_refs]

    @pl.loop(0, out_ref.shape[0] // wide)
    def _(ob):
        start = pl.multiple_of(ob * wide, 8)
        row = pl.multiple_of(half + first + start, 8)
        watch = [jnp.broadcast_to(watch_ref[pl.ds(row, wide), d : d + 1], (wide, 128)) for d in range(3)]
        acc[...] = jnp.zeros_like(acc)

        def radiate_tile(spec_ref, tile):
            point = [spec_ref[tile, 256 + d : 257 + d, :] for d in range(3)]
            along, amplitude, sine, cosine, near = geometry(plan, watch, point)
            twice = 2.0 * cosine
            cos_last, sin_last = amplitude, jnp.zeros_like(amplitude)
            cos_now, sin_now = amplitude * cosine, amplitude * sine
            for f in range(FREQ):
                rows = [spec_ref[tile, pl.ds(k * 32 + f, 1), :] for k in range(8)]
                d_re = along[0] * rows[2] + along[1] * rows[4] + along[2] * rows[6]
                d_im = along[0] * rows[3] + along[1] * rows[5] + along[2] * rows[7]
                weight = near * (1.0 / (f + 1))
                e_re = (rows[0] + d_re) + weight * d_im
                e_im = (rows[1] + d_im) - weight * d_re
                acc[f] = acc[f] + (sin_now * e_re - cos_now * e_im)
                acc[FREQ + f] = acc[FREQ + f] + (cos_now * e_re + sin_now * e_im)
                cos_now, cos_last = twice * cos_now - cos_last, cos_now
                sin_now, sin_last = twice * sin_now - sin_last, sin_now

        for spec_ref, count in zip(spec_refs, tiles, strict=True):
            pl.loop(0, count)(functools.partial(radiate_tile, spec_ref))

        out = jnp.zeros((wide, 64), jnp.float32)
        for f in range(2 * FREQ):
            out = jnp.where(lane == f, jnp.sum(acc[f], axis=1, keepdims=True), out)
        out_ref[pl.ds(start, wide), :] = out


def recent_kernel(plan, parts, list_ref, count_ref, samp_ref, obs_ref, tab_ref, *refs):
    hist_refs, out_ref = refs[:parts], refs[parts]
    value, place, cos_s, sin_s, mono, dip, full, acc, final = refs[parts + 1 :]
    q, c = plan.own_chunk()
    count = count_ref[0]
    tiles = plan.obs // 128
    lane = lax.broadcasted_iota(jnp.int32, (16, 128), 1)
    acc[...] = jnp.zeros_like(acc)

    groups = (count + 7) // 8

    def sample(group):
        picked, spots = [], []
        for k in range(8):
            entry = list_ref[group * 8 + k] & ((1 << 20) - 1)
            row, at = halves(entry, 128)
            tile = samp_ref[pl.ds(pl.multiple_of(row * 16, 16), 16), :]
            r_l, g = halves(row, 8)
            a, b = halves(g, plan.az)
            x_l, z_l = halves(at, plan.wz)
            spots.append((a * plan.wx + x_l, b * plan.wz + z_l, c * plan.wr + q * plan.chunk + r_l))
            at = jnp.where(group * 8 + k < count, at, -1)
            picked.append(jnp.sum(jnp.where(lane == at, tile, 0.0), axis=1, keepdims=True))
        return picked, spots

    def keep(found):
        for k in range(8):
            value[k * 16 : (k + 1) * 16, :] = jnp.broadcast_to(found[0][k], (16, 128))
            for d in range(3):
                spot = found[1][k][d].astype(jnp.float32) + 0.5
                place[d * 8 + k : d * 8 + k + 1, :] = jnp.full((1, 128), spot)

    keep(sample(0))

    @pl.loop(0, groups)
    def _(group):
        point = [place[d * 8 : (d + 1) * 8, :] for d in range(3)]
        drawn = [value[pl.ds(i, 8, stride=16), :] for i in range(4 * STEPS)]
        coming = sample(jnp.minimum(group + 1, groups - 1))
        for t in range(tiles):
            seen = obs_ref[:, t * 128 : (t + 1) * 128]
            watch = [
                seen[0:1] * float(plan.nx),
                seen[1:2] * float(plan.nz),
                (1.25 + 0.75 * seen[2:3]) * float(plan.nr),
            ]
            along, amplitude, sine, cosine, near = geometry(plan, watch, point)
            for s in range(STEPS):
                push = along[0] * drawn[STEPS + s] + along[1] * drawn[2 * STEPS + s] + along[2] * drawn[3 * STEPS + s]
                at = (t * STEPS + s) * 8
                mono[at : at + 8, :] = drawn[s] + push
                dip[at : at + 8, :] = near * push
            twice = 2.0 * cosine
            cos_last, sin_last = amplitude, jnp.zeros_like(amplitude)
            cos_now, sin_now = amplitude * cosine, amplitude * sine
            for f in range(FREQ):
                at = (t * FREQ + f) * 8
                cos_s[at : at + 8, :] = cos_now
                sin_s[at : at + 8, :] = sin_now
                cos_now, cos_last = twice * cos_now - cos_last, cos_now
                sin_now, sin_last = twice * sin_now - sin_last, sin_now
        for t in range(tiles):
            for fv in range(FREQ // 8):
                base = (t * (FREQ // 8) + fv) * 12
                sums = [acc[base + i] for i in range(12)]
                for k in range(8):
                    at = (t * FREQ + fv * 8) * 8 + k
                    wave_c = cos_s[pl.ds(at, 8, stride=8), :]
                    wave_s = sin_s[pl.ds(at, 8, stride=8), :]
                    for s in range(STEPS):
                        at = (t * STEPS + s) * 8 + k
                        m = mono[at : at + 1, :]
                        p = dip[at : at + 1, :]
                        sums[4 * s] = sums[4 * s] + wave_c * m
                        sums[4 * s + 1] = sums[4 * s + 1] + wave_s * m
                        sums[4 * s + 2] = sums[4 * s + 2] + wave_c * p
                        sums[4 * s + 3] = sums[4 * s + 3] + wave_s * p
                for i in range(12):
                    acc[base + i] = sums[i]
        keep(coming)

    scale = 1.0 / math.sqrt(plan.devices * SURF_DEV)
    final[...] = jnp.zeros_like(final)
    for t in range(tiles):
        for fv in range(FREQ // 8):
            base = (t * (FREQ // 8) + fv) * 12
            column = tab_ref[fv * 8 : (fv + 1) * 8, :]
            out_re = jnp.zeros((8, 128), jnp.float32)
            out_im = jnp.zeros((8, 128), jnp.float32)
            below = column[:, 6:7]
            for s in range(STEPS):
                part_re = acc[base + 4 * s + 1] + acc[base + 4 * s + 2] * below
                part_im = acc[base + 4 * s] - acc[base + 4 * s + 3] * below
                turn_re, turn_im = column[:, 2 * s : 2 * s + 1], column[:, 2 * s + 1 : 2 * s + 2]
                out_re = out_re + (turn_re * part_re - turn_im * part_im)
                out_im = out_im + (turn_im * part_re + turn_re * part_im)
            final[fv * 8 : (fv + 1) * 8, :] = out_re
            final[FREQ + fv * 8 : FREQ + (fv + 1) * 8, :] = out_im
        full[t * 128 : (t + 1) * 128, :] = final[...].T * scale
    share = hist_refs[0].shape[0]
    ways = plan.obs // (share * parts)
    half = (lax.axis_index("row") % ways) * (share * parts)
    for i in range(parts):
        row = pl.multiple_of(half + i * share, 8)
        full[pl.ds(row, share), : 2 * FREQ] = full[pl.ds(row, share), : 2 * FREQ] + hist_refs[i][...] * scale
    for k in range(4):
        low = full[pl.ds(k, plan.devices, stride=8), :]
        high = full[pl.ds(k + 4, plan.devices, stride=8), :]
        both = low + pltpu.roll(high, 64, 1)
        out_ref[pl.ds(k, plan.devices, stride=4), :] = both


def sum_kernel(pieces_ref, out_ref):
    total = pieces_ref[0]
    for i in range(1, pieces_ref.shape[0]):
        total = total + pieces_ref[i]
    out_ref[0:4, :] = total[:, :64]
    out_ref[4:8, :] = total[:, 64:]


def fourier_numpy(samples):
    turn = np.arange(1, FREQ + 1)[:, None] * np.arange(samples)[None, :] % samples
    angle = 2.0 * np.pi / samples * turn
    return np.cos(angle) / np.sqrt(samples), -np.sin(angle) / np.sqrt(samples)


def fast_device(plan, flow_field, flux_jacobian, history, surface_cell, surface_blocks, observers):
    f32 = jnp.float32
    shape = jax.ShapeDtypeStruct
    group, wr, lanes = plan.group, plan.wr, plan.lanes
    field_rows = 5 * (plan.ax + 2) * plan.az * plan.tall_pad
    parts = 4
    bind = functools.partial

    packed = call(
        bind(pack_kernel, plan),
        shape((group, plan.sent, lanes), f32),
        [VMEM, VMEM, SMEM],
        VMEM,
        [pltpu.VMEM((5 * wr, lanes), f32)],
        name="pack",
    )(flow_field.reshape(5, lanes, wr), surface_cell.T, surface_blocks)
    packed, surface_cell = lax.optimization_barrier((packed, surface_cell))
    got = lax.all_to_all(packed, GROUP, 0, 0, tiled=True)

    tile_count = plan.capacity // 128
    cell = surface_cell.reshape(-1)
    index_x, index_z, index_r = (lax.axis_index(name) for name in AXES)
    points = jnp.stack(
        [
            index_x * plan.wx + cell // (plan.wz * wr),
            index_z * plan.wz + cell // wr % plan.wz,
            index_r * wr + cell % wr,
        ]
    ).astype(f32) + 0.5
    points = jnp.transpose(points.reshape(3, tile_count, 128), (1, 0, 2))
    cos_t, sin_t = fourier_numpy(plan.samples)
    table = np.concatenate([cos_t, sin_t], axis=0).astype(np.float32)
    table[:, plan.samples - STEPS :] = 0.0
    spec = pl.pallas_call(
        bind(dft_kernel, plan),
        out_shape=shape((tile_count, 264, 128), f32),
        grid=(tile_count,),
        in_specs=[
            pl.BlockSpec((5, 128, plan.samples), lambda i: (0, i, 0)),
            pl.BlockSpec((64, plan.samples), lambda i: (0, 0)),
            pl.BlockSpec((1, 3, 128), lambda i: (i, 0, 0)),
            SMEM,
        ],
        out_specs=pl.BlockSpec((1, 264, 128), lambda i: (i, 0, 0)),
        name="dft",
        compiler_params=pltpu.CompilerParams(vmem_limit_bytes=40 * 1024 * 1024),
        cost_estimate=pl.CostEstimate(flops=10**9, bytes_accessed=10**6, transcendentals=0),
    )(jnp.transpose(history, (1, 0, 2)), jnp.asarray(table), points, surface_blocks)

    watch = jnp.stack(
        [
            observers[0] * plan.nx,
            observers[1] * plan.nz,
            (1.25 + 0.75 * observers[2]) * plan.nr,
        ],
        axis=1,
    )
    sources = [spec]
    if plan.rows % 2 == 0:
        sources.append(lax.ppermute(spec, "row", [(i, i ^ 1) for i in range(plan.rows)]))
    share = plan.obs // len(sources) // parts
    wide = 32
    hists = []
    for i in range(parts):
        hists.append(
            call(
                bind(hist_kernel, plan, i * share, wide),
                shape((share, 64), f32),
                [VMEM] * (1 + len(sources)),
                VMEM,
                [pltpu.VMEM((64, wide, 128), f32)],
                flops=10**9,
                name=f"hist{i}",
            )(watch, *sources)
        )

    flat = got.reshape(group * plan.sent, lanes)
    flat, hists[0], hists[1] = lax.optimization_barrier((flat, hists[0], hists[1]))
    first, second = call(
        bind(edge_kernel, plan),
        (shape((5 * group * HALO, lanes), f32),) * 2,
        [VMEM],
        (VMEM, VMEM),
        name="edges",
    )(flat)
    line = plan.line()
    swap_a = [(line[i], line[i ^ 1]) for i in range(len(line))]
    swap_b = [
        (line[i], line[((i + 1) ^ 1) - 1]) for i in range(1, len(line) - 1)
    ]
    first = lax.ppermute(first, AXES, swap_a)
    second = lax.ppermute(second, AXES, swap_b)

    ids = entries(plan, got[:, plan.body :, :])
    listed, count = call(
        bind(list_kernel, plan),
        (shape((group * plan.capacity + 8,), jnp.int32), shape((1,), jnp.int32)),
        [SMEM],
        (SMEM, SMEM),
        name="list",
    )(ids)

    flat, listed, count, hists = lax.optimization_barrier((flat, listed, count, hists))
    back, samp = call(
        bind(stencil_kernel, plan),
        (shape((group * plan.body, lanes), f32), shape((plan.chunk * 8 * 16, lanes), f32)),
        [VMEM, VMEM, VMEM, SMEM],
        (VMEM, VMEM),
        [
            pltpu.VMEM((3 * field_rows, lanes), f32),
            pltpu.VMEM((75, 8, lanes), f32),
            pltpu.VMEM((plan.tall_pad, lanes), f32),
            pltpu.VMEM((30 * plan.az, 8, lanes), f32),
        ],
        flops=10**9,
        name="stencil",
    )(flat, first, second, flux_jacobian)
    back = lax.all_to_all(back.reshape(group, plan.body, lanes), GROUP, 0, 0, tiled=True)

    columns = np.zeros((FREQ, 8), np.float32)
    for s in range(STEPS):
        columns[:, 2 * s] = cos_t[:, plan.samples - STEPS + s]
        columns[:, 2 * s + 1] = sin_t[:, plan.samples - STEPS + s]
    columns[:, 6] = 1.0 / np.arange(1, FREQ + 1)
    partial = call(
        bind(recent_kernel, plan, parts),
        shape((plan.obs // 2, 128), f32),
        [SMEM, SMEM, VMEM, VMEM, VMEM] + [VMEM] * parts,
        VMEM,
        [
            pltpu.VMEM((128, 128), f32),
            pltpu.VMEM((24, 128), f32),
            pltpu.VMEM((plan.obs // 128 * FREQ * 8, 128), f32),
            pltpu.VMEM((plan.obs // 128 * FREQ * 8, 128), f32),
            pltpu.VMEM((plan.obs // 128 * STEPS * 8, 128), f32),
            pltpu.VMEM((plan.obs // 128 * STEPS * 8, 128), f32),
            pltpu.VMEM((plan.obs, 128), f32),
            pltpu.VMEM((plan.obs // 128 * (FREQ // 8) * 12, 8, 128), f32),
            pltpu.VMEM((128, 128), f32),
        ],
        flops=10**9,
        name="recent",
    )(listed, count, samp, observers, jnp.asarray(columns), *hists)
    partial, back = lax.optimization_barrier((partial, back))
    pieces = lax.all_to_all(
        partial.reshape(plan.devices, 4, 128), AXES, 0, 0, tiled=True
    )
    spectrum = call(
        sum_kernel, shape((plan.per_obs, 2 * FREQ), f32), [VMEM], VMEM, name="sum"
    )(pieces)
    field = call(
        bind(unpack_kernel, plan),
        shape((5, lanes, wr), f32),
        [VMEM],
        VMEM,
        [pltpu.VMEM((5 * wr, lanes), f32)],
        name="unpack",
    )(back)
    return field.reshape(flow_field.shape), spectrum


def per_device(*args):
    flow_field, _, history, surface_cell, _, observers = args
    mesh = {name: lax.axis_size(name) for name in AXES}
    plan = Plan(mesh, flow_field.shape[1:], surface_cell.shape, history.shape, observers.shape[1])
    if plan.fits():
        return fast_device(plan, *args)
    return general_device(*args)


def solution(mesh):
    return jax.shard_map(
        per_device,
        mesh=mesh,
        in_specs=(
            P(None, "gx", "gz", "row"),
            P(),
            P(("gx", "gz", "row"), None, None),
            P(("gx", "gz", "row"), None),
            P("row", ("gx", "gz")),
            P(),
        ),
        out_specs=(P(None, "gx", "gz", "row"), P(("gx", "gz", "row"), None)),
        check_vma=False,
    )
```

```python
import functools
import math

import jax
import jax.numpy as jnp
import numpy as np
from jax import lax
from jax.experimental import pallas as pl
from jax.experimental.pallas import tpu as pltpu
from jax.sharding import PartitionSpec as P


SURF_DEV = 128
FREQ = 32
STEPS = 3


TIME_STEP = 0.3
VISCOSITY = 0.05


def padded_2(value, sides, width):
    for axis, dim in sides:
        peers, length = (lax.axis_size(axis), value.shape[dim])
        up = [(i, (i + 1) % peers) for i in range(peers - 1)]
        down = [(j, i) for i, j in up]
        last = lax.slice_in_dim(value, length - width, length, axis=dim)
        leading = lax.slice_in_dim(value, 0, width, axis=dim)
        before = lax.ppermute(last, axis, up)
        after = lax.ppermute(leading, axis, down)
        value = jnp.concatenate([before, value, after], axis=dim)
    return value


def stencil_rate(padded, flux_jacobian):
    center = padded[:, 1:-1, 1:-1, 1:-1]
    along_x = (padded[:, 2:, 1:-1, 1:-1] - padded[:, :-2, 1:-1, 1:-1]) * 0.5
    along_z = (padded[:, 1:-1, 2:, 1:-1] - padded[:, 1:-1, :-2, 1:-1]) * 0.5
    along_r = (padded[:, 1:-1, 1:-1, 2:] - padded[:, 1:-1, 1:-1, :-2]) * 0.5
    beside = padded[:, 2:, 1:-1, 1:-1] + padded[:, :-2, 1:-1, 1:-1]
    beside = beside + padded[:, 1:-1, 2:, 1:-1] + padded[:, 1:-1, :-2, 1:-1]
    beside = beside + padded[:, 1:-1, 1:-1, 2:] + padded[:, 1:-1, 1:-1, :-2]
    slopes = jnp.stack([along_x, along_z, along_r])
    transport = jnp.einsum(
        "dvw,dwxzr->vxzr", flux_jacobian, slopes, precision=lax.Precision.HIGHEST
    )
    return transport + VISCOSITY * (beside - 6.0 * center)


def fourier_table(samples, freq_count):
    time_ids = jnp.arange(samples, dtype=jnp.int32)
    freq_ids = jnp.arange(1, freq_count + 1, dtype=jnp.int32)
    turn_ids = freq_ids[:, None] * time_ids[None, :] % samples
    angles = 2.0 * math.pi / samples * turn_ids.astype(jnp.float32)
    norm_scale = 1.0 / math.sqrt(samples)
    return jnp.concatenate([jnp.cos(angles), -jnp.sin(angles)], axis=0) * norm_scale


def spectra_of(signals, fourier):
    return jnp.einsum("ft,svt->vfs", fourier, signals, precision=lax.Precision.HIGHEST)


def radiate(points, monopole, dipole, watchers, radial_cells, freq_count):
    wavenumbers = jnp.arange(1, freq_count + 1, dtype=jnp.float32) * (2.0 / radial_cells)
    offset_vec = watchers[:, :, None] - points[None, :, :]
    distance = jnp.sqrt(jnp.sum(offset_vec * offset_vec, axis=1))
    direction = offset_vec / distance[:, None, :]
    amplitude = (radial_cells / distance)[:, None, :]
    dip_real = direction[:, 0, None, :] * dipole[0, None, :freq_count, :]
    dip_real = dip_real + direction[:, 1, None, :] * dipole[1, None, :freq_count, :]
    dip_real = dip_real + direction[:, 2, None, :] * dipole[2, None, :freq_count, :]
    dip_imag = direction[:, 0, None, :] * dipole[0, None, freq_count:, :]
    dip_imag = dip_imag + direction[:, 1, None, :] * dipole[1, None, freq_count:, :]
    dip_imag = dip_imag + direction[:, 2, None, :] * dipole[2, None, freq_count:, :]
    mono_real = monopole[None, :freq_count, :]
    mono_imag = monopole[None, freq_count:, :]
    phase_arg = distance[:, None, :] * wavenumbers[None, :, None]
    near_term = 1.0 / phase_arg
    cosine = amplitude * jnp.cos(phase_arg)
    sine = amplitude * jnp.sin(phase_arg)
    plus_weight = cosine * near_term + sine
    minus_weight = cosine - sine * near_term
    out_real = jnp.sum(
        plus_weight * dip_real - minus_weight * dip_imag + sine * mono_real - cosine * mono_imag,
        axis=2,
    )
    out_imag = jnp.sum(
        minus_weight * dip_real + plus_weight * dip_imag + cosine * mono_real + sine * mono_imag,
        axis=2,
    )
    return jnp.concatenate([out_real, out_imag], axis=1)


def general_device(flow_field, flux_jacobian, history, surface_cell, surface_blocks, observers):
    width_x, width_z, width_r = (flow_field.shape[1], flow_field.shape[2], flow_field.shape[3])
    count_x, count_z, count_r = (lax.axis_size("gx"), lax.axis_size("gz"), lax.axis_size("row"))
    index_x, index_z, index_r = (lax.axis_index("gx"), lax.axis_index("gz"), lax.axis_index("row"))
    owners = count_x * count_z
    devices = owners * count_r
    radial_cells = width_r * count_r
    slot_rows = surface_cell.shape[0]
    capacity = slot_rows * owners
    samples = history.shape[2]
    cell_ids = surface_cell.reshape(-1)

    def inside_mask(margin):
        coord_x = index_x * width_x + jnp.arange(width_x + 2 * margin, dtype=jnp.int32) - margin
        coord_z = index_z * width_z + jnp.arange(width_z + 2 * margin, dtype=jnp.int32) - margin
        coord_r = index_r * width_r + jnp.arange(width_r + 2 * margin, dtype=jnp.int32) - margin
        valid_x = (coord_x >= 0) & (coord_x < width_x * count_x)
        valid_z = (coord_z >= 0) & (coord_z < width_z * count_z)
        valid_r = (coord_r >= 0) & (coord_r < radial_cells)
        joined = valid_x[:, None, None] & valid_z[None, :, None] & valid_r[None, None, :]
        return joined.astype(jnp.float32)[None]

    mask_outer = inside_mask(2)
    mask_inner = inside_mask(1)
    current = flow_field
    sampled = []
    for _ in range(STEPS):
        extended = padded_2(current, (("gx", 1), ("gz", 2), ("row", 3)), 3)
        section_one = (
            extended[:, 1:-1, 1:-1, 1:-1] + TIME_STEP * stencil_rate(extended, flux_jacobian)
        ) * mask_outer
        section_two = 0.75 * extended[:, 2:-2, 2:-2, 2:-2] + 0.25 * (
            section_one[:, 1:-1, 1:-1, 1:-1] + TIME_STEP * stencil_rate(section_one, flux_jacobian)
        )
        section_two = section_two * mask_inner
        current = extended[:, 3:-3, 3:-3, 3:-3] / 3.0 + 2.0 / 3.0 * (
            section_two[:, 1:-1, 1:-1, 1:-1] + TIME_STEP * stencil_rate(section_two, flux_jacobian)
        )
        sampled.append(jnp.take(current.reshape(5, -1), cell_ids, axis=1))
    recent = jnp.transpose(jnp.stack(sampled, axis=2), (1, 0, 2))
    signals = jnp.concatenate([history[:, :, : samples - STEPS], recent], axis=2)
    global_x = index_x * width_x + cell_ids // (width_z * width_r)
    global_z = index_z * width_z + cell_ids // width_r % width_z
    global_r = index_r * width_r + cell_ids % width_r
    positions = jnp.stack([global_x, global_z, global_r]).astype(jnp.float32) + 0.5
    fourier = fourier_table(samples, FREQ)
    live_mask = (jnp.arange(capacity, dtype=jnp.int32) // owners < surface_blocks[0, 0]).astype(
        jnp.float32
    )
    spectra = spectra_of(signals, fourier) * live_mask
    monopole = spectra[0] + spectra[4]
    dipole = spectra[1:4]
    watchers = jnp.stack(
        [
            observers[0] * (width_x * count_x),
            observers[1] * (width_z * count_z),
            (1.25 + 0.75 * observers[2]) * radial_cells,
        ],
        axis=1,
    )
    norm_scale = math.sqrt(devices * SURF_DEV)
    row_count = observers.shape[1] // devices * lax.axis_size(("gx", "gz", "row"))
    block_size = math.gcd(row_count, 32)

    def one_block(block):
        return radiate(positions, monopole, dipole, block, radial_cells, FREQ)

    blocks_out = lax.map(one_block, watchers.reshape(row_count // block_size, block_size, 3))
    spectrum = lax.psum_scatter(
        blocks_out.reshape(row_count, 2 * FREQ) / norm_scale,
        ("gx", "gz", "row"),
        scatter_dimension=0,
        tiled=True,
    )
    return (current, spectrum)


HALO = 3 * STEPS
AXES = ("gx", "gz", "row")
GROUP = ("gx", "gz")
VMEM = pl.BlockSpec(memory_space=pltpu.VMEM)
SMEM = pl.BlockSpec(memory_space=pltpu.SMEM)


def halves(value, by):
    if by & (by - 1) == 0:
        return value >> (by.bit_length() - 1), value & (by - 1)
    return value // by, value % by


def sin_cos(angle):
    turns = jnp.floor(angle * (2.0 / math.pi) + 0.5)
    rest = ((angle - turns * 1.5703125) - turns * 4.837512969970703e-4) - turns * 7.549789954891882e-8
    square = rest * rest
    sine = rest + rest * square * (
        -1.6666654611e-1 + square * (8.3321608736e-3 + square * -1.9515295891e-4)
    )
    cosine = (1.0 - 0.5 * square) + square * square * (
        4.166664568298827e-2 + square * (-1.388731625493765e-3 + square * 2.443315711809948e-5)
    )
    quarter = turns.astype(jnp.int32) & 3
    odd = (quarter & 1) == 1
    out_sine = jnp.where(odd, cosine, sine)
    out_cosine = jnp.where(odd, sine, cosine)
    out_sine = jnp.where(quarter >= 2, -out_sine, out_sine)
    out_cosine = jnp.where((quarter == 1) | (quarter == 2), -out_cosine, out_cosine)
    return out_sine, out_cosine


class Plan:
    def __init__(self, mesh, flow, cells, hist, obs):
        self.ax, self.az, self.rows = mesh["gx"], mesh["gz"], mesh["row"]
        self.group = self.ax * self.az
        self.devices = self.group * self.rows
        self.wx, self.wz, self.wr = flow
        self.blocks = cells[0]
        self.capacity = cells[0] * cells[1]
        self.samples = hist[2]
        self.lanes = self.wx * self.wz
        self.chunk = self.wr // self.group
        self.nx, self.nz, self.nr = self.wx * self.ax, self.wz * self.az, self.wr * self.rows
        self.obs = obs
        self.body = 5 * self.chunk
        self.sent = self.body + 8
        self.per_obs = obs // self.devices
        self.tall_pad = (self.chunk + 2 * HALO + 8) // 8 * 8 + 8

    def fits(self):
        return (
            self.group == 8
            and self.lanes == 128
            and self.wr % 128 == 0
            and self.chunk % 8 == 0
            and self.chunk >= 2 * 8
            and self.chunk >= HALO
            and self.capacity == self.blocks * 8
            and 2 * self.blocks < 127
            and self.capacity % 128 == 0
            and self.samples == 128
            and self.obs % 128 == 0
            and self.obs % self.devices == 0
            and self.obs // self.devices == 8
            and FREQ == 32
            and STEPS == 3
        )

    def order_of(self, a, b):
        return b * self.ax + (a if b % 2 == 0 else self.ax - 1 - a)

    def table(self):
        return [self.order_of(j // self.az, j % self.az) for j in range(self.group)]

    def line(self):
        out = []
        for c in range(self.rows):
            order = self.table()
            if c % 2:
                order = [self.group - 1 - q for q in order]
            for q in range(self.group):
                out.append(order.index(q) * self.rows + c)
        return out

    def chunk_of(self, j, c):
        q = self.table()[j]
        return jnp.where(c % 2 == 1, self.group - 1 - q, q)

    def own_chunk(self):
        a, b, c = lax.axis_index("gx"), lax.axis_index("gz"), lax.axis_index("row")
        q = b * self.ax + jnp.where(b % 2 == 0, a, self.ax - 1 - a)
        return jnp.where(c % 2 == 1, self.group - 1 - q, q), c


def call(kernel, out_shape, in_specs, out_specs, scratch=(), flops=10**6):
    kernel_call = pl.pallas_call(
        kernel,
        out_shape=out_shape,
        in_specs=in_specs,
        out_specs=out_specs,
        scratch_shapes=list(scratch),
        compiler_params=pltpu.CompilerParams(vmem_limit_bytes=40 * 1024 * 1024),
        cost_estimate=pl.CostEstimate(flops=flops, bytes_accessed=10**5, transcendentals=0),
    )
    return kernel_call


def move(axes, *pairs):
    if pairs:
        return lambda value: lax.ppermute(value, axes, pairs[0])
    return lambda value: lax.all_to_all(value, axes, 0, 0, tiled=True)


def pack_kernel(plan, flow_ref, cell_ref, live_ref, out_ref, turned):
    c = lax.axis_index("row")
    for v in range(5):
        turned[v * plan.wr : (v + 1) * plan.wr, :] = flow_ref[v].T
    cells = cell_ref[...].astype(jnp.float32)
    ids = jnp.concatenate([cells[:4], cells[4:], jnp.zeros((4, 128 - 2 * plan.blocks), jnp.float32)], axis=1)
    ids = jnp.concatenate([ids, jnp.zeros((4, 128), jnp.float32)], axis=0)
    lane = lax.broadcasted_iota(jnp.int32, (8, 128), 1)
    ids = jnp.where(lane == 127, live_ref[0, 0].astype(jnp.float32), ids)
    for j in range(plan.group):
        q = plan.chunk_of(j, c)
        for v in range(5):
            start = pl.multiple_of(v * plan.wr + q * plan.chunk, 8)
            out_ref[j, v * plan.chunk : (v + 1) * plan.chunk, :] = turned[pl.ds(start, plan.chunk), :]
        out_ref[j, plan.body : plan.body + 8, :] = ids


def edge_kernel(plan, got_ref, first_ref, second_ref, own_ref):
    q, c = plan.own_chunk()
    even = (c * plan.group + q) % 2 == 0
    high, low = plan.chunk - HALO, 0
    first = jnp.where(even, high, low)
    second = jnp.where(even, low, high)
    for v in range(5):
        for g in range(plan.group):
            at = (v * plan.group + g) * HALO
            row = g * plan.sent + v * plan.chunk
            first_ref[at : at + HALO, :] = got_ref[pl.ds(row + first, HALO), :]
            second_ref[at : at + HALO, :] = got_ref[pl.ds(row + second, HALO), :]
            at = (v * plan.group + g) * plan.chunk
            own_ref[at : at + plan.chunk, :] = got_ref[row : row + plan.chunk, :]


def stencil_kernel(plan, own_ref, first_ref, second_ref, jac_ref, back_ref, samp_ref, cur, one, two, coef, mask, side):
    q, c = plan.own_chunk()
    place = c * plan.group + q
    even = place % 2 == 0
    tall = plan.chunk + 2 * HALO
    wz, lanes, az, ax, wx = plan.wz, plan.lanes, plan.az, plan.ax, plan.wx
    high = plan.tall_pad
    per = (ax + 2) * az * high

    def base(v, a, b):
        return v * per + ((a + 1) * az + b) * high

    has_low = jnp.where(place > 0, 1.0, 0.0)
    has_high = jnp.where(place < plan.rows * plan.group - 1, 1.0, 0.0)
    row = lax.broadcasted_iota(jnp.int32, (high, 128), 0)
    mask[...] = jnp.where(row < HALO, has_low, jnp.where(row >= HALO + plan.chunk, has_high, 1.0))
    for d in range(3):
        for v in range(5):
            for w in range(5):
                coef[(d * 5 + v) * 5 + w] = jnp.full((8, 128), jac_ref[d, v, w] * (0.5 * TIME_STEP), jnp.float32)
    zeros = jnp.zeros((az * high, 128), jnp.float32)
    for ref in (cur, one, two):
        for v in range(5):
            for a in (-1, ax):
                ref[base(v, a, 0) : base(v, a, 0) + az * high, :] = zeros
    for v in range(5):
        for a in range(ax):
            for b in range(az):
                at = base(v, a, b) + HALO
                source = (v * plan.group + a * az + b) * plan.chunk
                cur[at : at + plan.chunk, :] = own_ref[source : source + plan.chunk, :]

    def put(low_ref, high_ref):
        for v in range(5):
            for a in range(ax):
                for b in range(az):
                    at = base(v, a, b)
                    source = (v * plan.group + a * az + b) * HALO
                    cur[at : at + HALO, :] = low_ref[source : source + HALO, :]
                    at = at + HALO + plan.chunk
                    cur[at : at + HALO, :] = high_ref[source : source + HALO, :]

    @pl.when(even)
    def _():
        put(second_ref, first_ref)

    @pl.when(jnp.logical_not(even))
    def _():
        put(first_ref, second_ref)

    lane = lax.broadcasted_iota(jnp.int32, (8, 128), 1)
    x_l, z_l = halves(lane, wz)
    zero = jnp.zeros((8, 128), jnp.float32)
    damp = VISCOSITY * TIME_STEP

    many = 2 if ax % 2 == 0 else 1
    spots = [(i, b) for i in range(many) for b in range(az)]
    keys = [(w, i, b) for w in range(5) for i, b in spots]
    far = {(w, i, b): w * per + (i * az + b) * high for w, i, b in keys}
    side_step = az * high

    def turns_of(number):
        return ((tall - 2 * number + 7) >> 3) * (ax // many)

    def places(number, turn):
        block, a = halves(turn, ax // many)
        start = number + block * 8
        return start, (a * many + 1) * (az * high) + start

    grids = (cur, one, two)

    def across(number, turn):
        src = grids[(number - 1) % 3]
        _, root = places(number, turn)
        mid = {k: src[pl.ds(root + far[k], 8), :] for k in keys}
        found = []
        for w, i, b in keys:
            k = (w, i, b)
            ahead = src[pl.ds(root + (far[k] + side_step), 8), :]
            behind = src[pl.ds(root + (far[k] - side_step), 8), :]
            x_next = pltpu.roll(jnp.where(x_l == 0, ahead, mid[k]), lanes - wz, 1)
            x_prev = pltpu.roll(jnp.where(x_l == wx - 1, behind, mid[k]), wz, 1)
            z_edge = pltpu.roll(mid[w, i, b + 1], wz - 1, 1) if b < az - 1 else zero
            z_next = jnp.where(z_l < wz - 1, pltpu.roll(mid[k], lanes - 1, 1), z_edge)
            z_edge = pltpu.roll(mid[w, i, b - 1], lanes - (wz - 1), 1) if b > 0 else zero
            z_prev = jnp.where(z_l > 0, pltpu.roll(mid[k], 1, 1), z_edge)
            found.append((x_next - x_prev, z_next - z_prev, (x_next + x_prev) + (z_next + z_prev)))
        return found

    def store(found):
        for i, values in enumerate(found):
            for d in range(3):
                side[3 * i + d] = values[d]

    order = {k: i for i, k in enumerate(keys)}

    def advance(number, turn, next_number, next_turn):
        part = (number - 1) % 3
        src, dst = grids[part], grids[(part + 1) % 3]
        keep, gain = ((0.0, 1.0), (0.75, 0.25), (1.0 / 3.0, 2.0 / 3.0))[part]
        start, root = places(number, turn)
        coming = across(next_number, next_turn)
        inside = mask[pl.ds(start, 8), :]
        for i, b in spots:
            total = []
            slopes = []
            for w in range(5):
                k = (w, i, b)
                after, before = src[pl.ds(root + (far[k] + 1), 8), :], src[pl.ds(root + (far[k] - 1), 8), :]
                around = side[3 * order[k] + 2] + (after + before)
                total.append((1.0 - 6.0 * damp) * src[pl.ds(root + far[k], 8), :] + damp * around)
                slopes.append((after - before, side[3 * order[k] + 1], side[3 * order[k]]))
            for d in range(3):
                for w in range(5):
                    for v in range(5):
                        total[v] = total[v] + coef[((2 - d) * 5 + v) * 5 + w] * slopes[w][d]
            for v in range(5):
                k = (v, i, b)
                value = total[v] * (gain * inside)
                if part:
                    value = (keep * inside) * cur[pl.ds(root + far[k], 8), :] + value
                dst[pl.ds(root + far[k], 8), :] = value
        store(coming)

    store(across(1, 0))
    for number in range(1, 3 * STEPS + 1):
        turns = turns_of(number)

        @pl.loop(0, turns - 1)
        def _(turn):
            advance(number, turn, number, turn + 1)

        if number < 3 * STEPS:
            advance(number, turns - 1, number + 1, 0)
        else:
            advance(number, turns - 1, number, turns - 1)
        if number % 3:
            continue
        step = number // 3 - 1
        for a in range(ax):
            for b in range(az):
                for r in range(0, plan.chunk, 8):
                    own = [cur[base(v, a, b) + HALO + r : base(v, a, b) + HALO + r + 8, :] for v in range(5)]
                    own[0] = own[0] + own[4]
                    for ch in range(4):
                        at = (r * plan.group + a * az + b) * 16 + ch * STEPS + step
                        samp_ref[pl.ds(at, 8, stride=plan.group * 16), :] = own[ch]
    for v in range(5):
        for a in range(ax):
            for b in range(az):
                at = base(v, a, b) + HALO
                target = (a * az + b) * plan.body + v * plan.chunk
                back_ref[target : target + plan.chunk, :] = cur[at : at + plan.chunk, :]


def unpack_kernel(plan, back_ref, out_ref, turned):
    c = lax.axis_index("row")
    for j in range(plan.group):
        q = plan.chunk_of(j, c)
        for v in range(5):
            start = pl.multiple_of(v * plan.wr + q * plan.chunk, 8)
            turned[pl.ds(start, plan.chunk), :] = back_ref[j, v * plan.chunk : (v + 1) * plan.chunk, :]
    for v in range(5):
        out_ref[v] = turned[v * plan.wr : (v + 1) * plan.wr, :].T


def list_kernel(plan, entry_ref, list_ref, count_ref):
    def source(g, count):
        def block(n, count):
            found = [entry_ref[g * 512 + n + (k % 4 * 128 + k // 4 * plan.blocks)] for k in range(8)]
            for entry in found:
                list_ref[count] = entry
                count = count + (entry >> 20)
            return count

        return lax.fori_loop(0, entry_ref[g * 512 + 127], block, count)

    count = lax.fori_loop(0, 8, source, 0)
    count_ref[0] = count
    for k in range(8):
        list_ref[count + k] = 0


def entries(plan, ids):
    cell = ids.astype(jnp.int32)
    lane, r = halves(cell, plan.wr)
    q, r_l = halves(r, plan.chunk)
    g = lax.broadcasted_iota(jnp.int32, cell.shape, 0)
    mine, _ = plan.own_chunk()
    entry = (r_l * 8 + g) * 128 + lane + jnp.where(q == mine, 1 << 20, 0)
    last = lax.broadcasted_iota(jnp.int32, cell.shape, 2) == 127
    return jnp.where(last, cell, entry).reshape(-1)


def dft_kernel(plan, hist_ref, table_ref, point_ref, obs_ref, live_ref, out_ref, watch_ref):
    tile = pl.program_id(0)

    @pl.when(tile == 0)
    def _():
        seen = obs_ref[...]
        rows = [seen[0:1] * float(plan.nx), seen[1:2] * float(plan.nz), (1.25 + 0.75 * seen[2:3]) * float(plan.nr)]
        rows.append(jnp.zeros((5, plan.obs), jnp.float32))
        watch_ref[...] = jnp.concatenate(rows, axis=0).T

    out_ref[0, 256:259, :] = point_ref[0]
    out_ref[0, 259:264, :] = jnp.full((5, 128), live_ref[0, 0].astype(jnp.float32))
    live = live_ref[0, 0] * 8
    keep = lax.broadcasted_iota(jnp.int32, (64, 128), 1) + tile * 128 < live
    for ch in range(4):
        signal = hist_ref[ch]
        if ch == 0:
            signal = signal + hist_ref[4]
        spec = lax.dot_general(
            table_ref[...],
            signal,
            (((1,), (1,)), ((), ())),
            precision=lax.Precision.HIGHEST,
            preferred_element_type=jnp.float32,
        )
        out_ref[0, ch * 64 : (ch + 1) * 64, :] = jnp.where(keep, spec, 0.0)


def geometry(plan, watch, point):
    offset = [w - p for w, p in zip(watch, point, strict=True)]
    square = offset[0] * offset[0] + offset[1] * offset[1] + offset[2] * offset[2]
    distance = jnp.sqrt(square)
    inverse = 1.0 / distance
    along = [o * inverse for o in offset]
    amplitude = plan.nr * inverse
    sine, cosine = sin_cos(distance * (2.0 / plan.nr))
    near = (plan.nr * 0.5) * inverse
    return along, amplitude, sine, cosine, near


def hist_kernel(plan, ways, first, wide, watch_ref, *refs):
    spec_refs, out_ref, acc = refs[:-2], refs[-2], refs[-1]
    lane = lax.broadcasted_iota(jnp.int32, (wide, 64), 1)
    mine = (lax.axis_index("row") % ways) * (plan.obs // ways)
    tiles = [(jnp.max(ref[0, 259:260, :]).astype(jnp.int32) * 8 + 127) // 128 for ref in spec_refs]

    @pl.loop(0, out_ref.shape[0] // wide)
    def _(ob):
        start = pl.multiple_of(ob * wide, 8)
        row = pl.multiple_of(mine + first + start, 8)
        watch = [jnp.broadcast_to(watch_ref[pl.ds(row, wide), d : d + 1], (wide, 128)) for d in range(3)]
        acc[...] = jnp.zeros_like(acc)

        def radiate_tile(spec_ref, tile):
            point = [spec_ref[tile, 256 + d : 257 + d, :] for d in range(3)]
            along, amplitude, sine, cosine, near = geometry(plan, watch, point)
            twice = 2.0 * cosine
            cos_last, sin_last = amplitude, jnp.zeros_like(amplitude)
            cos_now, sin_now = amplitude * cosine, amplitude * sine
            for f in range(FREQ):
                rows = [spec_ref[tile, pl.ds(k * 32 + f, 1), :] for k in range(8)]
                d_re = along[0] * rows[2] + along[1] * rows[4] + along[2] * rows[6]
                d_im = along[0] * rows[3] + along[1] * rows[5] + along[2] * rows[7]
                weight = near * (1.0 / (f + 1))
                e_re = (rows[0] + d_re) + weight * d_im
                e_im = (rows[1] + d_im) - weight * d_re
                acc[f] = acc[f] + (sin_now * e_re - cos_now * e_im)
                acc[FREQ + f] = acc[FREQ + f] + (cos_now * e_re + sin_now * e_im)
                cos_now, cos_last = twice * cos_now - cos_last, cos_now
                sin_now, sin_last = twice * sin_now - sin_last, sin_now

        for spec_ref, count in zip(spec_refs, tiles, strict=True):
            pl.loop(0, count)(functools.partial(radiate_tile, spec_ref))

        out = jnp.zeros((wide, 64), jnp.float32)
        for f in range(2 * FREQ):
            out = jnp.where(lane == f, jnp.sum(acc[f], axis=1, keepdims=True), out)
        out_ref[pl.ds(start, wide), :] = out


def recent_kernel(plan, parts, near_parts, list_ref, count_ref, samp_ref, obs_ref, tab_ref, *refs):
    hist_refs, out_ref = refs[:parts], refs[parts]
    value, place, cos_s, sin_s, mono, dip, full, acc, final = refs[parts + 1 :]
    q, c = plan.own_chunk()
    count = count_ref[0]
    tiles = plan.obs // 128
    lane = lax.broadcasted_iota(jnp.int32, (16, 128), 1)
    acc[...] = jnp.zeros_like(acc)

    groups = (count + 7) // 8

    def sample(group):
        picked, spots = [], []
        for k in range(8):
            entry = list_ref[group * 8 + k] & ((1 << 20) - 1)
            row, at = halves(entry, 128)
            tile = samp_ref[pl.ds(pl.multiple_of(row * 16, 16), 16), :]
            r_l, g = halves(row, 8)
            a, b = halves(g, plan.az)
            x_l, z_l = halves(at, plan.wz)
            spots.append((a * plan.wx + x_l, b * plan.wz + z_l, c * plan.wr + q * plan.chunk + r_l))
            at = jnp.where(group * 8 + k < count, at, -1)
            picked.append(jnp.sum(jnp.where(lane == at, tile, 0.0), axis=1, keepdims=True))
        return picked, spots

    def keep(found):
        for k in range(8):
            value[k * 16 : (k + 1) * 16, :] = jnp.broadcast_to(found[0][k], (16, 128))
            for d in range(3):
                spot = found[1][k][d].astype(jnp.float32) + 0.5
                place[d * 8 + k : d * 8 + k + 1, :] = jnp.full((1, 128), spot)

    keep(sample(0))

    @pl.loop(0, groups)
    def _(group):
        point = [place[d * 8 : (d + 1) * 8, :] for d in range(3)]
        drawn = [value[pl.ds(i, 8, stride=16), :] for i in range(4 * STEPS)]
        coming = sample(jnp.minimum(group + 1, groups - 1))
        for t in range(tiles):
            seen = obs_ref[:, t * 128 : (t + 1) * 128]
            watch = [
                seen[0:1] * float(plan.nx),
                seen[1:2] * float(plan.nz),
                (1.25 + 0.75 * seen[2:3]) * float(plan.nr),
            ]
            along, amplitude, sine, cosine, near = geometry(plan, watch, point)
            for s in range(STEPS):
                push = along[0] * drawn[STEPS + s] + along[1] * drawn[2 * STEPS + s] + along[2] * drawn[3 * STEPS + s]
                at = (t * STEPS + s) * 8
                mono[at : at + 8, :] = drawn[s] + push
                dip[at : at + 8, :] = near * push
            twice = 2.0 * cosine
            cos_last, sin_last = amplitude, jnp.zeros_like(amplitude)
            cos_now, sin_now = amplitude * cosine, amplitude * sine
            for f in range(FREQ):
                at = (t * FREQ + f) * 8
                cos_s[at : at + 8, :] = cos_now
                sin_s[at : at + 8, :] = sin_now
                cos_now, cos_last = twice * cos_now - cos_last, cos_now
                sin_now, sin_last = twice * sin_now - sin_last, sin_now
        for t in range(tiles):
            for fv in range(FREQ // 8):
                base = (t * (FREQ // 8) + fv) * 12
                sums = [acc[base + i] for i in range(12)]
                for k in range(8):
                    at = (t * FREQ + fv * 8) * 8 + k
                    wave_c = cos_s[pl.ds(at, 8, stride=8), :]
                    wave_s = sin_s[pl.ds(at, 8, stride=8), :]
                    for s in range(STEPS):
                        at = (t * STEPS + s) * 8 + k
                        m = mono[at : at + 1, :]
                        p = dip[at : at + 1, :]
                        sums[4 * s] = sums[4 * s] + wave_c * m
                        sums[4 * s + 1] = sums[4 * s + 1] + wave_s * m
                        sums[4 * s + 2] = sums[4 * s + 2] + wave_c * p
                        sums[4 * s + 3] = sums[4 * s + 3] + wave_s * p
                for i in range(12):
                    acc[base + i] = sums[i]
        keep(coming)

    scale = 1.0 / math.sqrt(plan.devices * SURF_DEV)
    final[...] = jnp.zeros_like(final)
    for t in range(tiles):
        for fv in range(FREQ // 8):
            base = (t * (FREQ // 8) + fv) * 12
            column = tab_ref[fv * 8 : (fv + 1) * 8, :]
            out_re = jnp.zeros((8, 128), jnp.float32)
            out_im = jnp.zeros((8, 128), jnp.float32)
            below = column[:, 6:7]
            for s in range(STEPS):
                part_re = acc[base + 4 * s + 1] + acc[base + 4 * s + 2] * below
                part_im = acc[base + 4 * s] - acc[base + 4 * s + 3] * below
                turn_re, turn_im = column[:, 2 * s : 2 * s + 1], column[:, 2 * s + 1 : 2 * s + 2]
                out_re = out_re + (turn_re * part_re - turn_im * part_im)
                out_im = out_im + (turn_im * part_re + turn_re * part_im)
            final[fv * 8 : (fv + 1) * 8, :] = out_re
            final[FREQ + fv * 8 : FREQ + (fv + 1) * 8, :] = out_im
        full[t * 128 : (t + 1) * 128, :] = final[...].T * scale
    share = hist_refs[0].shape[0] * near_parts
    mine = (lax.axis_index("row") % (plan.obs // share)) * share
    for i, hist_ref in enumerate(hist_refs):
        rows = hist_ref.shape[0]
        at = pl.multiple_of(mine + (i * rows if i < near_parts else 0), 8)
        full[pl.ds(at, rows), : 2 * FREQ] = full[pl.ds(at, rows), : 2 * FREQ] + hist_ref[...] * scale
    for k in range(4):
        low = full[pl.ds(k, plan.devices, stride=8), :]
        high = full[pl.ds(k + 4, plan.devices, stride=8), :]
        both = low + pltpu.roll(high, 64, 1)
        out_ref[pl.ds(k, plan.devices, stride=4), :] = both


def sum_kernel(pieces_ref, out_ref):
    total = pieces_ref[0]
    for i in range(1, pieces_ref.shape[0]):
        total = total + pieces_ref[i]
    out_ref[0:4, :] = total[:, :64]
    out_ref[4:8, :] = total[:, 64:]


def fourier_numpy(samples):
    turn = np.arange(1, FREQ + 1)[:, None] * np.arange(samples)[None, :] % samples
    angle = 2.0 * np.pi / samples * turn
    return np.cos(angle) / np.sqrt(samples), -np.sin(angle) / np.sqrt(samples)


def fast_device(plan, flow_field, flux_jacobian, history, surface_cell, surface_blocks, observers):
    f32 = jnp.float32
    shape = jax.ShapeDtypeStruct
    group, wr, lanes = plan.group, plan.wr, plan.lanes
    field_rows = 5 * (plan.ax + 2) * plan.az * plan.tall_pad
    bind = functools.partial

    packed = call(
        bind(pack_kernel, plan),
        shape((group, plan.sent, lanes), f32),
        [VMEM, VMEM, SMEM],
        VMEM,
        [pltpu.VMEM((5 * wr, lanes), f32)],
    )(flow_field.reshape(5, lanes, wr), surface_cell.T, surface_blocks)
    packed, surface_cell = lax.optimization_barrier((packed, surface_cell))
    got = move(GROUP)(packed)

    tile_count = plan.capacity // 128
    cell = surface_cell.reshape(-1)
    index_x, index_z, index_r = (lax.axis_index(name) for name in AXES)
    points = jnp.stack(
        [
            index_x * plan.wx + cell // (plan.wz * wr),
            index_z * plan.wz + cell // wr % plan.wz,
            index_r * wr + cell % wr,
        ]
    ).astype(f32) + 0.5
    points = jnp.transpose(points.reshape(3, tile_count, 128), (1, 0, 2))
    cos_t, sin_t = fourier_numpy(plan.samples)
    table = np.concatenate([cos_t, sin_t], axis=0).astype(np.float32)
    table[:, plan.samples - STEPS :] = 0.0
    spec, watch = pl.pallas_call(
        bind(dft_kernel, plan),
        out_shape=(shape((tile_count, 264, 128), f32), shape((plan.obs, 8), f32)),
        grid=(tile_count,),
        in_specs=[
            pl.BlockSpec((5, 128, plan.samples), lambda i: (0, i, 0)),
            pl.BlockSpec((64, plan.samples), lambda i: (0, 0)),
            pl.BlockSpec((1, 3, 128), lambda i: (i, 0, 0)),
            pl.BlockSpec((3, plan.obs), lambda i: (0, 0)),
            SMEM,
        ],
        out_specs=(
            pl.BlockSpec((1, 264, 128), lambda i: (i, 0, 0)),
            pl.BlockSpec((plan.obs, 8), lambda i: (0, 0)),
        ),
        name="dft",
        compiler_params=pltpu.CompilerParams(vmem_limit_bytes=40 * 1024 * 1024),
        cost_estimate=pl.CostEstimate(flops=10**9, bytes_accessed=10**6, transcendentals=0),
    )(jnp.transpose(history, (1, 0, 2)), jnp.asarray(table), points, observers, surface_blocks)

    def radiated(ways, sources, pieces=1):
        share = plan.obs // ways // pieces
        return [
            call(
                bind(hist_kernel, plan, ways, i * share, 32),
                shape((share, 64), f32),
                [VMEM] * (1 + len(sources)),
                VMEM,
                [pltpu.VMEM((64, 32, 128), f32)],
                flops=10**9,
            )(watch, *sources)
            for i in range(pieces)
        ]

    near_swap = [(i, i ^ 1) for i in range(plan.rows)]
    if plan.rows % 4 == 0:
        across = move("row", [(i, i ^ 2) for i in range(plan.rows)])(spec)
        hists = radiated(4, [spec, move("row", near_swap)(spec)], 2)
    elif plan.rows % 2 == 0:
        hists = radiated(2, [spec, move("row", near_swap)(spec)], 2)
    else:
        hists = radiated(1, [spec], 2)
    flat = got.reshape(group * plan.sent, lanes)
    flat, hists[0] = lax.optimization_barrier((flat, hists[0]))
    first, second, own = call(
        bind(edge_kernel, plan),
        (shape((5 * group * HALO, lanes), f32),) * 2 + (shape((group * plan.body, lanes), f32),),
        [VMEM],
        (VMEM, VMEM, VMEM),
    )(flat)
    ready = first
    line = plan.line()
    swap_a = [(line[i], line[i ^ 1]) for i in range(len(line))]
    swap_b = [
        (line[i], line[((i + 1) ^ 1) - 1]) for i in range(1, len(line) - 1)
    ]
    first = move(AXES, swap_a)(first)
    second = move(AXES, swap_b)(second)

    if plan.rows % 4 == 0:
        across, _ = lax.optimization_barrier((across, ready))
        hists += radiated(4, [across, move("row", near_swap)(across)])
    parts = len(hists)
    near_parts = 2

    ids = entries(plan, got[:, plan.body : plan.body + 4, :])
    listed, count = call(
        bind(list_kernel, plan),
        (shape((group * SURF_DEV + 8,), jnp.int32), shape((1,), jnp.int32)),
        [SMEM],
        (SMEM, SMEM),
    )(ids)

    own, listed, count, hists = lax.optimization_barrier((own, listed, count, hists))
    back, samp = call(
        bind(stencil_kernel, plan),
        (shape((group * plan.body, lanes), f32), shape((plan.chunk * 8 * 16, lanes), f32)),
        [VMEM, VMEM, VMEM, SMEM],
        (VMEM, VMEM),
        [
            pltpu.VMEM((field_rows, lanes), f32),
            pltpu.VMEM((field_rows, lanes), f32),
            pltpu.VMEM((field_rows, lanes), f32),
            pltpu.VMEM((75, 8, lanes), f32),
            pltpu.VMEM((plan.tall_pad, lanes), f32),
            pltpu.VMEM((30 * plan.az, 8, lanes), f32),
        ],
        flops=10**9,
    )(own, first, second, flux_jacobian)
    back = move(GROUP)(back.reshape(group, plan.body, lanes))

    columns = np.zeros((FREQ, 8), np.float32)
    for s in range(STEPS):
        columns[:, 2 * s] = cos_t[:, plan.samples - STEPS + s]
        columns[:, 2 * s + 1] = sin_t[:, plan.samples - STEPS + s]
    columns[:, 6] = 1.0 / np.arange(1, FREQ + 1)
    partial = call(
        bind(recent_kernel, plan, parts, near_parts),
        shape((plan.obs // 2, 128), f32),
        [SMEM, SMEM, VMEM, VMEM, VMEM] + [VMEM] * parts,
        VMEM,
        [
            pltpu.VMEM((128, 128), f32),
            pltpu.VMEM((24, 128), f32),
            pltpu.VMEM((plan.obs // 128 * FREQ * 8, 128), f32),
            pltpu.VMEM((plan.obs // 128 * FREQ * 8, 128), f32),
            pltpu.VMEM((plan.obs // 128 * STEPS * 8, 128), f32),
            pltpu.VMEM((plan.obs // 128 * STEPS * 8, 128), f32),
            pltpu.VMEM((plan.obs, 128), f32),
            pltpu.VMEM((plan.obs // 128 * (FREQ // 8) * 12, 8, 128), f32),
            pltpu.VMEM((128, 128), f32),
        ],
        flops=10**9,
    )(listed, count, samp, observers, jnp.asarray(columns), *hists)
    pieces = move(AXES)(partial.reshape(plan.devices, 4, 128))
    spectrum = call(sum_kernel, shape((plan.per_obs, 2 * FREQ), f32), [VMEM], VMEM)(pieces)
    field = call(
        bind(unpack_kernel, plan), shape((5, lanes, wr), f32), [VMEM], VMEM, [pltpu.VMEM((5 * wr, lanes), f32)]
    )(back)
    return field.reshape(flow_field.shape), spectrum


def per_device(*args):
    flow_field, _, history, surface_cell, _, observers = args
    mesh = {name: lax.axis_size(name) for name in AXES}
    plan = Plan(mesh, flow_field.shape[1:], surface_cell.shape, history.shape, observers.shape[1])
    if plan.fits():
        return fast_device(plan, *args)
    return general_device(*args)


def solution(mesh):
    return jax.shard_map(
        per_device,
        mesh=mesh,
        in_specs=(
            P(None, "gx", "gz", "row"),
            P(),
            P(("gx", "gz", "row"), None, None),
            P(("gx", "gz", "row"), None),
            P("row", ("gx", "gz")),
            P(),
        ),
        out_specs=(P(None, "gx", "gz", "row"), P(("gx", "gz", "row"), None)),
        check_vma=False,
    )
```

```python
import functools
import math

import jax
import jax.numpy as jnp
import numpy as np
from jax import lax
from jax.experimental import pallas as pl
from jax.experimental.pallas import tpu as pltpu
from jax.sharding import PartitionSpec as P


SURF_DEV = 128
FREQ = 32
STEPS = 3


TIME_STEP = 0.3
VISCOSITY = 0.05


def padded_2(value, sides, width):
    for axis, dim in sides:
        peers, length = (lax.axis_size(axis), value.shape[dim])
        up = [(i, (i + 1) % peers) for i in range(peers - 1)]
        down = [(j, i) for i, j in up]
        last = lax.slice_in_dim(value, length - width, length, axis=dim)
        leading = lax.slice_in_dim(value, 0, width, axis=dim)
        before = lax.ppermute(last, axis, up)
        after = lax.ppermute(leading, axis, down)
        value = jnp.concatenate([before, value, after], axis=dim)
    return value


def stencil_rate(padded, flux_jacobian):
    center = padded[:, 1:-1, 1:-1, 1:-1]
    along_x = (padded[:, 2:, 1:-1, 1:-1] - padded[:, :-2, 1:-1, 1:-1]) * 0.5
    along_z = (padded[:, 1:-1, 2:, 1:-1] - padded[:, 1:-1, :-2, 1:-1]) * 0.5
    along_r = (padded[:, 1:-1, 1:-1, 2:] - padded[:, 1:-1, 1:-1, :-2]) * 0.5
    beside = padded[:, 2:, 1:-1, 1:-1] + padded[:, :-2, 1:-1, 1:-1]
    beside = beside + padded[:, 1:-1, 2:, 1:-1] + padded[:, 1:-1, :-2, 1:-1]
    beside = beside + padded[:, 1:-1, 1:-1, 2:] + padded[:, 1:-1, 1:-1, :-2]
    slopes = jnp.stack([along_x, along_z, along_r])
    transport = jnp.einsum(
        "dvw,dwxzr->vxzr", flux_jacobian, slopes, precision=lax.Precision.HIGHEST
    )
    return transport + VISCOSITY * (beside - 6.0 * center)


def fourier_table(samples, freq_count):
    time_ids = jnp.arange(samples, dtype=jnp.int32)
    freq_ids = jnp.arange(1, freq_count + 1, dtype=jnp.int32)
    turn_ids = freq_ids[:, None] * time_ids[None, :] % samples
    angles = 2.0 * math.pi / samples * turn_ids.astype(jnp.float32)
    norm_scale = 1.0 / math.sqrt(samples)
    return jnp.concatenate([jnp.cos(angles), -jnp.sin(angles)], axis=0) * norm_scale


def spectra_of(signals, fourier):
    return jnp.einsum("ft,svt->vfs", fourier, signals, precision=lax.Precision.HIGHEST)


def radiate(points, monopole, dipole, watchers, radial_cells, freq_count):
    wavenumbers = jnp.arange(1, freq_count + 1, dtype=jnp.float32) * (2.0 / radial_cells)
    offset_vec = watchers[:, :, None] - points[None, :, :]
    distance = jnp.sqrt(jnp.sum(offset_vec * offset_vec, axis=1))
    direction = offset_vec / distance[:, None, :]
    amplitude = (radial_cells / distance)[:, None, :]
    dip_real = direction[:, 0, None, :] * dipole[0, None, :freq_count, :]
    dip_real = dip_real + direction[:, 1, None, :] * dipole[1, None, :freq_count, :]
    dip_real = dip_real + direction[:, 2, None, :] * dipole[2, None, :freq_count, :]
    dip_imag = direction[:, 0, None, :] * dipole[0, None, freq_count:, :]
    dip_imag = dip_imag + direction[:, 1, None, :] * dipole[1, None, freq_count:, :]
    dip_imag = dip_imag + direction[:, 2, None, :] * dipole[2, None, freq_count:, :]
    mono_real = monopole[None, :freq_count, :]
    mono_imag = monopole[None, freq_count:, :]
    phase_arg = distance[:, None, :] * wavenumbers[None, :, None]
    near_term = 1.0 / phase_arg
    cosine = amplitude * jnp.cos(phase_arg)
    sine = amplitude * jnp.sin(phase_arg)
    plus_weight = cosine * near_term + sine
    minus_weight = cosine - sine * near_term
    out_real = jnp.sum(
        plus_weight * dip_real - minus_weight * dip_imag + sine * mono_real - cosine * mono_imag,
        axis=2,
    )
    out_imag = jnp.sum(
        minus_weight * dip_real + plus_weight * dip_imag + cosine * mono_real + sine * mono_imag,
        axis=2,
    )
    return jnp.concatenate([out_real, out_imag], axis=1)


def general_device(flow_field, flux_jacobian, history, surface_cell, surface_blocks, observers):
    width_x, width_z, width_r = (flow_field.shape[1], flow_field.shape[2], flow_field.shape[3])
    count_x, count_z, count_r = (lax.axis_size("gx"), lax.axis_size("gz"), lax.axis_size("row"))
    index_x, index_z, index_r = (lax.axis_index("gx"), lax.axis_index("gz"), lax.axis_index("row"))
    owners = count_x * count_z
    devices = owners * count_r
    radial_cells = width_r * count_r
    slot_rows = surface_cell.shape[0]
    capacity = slot_rows * owners
    samples = history.shape[2]
    cell_ids = surface_cell.reshape(-1)

    def inside_mask(margin):
        coord_x = index_x * width_x + jnp.arange(width_x + 2 * margin, dtype=jnp.int32) - margin
        coord_z = index_z * width_z + jnp.arange(width_z + 2 * margin, dtype=jnp.int32) - margin
        coord_r = index_r * width_r + jnp.arange(width_r + 2 * margin, dtype=jnp.int32) - margin
        valid_x = (coord_x >= 0) & (coord_x < width_x * count_x)
        valid_z = (coord_z >= 0) & (coord_z < width_z * count_z)
        valid_r = (coord_r >= 0) & (coord_r < radial_cells)
        joined = valid_x[:, None, None] & valid_z[None, :, None] & valid_r[None, None, :]
        return joined.astype(jnp.float32)[None]

    mask_outer = inside_mask(2)
    mask_inner = inside_mask(1)
    current = flow_field
    sampled = []
    for _ in range(STEPS):
        extended = padded_2(current, (("gx", 1), ("gz", 2), ("row", 3)), 3)
        section_one = (
            extended[:, 1:-1, 1:-1, 1:-1] + TIME_STEP * stencil_rate(extended, flux_jacobian)
        ) * mask_outer
        section_two = 0.75 * extended[:, 2:-2, 2:-2, 2:-2] + 0.25 * (
            section_one[:, 1:-1, 1:-1, 1:-1] + TIME_STEP * stencil_rate(section_one, flux_jacobian)
        )
        section_two = section_two * mask_inner
        current = extended[:, 3:-3, 3:-3, 3:-3] / 3.0 + 2.0 / 3.0 * (
            section_two[:, 1:-1, 1:-1, 1:-1] + TIME_STEP * stencil_rate(section_two, flux_jacobian)
        )
        sampled.append(jnp.take(current.reshape(5, -1), cell_ids, axis=1))
    recent = jnp.transpose(jnp.stack(sampled, axis=2), (1, 0, 2))
    signals = jnp.concatenate([history[:, :, : samples - STEPS], recent], axis=2)
    global_x = index_x * width_x + cell_ids // (width_z * width_r)
    global_z = index_z * width_z + cell_ids // width_r % width_z
    global_r = index_r * width_r + cell_ids % width_r
    positions = jnp.stack([global_x, global_z, global_r]).astype(jnp.float32) + 0.5
    fourier = fourier_table(samples, FREQ)
    live_mask = (jnp.arange(capacity, dtype=jnp.int32) // owners < surface_blocks[0, 0]).astype(
        jnp.float32
    )
    spectra = spectra_of(signals, fourier) * live_mask
    monopole = spectra[0] + spectra[4]
    dipole = spectra[1:4]
    watchers = jnp.stack(
        [
            observers[0] * (width_x * count_x),
            observers[1] * (width_z * count_z),
            (1.25 + 0.75 * observers[2]) * radial_cells,
        ],
        axis=1,
    )
    norm_scale = math.sqrt(devices * SURF_DEV)
    row_count = observers.shape[1] // devices * lax.axis_size(("gx", "gz", "row"))
    block_size = math.gcd(row_count, 32)

    def one_block(block):
        return radiate(positions, monopole, dipole, block, radial_cells, FREQ)

    blocks_out = lax.map(one_block, watchers.reshape(row_count // block_size, block_size, 3))
    spectrum = lax.psum_scatter(
        blocks_out.reshape(row_count, 2 * FREQ) / norm_scale,
        ("gx", "gz", "row"),
        scatter_dimension=0,
        tiled=True,
    )
    return (current, spectrum)


HALO = 3 * STEPS
AXES = ("gx", "gz", "row")
GROUP = ("gx", "gz")
VMEM = pl.BlockSpec(memory_space=pltpu.VMEM)
SMEM = pl.BlockSpec(memory_space=pltpu.SMEM)


def halves(value, by):
    if by & (by - 1) == 0:
        return value >> (by.bit_length() - 1), value & (by - 1)
    return value // by, value % by


def sin_cos(angle):
    turns = jnp.floor(angle * (2.0 / math.pi) + 0.5)
    rest = ((angle - turns * 1.5703125) - turns * 4.837512969970703e-4) - turns * 7.549789954891882e-8
    square = rest * rest
    sine = rest + rest * square * (
        -1.6666654611e-1 + square * (8.3321608736e-3 + square * -1.9515295891e-4)
    )
    cosine = (1.0 - 0.5 * square) + square * square * (
        4.166664568298827e-2 + square * (-1.388731625493765e-3 + square * 2.443315711809948e-5)
    )
    quarter = turns.astype(jnp.int32) & 3
    odd = (quarter & 1) == 1
    out_sine = jnp.where(odd, cosine, sine)
    out_cosine = jnp.where(odd, sine, cosine)
    out_sine = jnp.where(quarter >= 2, -out_sine, out_sine)
    out_cosine = jnp.where((quarter == 1) | (quarter == 2), -out_cosine, out_cosine)
    return out_sine, out_cosine


class Plan:
    def __init__(self, mesh, flow, cells, hist, obs):
        self.ax, self.az, self.rows = mesh["gx"], mesh["gz"], mesh["row"]
        self.group = self.ax * self.az
        self.devices = self.group * self.rows
        self.wx, self.wz, self.wr = flow
        self.blocks = cells[0]
        self.capacity = cells[0] * cells[1]
        self.samples = hist[2]
        self.lanes = self.wx * self.wz
        self.chunk = self.wr // self.group
        self.nx, self.nz, self.nr = self.wx * self.ax, self.wz * self.az, self.wr * self.rows
        self.obs = obs
        self.body = 5 * self.chunk
        self.sent = self.body + 8
        self.per_obs = obs // self.devices
        self.tall_pad = (self.chunk + 2 * HALO + 8) // 8 * 8 + 8

    def fits(self):
        return (
            self.group == 8
            and self.lanes == 128
            and self.wr % 128 == 0
            and self.chunk % 8 == 0
            and self.chunk >= 2 * 8
            and self.chunk >= HALO
            and self.capacity == self.blocks * 8
            and 2 * self.blocks < 127
            and self.capacity % 128 == 0
            and self.samples == 128
            and self.obs % 128 == 0
            and self.obs % self.devices == 0
            and self.obs // self.devices == 8
            and FREQ == 32
            and STEPS == 3
        )

    def order_of(self, a, b):
        return b * self.ax + (a if b % 2 == 0 else self.ax - 1 - a)

    def table(self):
        return [self.order_of(j // self.az, j % self.az) for j in range(self.group)]

    def line(self):
        out = []
        for c in range(self.rows):
            order = self.table()
            if c % 2:
                order = [self.group - 1 - q for q in order]
            for q in range(self.group):
                out.append(order.index(q) * self.rows + c)
        return out

    def chunk_of(self, j, c):
        q = self.table()[j]
        return jnp.where(c % 2 == 1, self.group - 1 - q, q)

    def own_chunk(self):
        a, b, c = lax.axis_index("gx"), lax.axis_index("gz"), lax.axis_index("row")
        q = b * self.ax + jnp.where(b % 2 == 0, a, self.ax - 1 - a)
        return jnp.where(c % 2 == 1, self.group - 1 - q, q), c


def call(kernel, out_shape, in_specs, out_specs, scratch=(), flops=10**6):
    kernel_call = pl.pallas_call(
        kernel,
        out_shape=out_shape,
        in_specs=in_specs,
        out_specs=out_specs,
        scratch_shapes=list(scratch),
        compiler_params=pltpu.CompilerParams(vmem_limit_bytes=40 * 1024 * 1024),
        cost_estimate=pl.CostEstimate(flops=flops, bytes_accessed=10**5, transcendentals=0),
    )
    return kernel_call


def move(axes, *pairs):
    if pairs:
        return lambda value: lax.ppermute(value, axes, pairs[0])
    return lambda value: lax.all_to_all(value, axes, 0, 0, tiled=True)


def pack_kernel(plan, flow_ref, cell_ref, live_ref, out_ref, turned):
    c = lax.axis_index("row")
    for v in range(5):
        turned[v * plan.wr : (v + 1) * plan.wr, :] = flow_ref[v].T
    cells = cell_ref[...].astype(jnp.float32)
    ids = jnp.concatenate([cells[:4], cells[4:], jnp.zeros((4, 128 - 2 * plan.blocks), jnp.float32)], axis=1)
    ids = jnp.concatenate([ids, jnp.zeros((4, 128), jnp.float32)], axis=0)
    lane = lax.broadcasted_iota(jnp.int32, (8, 128), 1)
    ids = jnp.where(lane == 127, live_ref[0, 0].astype(jnp.float32), ids)
    for j in range(plan.group):
        q = plan.chunk_of(j, c)
        for v in range(5):
            start = pl.multiple_of(v * plan.wr + q * plan.chunk, 8)
            out_ref[j, v * plan.chunk : (v + 1) * plan.chunk, :] = turned[pl.ds(start, plan.chunk), :]
        out_ref[j, plan.body : plan.body + 8, :] = ids


def edge_kernel(plan, got_ref, first_ref, second_ref, own_ref):
    q, c = plan.own_chunk()
    even = (c * plan.group + q) % 2 == 0
    high, low = plan.chunk - HALO, 0
    first = jnp.where(even, high, low)
    second = jnp.where(even, low, high)
    for v in range(5):
        for g in range(plan.group):
            at = (v * plan.group + g) * HALO
            row = g * plan.sent + v * plan.chunk
            first_ref[at : at + HALO, :] = got_ref[pl.ds(row + first, HALO), :]
            second_ref[at : at + HALO, :] = got_ref[pl.ds(row + second, HALO), :]
            at = (v * plan.group + g) * plan.chunk
            own_ref[at : at + plan.chunk, :] = got_ref[row : row + plan.chunk, :]


def stencil_kernel(plan, own_ref, first_ref, second_ref, jac_ref, back_ref, samp_ref, staged, done, cur, one, two, coef, mask, side):
    q, c = plan.own_chunk()
    place = c * plan.group + q
    even = place % 2 == 0
    tall = plan.chunk + 2 * HALO
    wz, lanes, az, ax, wx = plan.wz, plan.lanes, plan.az, plan.ax, plan.wx
    high = plan.tall_pad
    per = (ax + 2) * az * high

    def base(v, a, b):
        return v * per + ((a + 1) * az + b) * high

    has_low = jnp.where(place > 0, 1.0, 0.0)
    has_high = jnp.where(place < plan.rows * plan.group - 1, 1.0, 0.0)
    row = lax.broadcasted_iota(jnp.int32, (high, 128), 0)
    mask[...] = jnp.where(row < HALO, has_low, jnp.where(row >= HALO + plan.chunk, has_high, 1.0))
    for d in range(3):
        scaled = jac_ref[d] * (0.5 * TIME_STEP)
        for v in range(5):
            for w in range(5):
                coef[(d * 5 + v) * 5 + w] = jnp.broadcast_to(scaled[v : v + 1, w : w + 1], (8, 128))
    zeros = jnp.zeros((az * high, 128), jnp.float32)
    for ref in (cur, one, two):
        for v in range(5):
            for a in (-1, ax):
                ref[base(v, a, 0) : base(v, a, 0) + az * high, :] = zeros
    for v in range(5):
        for a in range(ax):
            for b in range(az):
                at = base(v, a, b) + HALO
                source = (v * plan.group + a * az + b) * plan.chunk
                cur[at : at + plan.chunk, :] = own_ref[source : source + plan.chunk, :]

    def put(low_ref, high_ref):
        for v in range(5):
            for a in range(ax):
                for b in range(az):
                    at = base(v, a, b)
                    source = (v * plan.group + a * az + b) * HALO
                    cur[at : at + HALO, :] = low_ref[source : source + HALO, :]
                    at = at + HALO + plan.chunk
                    cur[at : at + HALO, :] = high_ref[source : source + HALO, :]

    @pl.when(even)
    def _():
        put(second_ref, first_ref)

    @pl.when(jnp.logical_not(even))
    def _():
        put(first_ref, second_ref)

    lane = lax.broadcasted_iota(jnp.int32, (8, 128), 1)
    x_l, z_l = halves(lane, wz)
    zero = jnp.zeros((8, 128), jnp.float32)
    damp = VISCOSITY * TIME_STEP

    many = 2 if ax % 2 == 0 else 1
    spots = [(i, b) for i in range(many) for b in range(az)]
    keys = [(w, i, b) for w in range(5) for i, b in spots]
    far = {(w, i, b): w * per + (i * az + b) * high for w, i, b in keys}
    side_step = az * high

    def turns_of(number):
        return ((tall - 2 * number + 7) >> 3) * (ax // many)

    def places(number, turn):
        block, a = halves(turn, ax // many)
        start = number + block * 8
        return start, (a * many + 1) * (az * high) + start

    grids = (cur, one, two)

    def across(number, turn):
        src = grids[(number - 1) % 3]
        _, root = places(number, turn)
        mid = {k: src[pl.ds(root + far[k], 8), :] for k in keys}
        found = []
        for w, i, b in keys:
            k = (w, i, b)
            ahead = src[pl.ds(root + (far[k] + side_step), 8), :]
            behind = src[pl.ds(root + (far[k] - side_step), 8), :]
            x_next = pltpu.roll(jnp.where(x_l == 0, ahead, mid[k]), lanes - wz, 1)
            x_prev = pltpu.roll(jnp.where(x_l == wx - 1, behind, mid[k]), wz, 1)
            z_edge = pltpu.roll(mid[w, i, b + 1], wz - 1, 1) if b < az - 1 else zero
            z_next = jnp.where(z_l < wz - 1, pltpu.roll(mid[k], lanes - 1, 1), z_edge)
            z_edge = pltpu.roll(mid[w, i, b - 1], lanes - (wz - 1), 1) if b > 0 else zero
            z_prev = jnp.where(z_l > 0, pltpu.roll(mid[k], 1, 1), z_edge)
            found.append((x_next - x_prev, z_next - z_prev, (x_next + x_prev) + (z_next + z_prev)))
        return found

    def store(found):
        for i, values in enumerate(found):
            for d in range(3):
                side[3 * i + d] = values[d]

    order = {k: i for i, k in enumerate(keys)}

    def advance(number, turn, next_number, next_turn):
        part = (number - 1) % 3
        src, dst = grids[part], grids[(part + 1) % 3]
        keep, gain = ((0.0, 1.0), (0.75, 0.25), (1.0 / 3.0, 2.0 / 3.0))[part]
        start, root = places(number, turn)
        coming = across(next_number, next_turn)
        inside = mask[pl.ds(start, 8), :]
        for i, b in spots:
            total = []
            slopes = []
            for w in range(5):
                k = (w, i, b)
                after, before = src[pl.ds(root + (far[k] + 1), 8), :], src[pl.ds(root + (far[k] - 1), 8), :]
                around = side[3 * order[k] + 2] + (after + before)
                total.append((1.0 - 6.0 * damp) * src[pl.ds(root + far[k], 8), :] + damp * around)
                slopes.append((after - before, side[3 * order[k] + 1], side[3 * order[k]]))
            for d in range(3):
                for w in range(5):
                    for v in range(5):
                        total[v] = total[v] + coef[((2 - d) * 5 + v) * 5 + w] * slopes[w][d]
            for v in range(5):
                k = (v, i, b)
                value = total[v] * (gain * inside)
                if part:
                    value = (keep * inside) * cur[pl.ds(root + far[k], 8), :] + value
                dst[pl.ds(root + far[k], 8), :] = value
        store(coming)

    store(across(1, 0))
    for number in range(1, 3 * STEPS + 1):
        turns = turns_of(number)

        @pl.loop(0, turns - 1)
        def _(turn):
            advance(number, turn, number, turn + 1)

        if number < 3 * STEPS:
            advance(number, turns - 1, number + 1, 0)
        else:
            advance(number, turns - 1, number, turns - 1)
        if number % 3:
            continue
        step = number // 3 - 1
        if step == STEPS - 1:
            for v in range(5):
                for a in range(ax):
                    for b in range(az):
                        at = base(v, a, b) + HALO
                        target = (a * az + b) * plan.body + v * plan.chunk
                        staged[target : target + plan.chunk, :] = cur[at : at + plan.chunk, :]
            leave = pltpu.make_async_copy(staged, back_ref, done)
            leave.start()
        for a in range(ax):
            for b in range(az):
                for r in range(0, plan.chunk, 8):
                    own = [cur[base(v, a, b) + HALO + r : base(v, a, b) + HALO + r + 8, :] for v in range(5)]
                    own[0] = own[0] + own[4]
                    for ch in range(4):
                        at = (r * plan.group + a * az + b) * 16 + ch * STEPS + step
                        samp_ref[pl.ds(at, 8, stride=plan.group * 16), :] = own[ch]
    leave.wait()


def unpack_kernel(plan, back_ref, out_ref, turned):
    c = lax.axis_index("row")
    for j in range(plan.group):
        q = plan.chunk_of(j, c)
        for v in range(5):
            start = pl.multiple_of(v * plan.wr + q * plan.chunk, 8)
            turned[pl.ds(start, plan.chunk), :] = back_ref[j, v * plan.chunk : (v + 1) * plan.chunk, :]
    for v in range(5):
        out_ref[v] = turned[v * plan.wr : (v + 1) * plan.wr, :].T


def list_kernel(plan, entry_ref, list_ref, count_ref):
    def source(g, count):
        def block(n, count):
            found = [entry_ref[g * 512 + n + (k % 4 * 128 + k // 4 * plan.blocks)] for k in range(8)]
            for entry in found:
                list_ref[count] = entry
                count = count + (entry >> 20)
            return count

        return lax.fori_loop(0, entry_ref[g * 512 + 127], block, count)

    count = lax.fori_loop(0, 8, source, 0)
    count_ref[0] = count
    for k in range(8):
        list_ref[count + k] = 0


def entries(plan, ids):
    cell = ids.astype(jnp.int32)
    lane, r = halves(cell, plan.wr)
    q, r_l = halves(r, plan.chunk)
    g = lax.broadcasted_iota(jnp.int32, cell.shape, 0)
    mine, _ = plan.own_chunk()
    entry = (r_l * 8 + g) * 128 + lane + jnp.where(q == mine, 1 << 20, 0)
    last = lax.broadcasted_iota(jnp.int32, cell.shape, 2) == 127
    return jnp.where(last, cell, entry).reshape(-1)


def dft_kernel(plan, hist_ref, point_ref, obs_ref, live_ref, out_ref, watch_ref):
    tile = pl.program_id(0)

    @pl.when(tile == 0)
    def _():
        seen = obs_ref[...]
        rows = [seen[0:1] * float(plan.nx), seen[1:2] * float(plan.nz), (1.25 + 0.75 * seen[2:3]) * float(plan.nr)]
        rows.append(jnp.zeros((5, plan.obs), jnp.float32))
        watch_ref[...] = jnp.concatenate(rows, axis=0).T

    out_ref[0, 256:259, :] = point_ref[0]
    out_ref[0, 259:264, :] = jnp.full((5, 128), live_ref[0, 0].astype(jnp.float32))
    live = live_ref[0, 0] * 8
    keep = lax.broadcasted_iota(jnp.int32, (64, 128), 1) + tile * 128 < live
    row = lax.broadcasted_iota(jnp.int32, (64, 128), 0)
    time = lax.broadcasted_iota(jnp.int32, (64, 128), 1)
    freq = jnp.where(row < FREQ, row, row - FREQ) + 1
    turn = halves(freq * time, plan.samples)[1]
    sine, cosine = sin_cos(turn.astype(jnp.float32) * (2.0 * math.pi / plan.samples))
    table = jnp.where(row < FREQ, cosine, -sine) * (1.0 / math.sqrt(plan.samples))
    table = split(jnp.where(time < plan.samples - STEPS, table, 0.0))
    for ch in range(4):
        signal = hist_ref[ch]
        if ch == 0:
            signal = signal + hist_ref[4]
        signal = split(signal)
        spec = jnp.zeros((64, 128), jnp.float32)
        for i, j in ((0, 1), (1, 0), (0, 0)):
            spec = spec + lax.dot_general(
                table[i], signal[j], (((1,), (1,)), ((), ())), preferred_element_type=jnp.float32
            )
        out_ref[0, ch * 64 : (ch + 1) * 64, :] = jnp.where(keep, spec, 0.0)


def split(value):
    high = value.astype(jnp.bfloat16)
    return high, (value - high.astype(jnp.float32)).astype(jnp.bfloat16)


def geometry(plan, watch, point):
    offset = [w - p for w, p in zip(watch, point, strict=True)]
    square = offset[0] * offset[0] + offset[1] * offset[1] + offset[2] * offset[2]
    distance = jnp.sqrt(square)
    inverse = 1.0 / distance
    along = [o * inverse for o in offset]
    amplitude = plan.nr * inverse
    sine, cosine = sin_cos(distance * (2.0 / plan.nr))
    near = (plan.nr * 0.5) * inverse
    return along, amplitude, sine, cosine, near


def hist_kernel(plan, ways, first, wide, watch_ref, *refs):
    spec_refs, out_ref, acc = refs[:-2], refs[-2], refs[-1]
    lane = lax.broadcasted_iota(jnp.int32, (wide, 64), 1)
    mine = (lax.axis_index("row") % ways) * (plan.obs // ways)
    tiles = [(jnp.max(ref[0, 259:260, :]).astype(jnp.int32) * 8 + 127) // 128 for ref in spec_refs]

    @pl.loop(0, out_ref.shape[0] // wide)
    def _(ob):
        start = pl.multiple_of(ob * wide, 8)
        row = pl.multiple_of(mine + first + start, 8)
        watch = [jnp.broadcast_to(watch_ref[pl.ds(row, wide), d : d + 1], (wide, 128)) for d in range(3)]
        acc[...] = jnp.zeros_like(acc)

        def radiate_tile(spec_ref, tile):
            point = [spec_ref[tile, 256 + d : 257 + d, :] for d in range(3)]
            along, amplitude, sine, cosine, near = geometry(plan, watch, point)
            twice = 2.0 * cosine
            cos_last, sin_last = amplitude, jnp.zeros_like(amplitude)
            cos_now, sin_now = amplitude * cosine, amplitude * sine
            for f in range(FREQ):
                rows = [spec_ref[tile, pl.ds(k * 32 + f, 1), :] for k in range(8)]
                d_re = along[0] * rows[2] + along[1] * rows[4] + along[2] * rows[6]
                d_im = along[0] * rows[3] + along[1] * rows[5] + along[2] * rows[7]
                weight = near * (1.0 / (f + 1))
                e_re = (rows[0] + d_re) + weight * d_im
                e_im = (rows[1] + d_im) - weight * d_re
                acc[f] = acc[f] + (sin_now * e_re - cos_now * e_im)
                acc[FREQ + f] = acc[FREQ + f] + (cos_now * e_re + sin_now * e_im)
                cos_now, cos_last = twice * cos_now - cos_last, cos_now
                sin_now, sin_last = twice * sin_now - sin_last, sin_now

        for spec_ref, count in zip(spec_refs, tiles, strict=True):
            pl.loop(0, count)(functools.partial(radiate_tile, spec_ref))

        out = jnp.zeros((wide, 64), jnp.float32)
        for f in range(2 * FREQ):
            out = jnp.where(lane == f, jnp.sum(acc[f], axis=1, keepdims=True), out)
        out_ref[pl.ds(start, wide), :] = out


def recent_kernel(plan, parts, near_parts, list_ref, count_ref, samp_ref, obs_ref, tab_ref, *refs):
    hist_refs, out_ref = refs[:parts], refs[parts]
    value, place, cos_s, sin_s, mono, dip, full, acc, final = refs[parts + 1 :]
    q, c = plan.own_chunk()
    count = count_ref[0]
    tiles = plan.obs // 128
    lane = lax.broadcasted_iota(jnp.int32, (16, 128), 1)
    acc[...] = jnp.zeros_like(acc)

    groups = (count + 7) // 8

    def sample(group):
        picked, spots = [], []
        for k in range(8):
            entry = list_ref[group * 8 + k] & ((1 << 20) - 1)
            row, at = halves(entry, 128)
            tile = samp_ref[pl.ds(pl.multiple_of(row * 16, 16), 16), :]
            r_l, g = halves(row, 8)
            a, b = halves(g, plan.az)
            x_l, z_l = halves(at, plan.wz)
            spots.append((a * plan.wx + x_l, b * plan.wz + z_l, c * plan.wr + q * plan.chunk + r_l))
            at = jnp.where(group * 8 + k < count, at, -1)
            picked.append(jnp.sum(jnp.where(lane == at, tile, 0.0), axis=1, keepdims=True))
        return picked, spots

    def keep(found):
        for k in range(8):
            value[k * 16 : (k + 1) * 16, :] = jnp.broadcast_to(found[0][k], (16, 128))
            for d in range(3):
                spot = found[1][k][d].astype(jnp.float32) + 0.5
                place[d * 8 + k : d * 8 + k + 1, :] = jnp.full((1, 128), spot)

    keep(sample(0))

    @pl.loop(0, groups)
    def _(group):
        point = [place[d * 8 : (d + 1) * 8, :] for d in range(3)]
        drawn = [value[pl.ds(i, 8, stride=16), :] for i in range(4 * STEPS)]
        coming = sample(jnp.minimum(group + 1, groups - 1))
        for t in range(tiles):
            seen = obs_ref[:, t * 128 : (t + 1) * 128]
            watch = [
                seen[0:1] * float(plan.nx),
                seen[1:2] * float(plan.nz),
                (1.25 + 0.75 * seen[2:3]) * float(plan.nr),
            ]
            along, amplitude, sine, cosine, near = geometry(plan, watch, point)
            for s in range(STEPS):
                push = along[0] * drawn[STEPS + s] + along[1] * drawn[2 * STEPS + s] + along[2] * drawn[3 * STEPS + s]
                at = (t * STEPS + s) * 8
                mono[at : at + 8, :] = drawn[s] + push
                dip[at : at + 8, :] = near * push
            twice = 2.0 * cosine
            cos_last, sin_last = amplitude, jnp.zeros_like(amplitude)
            cos_now, sin_now = amplitude * cosine, amplitude * sine
            for f in range(FREQ):
                at = (t * FREQ + f) * 8
                cos_s[at : at + 8, :] = cos_now
                sin_s[at : at + 8, :] = sin_now
                cos_now, cos_last = twice * cos_now - cos_last, cos_now
                sin_now, sin_last = twice * sin_now - sin_last, sin_now
        for t in range(tiles):
            for fv in range(FREQ // 8):
                base = (t * (FREQ // 8) + fv) * 12
                sums = [acc[base + i] for i in range(12)]
                for k in range(8):
                    at = (t * FREQ + fv * 8) * 8 + k
                    wave_c = cos_s[pl.ds(at, 8, stride=8), :]
                    wave_s = sin_s[pl.ds(at, 8, stride=8), :]
                    for s in range(STEPS):
                        at = (t * STEPS + s) * 8 + k
                        m = mono[at : at + 1, :]
                        p = dip[at : at + 1, :]
                        sums[4 * s] = sums[4 * s] + wave_c * m
                        sums[4 * s + 1] = sums[4 * s + 1] + wave_s * m
                        sums[4 * s + 2] = sums[4 * s + 2] + wave_c * p
                        sums[4 * s + 3] = sums[4 * s + 3] + wave_s * p
                for i in range(12):
                    acc[base + i] = sums[i]
        keep(coming)

    scale = 1.0 / math.sqrt(plan.devices * SURF_DEV)
    final[...] = jnp.zeros_like(final)
    for t in range(tiles):
        for fv in range(FREQ // 8):
            base = (t * (FREQ // 8) + fv) * 12
            column = tab_ref[fv * 8 : (fv + 1) * 8, :]
            out_re = jnp.zeros((8, 128), jnp.float32)
            out_im = jnp.zeros((8, 128), jnp.float32)
            below = column[:, 6:7]
            for s in range(STEPS):
                part_re = acc[base + 4 * s + 1] + acc[base + 4 * s + 2] * below
                part_im = acc[base + 4 * s] - acc[base + 4 * s + 3] * below
                turn_re, turn_im = column[:, 2 * s : 2 * s + 1], column[:, 2 * s + 1 : 2 * s + 2]
                out_re = out_re + (turn_re * part_re - turn_im * part_im)
                out_im = out_im + (turn_im * part_re + turn_re * part_im)
            final[fv * 8 : (fv + 1) * 8, :] = out_re
            final[FREQ + fv * 8 : FREQ + (fv + 1) * 8, :] = out_im
        full[t * 128 : (t + 1) * 128, :] = final[...].T * scale
    share = sum(ref.shape[0] for ref in hist_refs[:near_parts])
    mine = (lax.axis_index("row") % (plan.obs // share)) * share
    first = 0
    for hist_ref in hist_refs:
        rows = hist_ref.shape[0]
        at = pl.multiple_of(mine + first % share, 8)
        full[pl.ds(at, rows), : 2 * FREQ] = full[pl.ds(at, rows), : 2 * FREQ] + hist_ref[...] * scale
        first += rows
    for k in range(4):
        low = full[pl.ds(k, plan.devices, stride=8), :]
        high = full[pl.ds(k + 4, plan.devices, stride=8), :]
        both = low + pltpu.roll(high, 64, 1)
        out_ref[pl.ds(k, plan.devices, stride=4), :] = both


def sum_kernel(pieces_ref, out_ref):
    total = pieces_ref[0]
    for i in range(1, pieces_ref.shape[0]):
        total = total + pieces_ref[i]
    out_ref[0:4, :] = total[:, :64]
    out_ref[4:8, :] = total[:, 64:]


def fourier_numpy(samples):
    turn = np.arange(1, FREQ + 1)[:, None] * np.arange(samples)[None, :] % samples
    angle = 2.0 * np.pi / samples * turn
    return np.cos(angle) / np.sqrt(samples), -np.sin(angle) / np.sqrt(samples)


def fast_device(plan, flow_field, flux_jacobian, history, surface_cell, surface_blocks, observers):
    f32 = jnp.float32
    shape = jax.ShapeDtypeStruct
    group, wr, lanes = plan.group, plan.wr, plan.lanes
    field_rows = 5 * (plan.ax + 2) * plan.az * plan.tall_pad
    bind = functools.partial

    packed = call(
        bind(pack_kernel, plan),
        shape((group, plan.sent, lanes), f32),
        [VMEM, VMEM, SMEM],
        VMEM,
        [pltpu.VMEM((5 * wr, lanes), f32)],
    )(flow_field.reshape(5, lanes, wr), surface_cell.T, surface_blocks)
    packed, surface_cell = lax.optimization_barrier((packed, surface_cell))
    got = move(GROUP)(packed)

    tile_count = plan.capacity // 128
    cell = surface_cell.reshape(-1)
    index_x, index_z, index_r = (lax.axis_index(name) for name in AXES)
    points = jnp.stack(
        [
            index_x * plan.wx + cell // (plan.wz * wr),
            index_z * plan.wz + cell // wr % plan.wz,
            index_r * wr + cell % wr,
        ]
    ).astype(f32) + 0.5
    points = jnp.transpose(points.reshape(3, tile_count, 128), (1, 0, 2))
    cos_t, sin_t = fourier_numpy(plan.samples)
    cell = surface_cell.reshape(-1)
    index_x, index_z, index_r = (lax.axis_index(name) for name in AXES)
    points = jnp.stack(
        [
            index_x * plan.wx + cell // (plan.wz * wr),
            index_z * plan.wz + cell // wr % plan.wz,
            index_r * wr + cell % wr,
        ]
    ).astype(f32) + 0.5
    points = jnp.transpose(points.reshape(3, tile_count, 128), (1, 0, 2))
    cos_t, sin_t = fourier_numpy(plan.samples)
    table = np.concatenate([cos_t, sin_t], axis=0).astype(np.float32)
    table[:, plan.samples - STEPS :] = 0.0
    spec, watch = pl.pallas_call(
        bind(dft_kernel, plan),
        out_shape=(shape((tile_count, 264, 128), f32), shape((plan.obs, 8), f32)),
        grid=(tile_count,),
        in_specs=[
            pl.BlockSpec((5, 128, plan.samples), lambda i: (0, i, 0)),
            pl.BlockSpec((1, 3, 128), lambda i: (i, 0, 0)),
            pl.BlockSpec((3, plan.obs), lambda i: (0, 0)),
            SMEM,
        ],
        out_specs=(
            pl.BlockSpec((1, 264, 128), lambda i: (i, 0, 0)),
            pl.BlockSpec((plan.obs, 8), lambda i: (0, 0)),
        ),
        name="dft",
        compiler_params=pltpu.CompilerParams(vmem_limit_bytes=40 * 1024 * 1024),
        cost_estimate=pl.CostEstimate(flops=10**9, bytes_accessed=10**6, transcendentals=0),
    )(jnp.transpose(history, (1, 0, 2)), points, observers, surface_blocks)

    def radiated(ways, sources, quarters=(4,)):
        share = plan.obs // ways // 4
        out, first = [], 0
        for count in quarters:
            wide = 32 if count % 2 == 0 and share % 16 == 0 else 16
            out.append(
                call(
                    bind(hist_kernel, plan, ways, first * share, wide),
                    shape((count * share, 64), f32),
                    [VMEM] * (1 + len(sources)),
                    VMEM,
                    [pltpu.VMEM((64, wide, 128), f32)],
                    flops=10**9,
                )(watch, *sources)
            )
            first += count
        return out

    near_swap = [(i, i ^ 1) for i in range(plan.rows)]
    if plan.rows % 4 == 0:
        across = move("row", [(i, i ^ 2) for i in range(plan.rows)])(spec)
        hists = radiated(4, [spec, move("row", near_swap)(spec)], (3, 1))
    elif plan.rows % 2 == 0:
        hists = radiated(2, [spec, move("row", near_swap)(spec)], (3, 1))
    else:
        hists = radiated(1, [spec], (3, 1))
    flat = got.reshape(group * plan.sent, lanes)
    flat, hists[0] = lax.optimization_barrier((flat, hists[0]))
    first, second, own = call(
        bind(edge_kernel, plan),
        (shape((5 * group * HALO, lanes), f32),) * 2 + (shape((group * plan.body, lanes), f32),),
        [VMEM],
        (VMEM, VMEM, VMEM),
    )(flat)
    ready = first
    line = plan.line()
    swap_a = [(line[i], line[i ^ 1]) for i in range(len(line))]
    swap_b = [
        (line[i], line[((i + 1) ^ 1) - 1]) for i in range(1, len(line) - 1)
    ]
    first = move(AXES, swap_a)(first)
    second = move(AXES, swap_b)(second)

    if plan.rows % 4 == 0:
        across, _ = lax.optimization_barrier((across, ready))
        hists += radiated(4, [across, move("row", near_swap)(across)], (2, 2))
    parts = len(hists)
    near_parts = 2

    ids = entries(plan, got[:, plan.body : plan.body + 4, :])
    listed, count = call(
        bind(list_kernel, plan),
        (shape((group * SURF_DEV + 8,), jnp.int32), shape((1,), jnp.int32)),
        [SMEM],
        (SMEM, SMEM),
    )(ids)

    own, listed, count, hists[:3] = lax.optimization_barrier((own, listed, count, hists[:3]))
    back, samp = call(
        bind(stencil_kernel, plan),
        (shape((group * plan.body, lanes), f32), shape((plan.chunk * 8 * 16, lanes), f32)),
        [VMEM, VMEM, VMEM, VMEM],
        (pl.BlockSpec(memory_space=pl.ANY), VMEM),
        [
            pltpu.VMEM((group * plan.body, lanes), f32),
            pltpu.SemaphoreType.DMA(()),
            pltpu.VMEM((field_rows, lanes), f32),
            pltpu.VMEM((field_rows, lanes), f32),
            pltpu.VMEM((field_rows, lanes), f32),
            pltpu.VMEM((75, 8, lanes), f32),
            pltpu.VMEM((plan.tall_pad, lanes), f32),
            pltpu.VMEM((30 * plan.az, 8, lanes), f32),
        ],
        flops=10**9,
    )(own, first, second, flux_jacobian)
    back = move(GROUP)(back.reshape(group, plan.body, lanes))

    columns = np.zeros((FREQ, 8), np.float32)
    for s in range(STEPS):
        columns[:, 2 * s] = cos_t[:, plan.samples - STEPS + s]
        columns[:, 2 * s + 1] = sin_t[:, plan.samples - STEPS + s]
    columns[:, 6] = 1.0 / np.arange(1, FREQ + 1)
    partial = call(
        bind(recent_kernel, plan, parts, near_parts),
        shape((plan.obs // 2, 128), f32),
        [SMEM, SMEM, VMEM, VMEM, VMEM] + [VMEM] * parts,
        VMEM,
        [
            pltpu.VMEM((128, 128), f32),
            pltpu.VMEM((24, 128), f32),
            pltpu.VMEM((plan.obs // 128 * FREQ * 8, 128), f32),
            pltpu.VMEM((plan.obs // 128 * FREQ * 8, 128), f32),
            pltpu.VMEM((plan.obs // 128 * STEPS * 8, 128), f32),
            pltpu.VMEM((plan.obs // 128 * STEPS * 8, 128), f32),
            pltpu.VMEM((plan.obs, 128), f32),
            pltpu.VMEM((plan.obs // 128 * (FREQ // 8) * 12, 8, 128), f32),
            pltpu.VMEM((128, 128), f32),
        ],
        flops=10**9,
    )(listed, count, samp, observers, jnp.asarray(columns), *hists)
    pieces = move(AXES)(partial.reshape(plan.devices, 4, 128))
    spectrum = call(sum_kernel, shape((plan.per_obs, 2 * FREQ), f32), [VMEM], VMEM)(pieces)
    field = call(
        bind(unpack_kernel, plan),
        shape((5, lanes, wr), f32),
        [VMEM],
        VMEM,
        [pltpu.VMEM((5 * wr, lanes), f32)],
    )(back)
    return field.reshape(flow_field.shape), spectrum


def per_device(*args):
    flow_field, _, history, surface_cell, _, observers = args
    mesh = {name: lax.axis_size(name) for name in AXES}
    plan = Plan(mesh, flow_field.shape[1:], surface_cell.shape, history.shape, observers.shape[1])
    if plan.fits():
        return fast_device(plan, *args)
    return general_device(*args)


def solution(mesh):
    return jax.shard_map(
        per_device,
        mesh=mesh,
        in_specs=(
            P(None, "gx", "gz", "row"),
            P(),
            P(("gx", "gz", "row"), None, None),
            P(("gx", "gz", "row"), None),
            P("row", ("gx", "gz")),
            P(),
        ),
        out_specs=(P(None, "gx", "gz", "row"), P(("gx", "gz", "row"), None)),
        check_vma=False,
    )
```
